32 devices in a mesh: items: 16 (over z, y, core), seq: 2 (over x).
Axes of the slice: x: 2, y: 2, z: 4, core: 2. Of those that a mesh axis runs over, the one named last changes fastest.
Arguments:
- frames: bfloat16 [16, 1280, 1024], P('items', 'seq'), may hold values from -6 to 6
- cotangent: bfloat16 [16, 1280, 1024], P('items', 'seq'), may hold values from -6 to 6
- section: int32 [16], P('items'), may hold values from 0 to 7
- prompt_len: int32 [16], P('items'), may hold values from 150 to 600, as said below
- section_embed: float32 [8, 1024], replicated, may hold values from -6 to 6
- ada_proj: bfloat16 [1024, 4096], replicated, may hold values from -0.09375 to 0.09375
- ada_bias: float32 [4096], replicated, may hold values from -4 to 4
- w_qkv: bfloat16 [1024, 3072], replicated, may hold values from -0.1875 to 0.1875
- w_out: bfloat16 [1024, 1024], replicated, may hold values from -3.5 to 3.5
- w_up: bfloat16 [1024, 4096], replicated, may hold values from -0.1875 to 0.1875
- w_down: bfloat16 [4096, 1024], replicated, may hold values from -0.125 to 0.125
Outputs:
- out_frames: bfloat16 [16, 1280, 1024], P('items', 'seq')
- frames_grad: bfloat16 [16, 1280, 1024], P('items', 'seq')
- section_embed_grad: float32 [8, 1024], P(None, 'items')
- ada_proj_grad: float32 [1024, 4096], P('items')
- ada_bias_grad: float32 [4096], P('items')
- w_qkv_grad: float32 [1024, 3072], P('items')
- w_out_grad: float32 [1024, 1024], P('items')
- w_up_grad: float32 [1024, 4096], P('items')
- w_down_grad: float32 [4096, 1024], P('items')
The draws below stay inside these ranges and needn't reach their ends.
Inputs may be any that keep to these rules, and one draw needn't show every extreme that they name: `prompt_len`: some item has exactly 600 prompt frames.
All inputs are finite; a program needn't handle non-finite values.
Results may differ from the reference program's by a relative error of at most 0.018.
Values may be sent and summed in bfloat16 or wider, within the bound.
A program may use at most 640 MiB of HBM per device.

```python
import jax
import jax.numpy as jnp
from jax import lax

D = 1024
HEADS = 16
HEAD_DIM = 64
FF = 4096
SECTIONS = 8
ROWS = 640
PROMPT_MAX = 600
PROMPT_MIN = 150
ITEMS = 16
LEN = 1280


def draw_prompt_len(key, part):
    first, second = jax.random.split(key)
    lengths = jax.random.randint(first, (ITEMS,), PROMPT_MIN, PROMPT_MAX + 1)
    chosen = jax.random.randint(second, (), 0, ITEMS)
    return jnp.where(jnp.arange(ITEMS) == chosen, PROMPT_MAX, lengths).astype(jnp.int32)


def touch_ends(result, own_key, smallest, largest):
    longest = result.shape.index(max(result.shape))
    spots = []
    for shift in (0, 1):
        where = [jax.random.randint(jax.random.fold_in(own_key, axis), (), 0, length) for axis, length in enumerate(result.shape)]
        where[longest] = (where[longest] + shift) % result.shape[longest]
        spots.append(tuple(where))
    return result.at[spots[0]].set(smallest).at[spots[1]].set(largest)


def block_scale(stream_key, dims, shards, smallest, largest):
    level = 1.0
    for dim, blocks in shards:
        heights = jax.random.uniform(jax.random.fold_in(jax.random.fold_in(stream_key, 6), dim), (blocks,), jnp.float32, smallest / len(shards), largest / len(shards))
        level = level * jnp.repeat(jnp.exp(heights), dims[dim] // blocks).reshape((-1,) + (1,) * (len(dims) - 1 - dim))
    return level


def noise(own_key, shape, deviation, reach, cuts=(), held_as=jnp.bfloat16):
    drawn = deviation * jax.random.normal(own_key, shape, jnp.float32)
    if cuts:
        drawn = drawn * block_scale(own_key, shape, cuts, -0.22, 0.18)
    return jnp.clip(drawn, -reach, reach).astype(held_as)


def setup_inputs(seed: int = 0) -> dict:
    arg_keys = jax.random.split(jax.random.key(seed), 12)
    return {
        "frames": noise(arg_keys[0], (ITEMS, LEN, D), 1.0, 6.0, ((0, 16), (1, 2))),
        "cotangent": noise(arg_keys[1], (ITEMS, LEN, D), 1.0, 6.0, ((0, 16), (1, 2))),
        "section": touch_ends(jax.random.randint(arg_keys[2], (ITEMS,), 0, SECTIONS), jax.random.fold_in(arg_keys[2], 1), 0, SECTIONS - 1).astype(jnp.int32),
        "prompt_len": draw_prompt_len(jax.random.fold_in(arg_keys[11], 71), 0),
        "section_embed": noise(arg_keys[4], (SECTIONS, D), 1.0, 6.0, (), jnp.float32),
        "ada_proj": noise(arg_keys[5], (D, 4 * D), (4 * D) ** -0.5, 0.09375),
        "ada_bias": noise(arg_keys[6], (4 * D,), 0.3, 4.0, (), jnp.float32),
        "w_qkv": noise(arg_keys[7], (D, 3 * D), D ** -0.5, 0.1875),
        "w_out": noise(arg_keys[8], (D, D), (max(1, 4 * D // LEN)) ** -0.5, 3.5),
        "w_up": noise(arg_keys[9], (D, FF), D ** -0.5, 0.1875),
        "w_down": noise(arg_keys[10], (FF, D), (FF // 2) ** -0.5, 0.125),
    }


EPS = 1e-05
NEGATIVE = -1e+30
SQRT_HALF = 0.7071067811865476
HIGHEST = lax.Precision.HIGHEST

@jax.custom_vjp
def low(v):
    return lax.optimization_barrier(v.astype(jnp.bfloat16)).astype(jnp.float32)

@jax.custom_vjp
def low_back(v):
    return v

def low_keep(v):
    return (low(v), None)

def low_pass(kept, grad):
    return (grad,)

def back_keep(v):
    return (v, None)

def back_low(kept, grad):
    return (low(grad),)
low.defvjp(low_keep, low_pass)
low_back.defvjp(back_keep, back_low)

def layer_norm(values):
    mean = lax.optimization_barrier(jnp.mean(values, -1, keepdims=True))
    centered = values - mean
    variance = lax.optimization_barrier(jnp.mean(centered * centered, -1, keepdims=True))
    return centered * lax.rsqrt(variance + EPS)

def gelu_exact(values):
    return 0.5 * values * (1.0 + lax.erf(values * SQRT_HALF))

def item_layer(item_frames, item_section, item_len, params):
    section_embed, ada_proj, ada_bias, w_qkv, w_out, w_up, w_down = params
    onehot = (jnp.arange(SECTIONS, dtype=jnp.int32) == item_section).astype(jnp.float32)
    cond = jnp.dot(onehot, section_embed, precision=HIGHEST)
    modul = jnp.dot(cond, ada_proj, precision=HIGHEST) + ada_bias
    scale_one, shift_one, scale_two, shift_two = jnp.split(modul, 4)
    attn_in = low(layer_norm(item_frames) * (1.0 + scale_one) + shift_one)
    qkv = jnp.dot(attn_in, w_qkv, precision=HIGHEST)
    query = low_back(low(qkv[:, :D])).reshape(LEN, HEADS, HEAD_DIM)
    keys = low_back(low(qkv[:, D:2 * D])).reshape(LEN, HEADS, HEAD_DIM)
    values = low_back(low(qkv[:, 2 * D:])).reshape(LEN, HEADS, HEAD_DIM)
    scores = low_back(jnp.einsum('qhd,khd->hqk', query, keys, precision=HIGHEST) * HEAD_DIM ** (-0.5))
    position = jnp.arange(LEN, dtype=jnp.int32)
    valid = ((position >= ROWS) | (position < item_len))[None, None, :]
    scores = jnp.where(valid, scores, NEGATIVE)
    top = lax.optimization_barrier(jnp.max(scores, -1, keepdims=True))
    expd = jnp.where(valid, jnp.exp(scores - top), 0.0)
    probs = low(expd / lax.optimization_barrier(jnp.sum(expd, -1, keepdims=True)))
    att = jnp.einsum('hqk,khd->qhd', probs, values, precision=HIGHEST).reshape(LEN, D)
    att = low_back(low(att))
    attn = low_back(jnp.dot(att, w_out, precision=HIGHEST))
    mid = item_frames + attn
    ffn_in = low(layer_norm(mid) * (1.0 + scale_two) + shift_two)
    upper = low_back(jnp.dot(ffn_in, w_up, precision=HIGHEST))
    act = low(gelu_exact(upper))
    down = low_back(jnp.dot(act, w_down, precision=HIGHEST))
    return mid + down

def reference(frames, cotangent, section, prompt_len, section_embed, ada_proj, ada_bias, w_qkv, w_out, w_up, w_down):
    params = (section_embed.astype(jnp.float32), ada_proj.astype(jnp.float32), ada_bias.astype(jnp.float32), w_qkv.astype(jnp.float32), w_out.astype(jnp.float32), w_up.astype(jnp.float32), w_down.astype(jnp.float32))
    inputs = frames.astype(jnp.float32)

    def forward(inputs, params):

        def one_item(triple):
            return item_layer(triple[0], triple[1], triple[2], params)
        return lax.map(jax.checkpoint(one_item), (inputs, section, prompt_len))
    outputs, pullback = jax.vjp(forward, inputs, params)
    grad_inputs, grad_params = pullback(cotangent.astype(jnp.float32))
    return (outputs.astype(jnp.bfloat16), grad_inputs.astype(jnp.bfloat16), grad_params[0], grad_params[1], grad_params[2], grad_params[3], grad_params[4], grad_params[5], grad_params[6])
```

```python
import functools

import jax
import jax.numpy as jnp
from jax import lax
from jax.experimental import pallas as pl
from jax.experimental.pallas import tpu as pltpu
from jax.sharding import PartitionSpec as P

HEADS = 16


EPS = 1e-05
NEGATIVE = -1e30
SQRT_HALF = 0.7071067811865476
INV_SQRT_TAU = 0.3989422804014327
HIGHEST = lax.Precision.HIGHEST


def normalize(values):
    mean = jnp.mean(values, -1, keepdims=True)
    centered = values - mean
    inverse = lax.rsqrt(jnp.mean(centered * centered, -1, keepdims=True) + EPS)
    return (centered * inverse, inverse)


def norm_back(grad, normed, inverse):
    first = jnp.mean(grad, -1, keepdims=True)
    second = jnp.mean(grad * normed, -1, keepdims=True)
    return (grad - first - normed * second) * inverse


def gelu_exact(values):
    return 0.5 * values * (1.0 + lax.erf(values * SQRT_HALF))


def gelu_slope(values):
    return (
        0.5 * (1.0 + lax.erf(values * SQRT_HALF))
        + values * jnp.exp(-0.5 * values * values) * INV_SQRT_TAU
    )


def project(left, weight):
    flat = left.reshape(-1, left.shape[-1])
    result = jnp.dot(flat, weight, preferred_element_type=jnp.float32)
    return result.reshape(left.shape[:-1] + (weight.shape[1],))


def back_project(grad, weight):
    flat = grad.reshape(-1, grad.shape[-1])
    result = lax.dot_general(
        flat, weight, (((1,), (1,)), ((), ())), preferred_element_type=jnp.float32
    )
    return result.reshape(grad.shape[:-1] + (weight.shape[0],))


BIG = 1e30

def split3(x):
    hi = x.astype(jnp.bfloat16).astype(jnp.float32)
    rest = x - hi
    mid = rest.astype(jnp.bfloat16).astype(jnp.float32)
    return hi, mid, rest - mid

def dot(a, b, ca, cb):
    return lax.dot_general(a, b, (((ca,), (cb,)), ((), ())), preferred_element_type=jnp.float32)


def fwd_kernel(rows, blocks, lim_ref, q_ref, ko_ref, vo_ref, kt_ref, vt_ref, o_ref, lse_ref):
    lane = lax.broadcasted_iota(jnp.int32, (1, 128), 1)
    low = lane < 64
    row = lax.broadcasted_iota(jnp.int32, (rows, 1), 0)
    q = q_ref[...].astype(jnp.float32) * 0.125
    outs, lses = [], []
    for h in range(2):
        own = low if h == 0 else jnp.logical_not(low)
        first = 64 * (1 - h)
        qa = jnp.where(own, q, jnp.where(lane == first, 1.0, 0.0)).astype(jnp.bfloat16)
        scores, values = [], []
        for j in range(blocks):
            k = ko_ref[...] if j == 0 else kt_ref[pl.ds((j - 1) * rows, rows), :]
            v = vo_ref[...] if j == 0 else vt_ref[pl.ds((j - 1) * rows, rows), :]
            bias = jnp.where(row < lim_ref[j], 0.0, -BIG)
            ka = jnp.where(own, k.astype(jnp.float32), jnp.where(lane == first, bias, 0.0)).astype(jnp.bfloat16)
            va = jnp.where(own, v.astype(jnp.float32), 1.0).astype(jnp.bfloat16)
            scores.append(dot(qa, ka, 1, 1))
            values.append(va)
        top = functools.reduce(jnp.maximum, [jnp.max(s, -1, keepdims=True) for s in scores])
        total = None
        for s, va in zip(scores, values):
            p = jnp.exp(s - top).astype(jnp.bfloat16)
            part = dot(p, va, 1, 0)
            total = part if total is None else total + part
        outs.append(total / pltpu.roll(total, 64, 1))
        lses.append(top + jnp.log(total))
    o_ref[...] = jnp.where(low, outs[0], outs[1]).astype(o_ref.dtype)
    lse_ref[...] = jnp.where(low, lses[1], lses[0])


def bwd_kernel(rows, blocks, lim_ref, q_ref, ko_ref, vo_ref, kt_ref, vt_ref, do_ref, o_ref, lse_ref,
               dq_ref, dko_ref, dvo_ref, dkt_ref, dvt_ref):
    lane = lax.broadcasted_iota(jnp.int32, (1, 128), 1)
    low = lane < 64
    row = lax.broadcasted_iota(jnp.int32, (rows, 1), 0)
    q = q_ref[...].astype(jnp.float32) * 0.125
    qs = q.astype(jnp.bfloat16)
    do_low = do_ref[...]
    do = do_low.astype(jnp.float32)
    prod = do * o_ref[...].astype(jnp.float32)
    lh, lm, ll = split3(lse_ref[...])
    heads = []
    for h in range(2):
        own = low if h == 0 else jnp.logical_not(low)
        f = 64 * (1 - h)
        delta = jnp.sum(jnp.where(own, prod, 0.0), -1, keepdims=True)
        dh, dm, dl = split3(delta)
        qa = jnp.where(own, q, jnp.where(lane == f, 1.0, jnp.where(lane == f + 1, -lh, jnp.where(lane == f + 2, -lm, jnp.where(lane == f + 3, -ll, 0.0))))).astype(jnp.bfloat16)
        doa = jnp.where(own, do, jnp.where(lane == f, -dh, jnp.where(lane == f + 1, -dm, jnp.where(lane == f + 2, -dl, 0.0)))).astype(jnp.bfloat16)
        kone = jnp.where((lane > f) & (lane <= f + 3), 1.0, 0.0)
        vone = jnp.where((lane >= f) & (lane < f + 3), 1.0, 0.0)
        dq = None
        res = []
        for j in range(blocks):
            k = ko_ref[...] if j == 0 else kt_ref[pl.ds((j - 1) * rows, rows), :]
            v = vo_ref[...] if j == 0 else vt_ref[pl.ds((j - 1) * rows, rows), :]
            bias = jnp.where(row < lim_ref[j], 0.0, -BIG)
            ka = jnp.where(own, k.astype(jnp.float32), jnp.where(lane == f, bias, kone)).astype(jnp.bfloat16)
            va = jnp.where(own, v.astype(jnp.float32), vone).astype(jnp.bfloat16)
            pt = jnp.exp(dot(ka, qa, 1, 1))
            dpt = dot(va, doa, 1, 1)
            dst = (pt * dpt).astype(jnp.bfloat16)
            dv = dot(pt.astype(jnp.bfloat16), do_low, 1, 0)
            dk = dot(dst, qs, 1, 0)
            part = dot(dst, k, 0, 0)
            dq = part if dq is None else dq + part
            res.append((dk, dv))
        heads.append((dq, res))
    dq_ref[...] = (jnp.where(low, heads[0][0], heads[1][0]) * 0.125).astype(dq_ref.dtype)
    for j in range(blocks):
        dk = jnp.where(low, heads[0][1][j][0], heads[1][1][j][0]).astype(dko_ref.dtype)
        dv = jnp.where(low, heads[0][1][j][1], heads[1][1][j][1]).astype(dko_ref.dtype)
        if j == 0:
            dko_ref[...] = dk
            dvo_ref[...] = dv
        else:
            dkt_ref[pl.ds((j - 1) * rows, rows), :] = dk
            dvt_ref[pl.ds((j - 1) * rows, rows), :] = dv


def specs_of(rows, others, width):
    pairs = width // 128
    place = lambda count, skip: pl.BlockSpec((count, 128), lambda i, lim: (0, i + skip))
    inputs = [place(rows, 0), place(rows, pairs), place(rows, 2 * pairs), place(others, 0), place(others, pairs)]
    return inputs, place(rows, 0), place(others, 0)


def attend(lim, qkv, kv_rest, width):
    rows, others = qkv.shape[0], kv_rest.shape[0]
    blocks = 1 + others // rows
    inputs, own, oth = specs_of(rows, others, width)
    keys = rows + others
    return pl.pallas_call(
        functools.partial(fwd_kernel, rows, blocks),
        grid_spec=pltpu.PrefetchScalarGridSpec(num_scalar_prefetch=1, grid=(width // 128,),
            in_specs=inputs, out_specs=[own, own]),
        out_shape=[jax.ShapeDtypeStruct((rows, width), jnp.bfloat16), jax.ShapeDtypeStruct((rows, width), jnp.float32)],
        compiler_params=pltpu.CompilerParams(vmem_limit_bytes=56 << 20),
        cost_estimate=pl.CostEstimate(flops=16 * rows * keys * width, transcendentals=rows * keys * width // 64,
            bytes_accessed=2 * width * (2 * rows + 2 * keys) + 4 * rows * width),
    )(lim, qkv, qkv, qkv, kv_rest, kv_rest)


def attend_back(lim, qkv, kv_rest, do, o, lse):
    (rows, width), others = do.shape, kv_rest.shape[0]
    blocks = 1 + others // rows
    inputs, own, oth = specs_of(rows, others, width)
    keys = rows + others
    s = lambda n: jax.ShapeDtypeStruct((n, width), jnp.bfloat16)
    return pl.pallas_call(
        functools.partial(bwd_kernel, rows, blocks),
        grid_spec=pltpu.PrefetchScalarGridSpec(num_scalar_prefetch=1, grid=(width // 128,),
            in_specs=inputs + [own, own, own], out_specs=[own, own, own, oth, oth]),
        out_shape=[s(rows), s(rows), s(rows), s(others), s(others)],
        compiler_params=pltpu.CompilerParams(vmem_limit_bytes=56 << 20),
        cost_estimate=pl.CostEstimate(flops=40 * rows * keys * width, transcendentals=rows * keys * width // 64,
            bytes_accessed=2 * width * (4 * rows + 4 * keys) + 4 * rows * width),
    )(lim, qkv, qkv, qkv, kv_rest, kv_rest, do, o, lse)


def outer_kernel(plan, halves, first_tiles, side_ref, *refs):
    lefts, plan_rights, outs, turned = refs[: plan[0]], refs[plan[0] : plan[1]], refs[plan[1] : plan[1] + 4], refs[plan[1] + 4 :]
    step = pl.program_id(0)

    @pl.when(step == 0)
    def _():
        for left, flip in zip(lefts, turned):
            flip[...] = left[...].T

    at = 0
    place = 0
    for tiles, terms in plan[2]:
        rights = plan_rights[place : place + len(terms)]
        place += len(terms)

        @pl.when((step >= at) & (step < at + tiles))
        def _(rights=rights, terms=terms):
            total = None
            for which, right in zip(terms, rights):
                part = dot(turned[which][...], right[...], 1, 0)
                total = part if total is None else total + part
            rows, columns = total.shape
            split = total.astype(jnp.bfloat16).reshape(halves, 2, rows // (2 * halves), columns)
            even = side_ref[0] == 0
            keep = jnp.where(even, split[:, 0], split[:, 1])
            send = jnp.where(even, split[:, 1], split[:, 0])

            @pl.when(step < first_tiles)
            def _():
                outs[0][...] = send
                outs[1][...] = keep

            @pl.when(step >= first_tiles)
            def _():
                outs[2][...] = send
                outs[3][...] = keep

        at += tiles


def outer(side, lefts, segments, parts, tile):
    rows = lefts[0].shape[1]
    halves = parts // 2
    block = rows // parts
    width = sum(segment[0][1].shape[1] for segment in segments)
    steps = width // tile
    first_tiles = steps // 2
    in_specs = [pl.BlockSpec(left.shape, lambda i, s: (0, 0)) for left in lefts]
    operands = list(lefts)
    plan = []
    at = 0
    flops = 0
    for segment in segments:
        tiles = segment[0][1].shape[1] // tile
        for which, right in segment:
            in_specs.append(
                pl.BlockSpec(
                    (right.shape[0], tile),
                    lambda i, s, at=at, tiles=tiles: (0, jnp.clip(i - at, 0, tiles - 1)),
                )
            )
            operands.append(right)
            flops += 2 * rows * right.shape[0] * right.shape[1]
        plan.append((tiles, tuple(which for which, _ in segment)))
        at += tiles
    first = pl.BlockSpec((halves, block, tile), lambda i, s: (0, 0, jnp.minimum(i, first_tiles - 1)))
    second = pl.BlockSpec((halves, block, tile), lambda i, s: (0, 0, jnp.maximum(i - first_tiles, 0)))
    shape = lambda count: jax.ShapeDtypeStruct((halves, block, count * tile), jnp.bfloat16)
    moved = sum(2 * operand.size for operand in operands) + 2 * rows * width
    return pl.pallas_call(
        functools.partial(
            outer_kernel, (len(lefts), len(operands), tuple(plan)), halves, first_tiles
        ),
        grid_spec=pltpu.PrefetchScalarGridSpec(
            num_scalar_prefetch=1,
            grid=(steps,),
            in_specs=in_specs,
            out_specs=[first, first, second, second],
            scratch_shapes=[pltpu.VMEM(left.shape[::-1], jnp.bfloat16) for left in lefts],
        ),
        out_shape=[shape(first_tiles)] * 2 + [shape(steps - first_tiles)] * 2,
        compiler_params=pltpu.CompilerParams(vmem_limit_bytes=58 << 20),
        cost_estimate=pl.CostEstimate(flops=flops, transcendentals=0, bytes_accessed=moved),
    )(side, *operands)


def swap(values, axis, bit):
    size = lax.axis_size(axis)
    return lax.ppermute(values, axis, [(i, i ^ bit) for i in range(size)])


def bits_of(axis):
    size = lax.axis_size(axis)
    return [1 << place for place in range(size.bit_length() - 1)]


def add_low(left, right):
    return (left.astype(jnp.float32) + right.astype(jnp.float32)).astype(jnp.bfloat16)


def half_of(values, dim, which):
    return lax.dynamic_index_in_dim(values, which, dim, keepdims=False)


def reduce_rows(keep, got, axis):
    me = lax.axis_index(axis)
    for bit in bits_of(axis)[1:]:
        mine = jnp.bitwise_and(me // bit, 1)
        shape = keep.shape
        view = (shape[0] // 2, 2) + shape[1:]
        keep, got = keep.reshape(view), got.reshape(view)
        send = add_low(half_of(keep, 1, 1 - mine), half_of(got, 1, 1 - mine))
        keep = add_low(half_of(keep, 1, mine), half_of(got, 1, mine))
        got = swap(send, axis, bit)
    return keep, got


def finish(pieces, rows_axis, seq_axis):
    send_a, keep_a, send_b, keep_b = pieces
    got_a = swap(send_a, rows_axis, 1)
    got_b = swap(send_b, rows_axis, 1)
    keep_a, got_a = reduce_rows(keep_a, got_a, rows_axis)
    total_a = (keep_a.astype(jnp.float32) + got_a.astype(jnp.float32))[0]
    for bit in bits_of(seq_axis):
        low = total_a.astype(jnp.bfloat16)
        total_a = low.astype(jnp.float32) + swap(low, seq_axis, bit).astype(jnp.float32)
    me = lax.axis_index(seq_axis)
    for bit in bits_of(seq_axis):
        mine = jnp.bitwise_and(me // bit, 1)
        width = keep_b.shape[-1] // 2
        cut = lambda values, which: lax.dynamic_slice_in_dim(values, which * width, width, 2)
        send = add_low(cut(keep_b, 1 - mine), cut(got_b, 1 - mine))
        keep_b = add_low(cut(keep_b, mine), cut(got_b, mine))
        got_b = swap(send, seq_axis, bit)
    keep_b, got_b = reduce_rows(keep_b, got_b, rows_axis)
    total_b = add_low(keep_b, got_b)[0]
    for bit in reversed(bits_of(seq_axis)):
        mine = jnp.bitwise_and(me // bit, 1)
        other = swap(total_b, seq_axis, bit)
        total_b = jnp.where(
            mine == 0,
            jnp.concatenate([total_b, other], -1),
            jnp.concatenate([other, total_b], -1),
        )
    return jnp.concatenate([total_a, total_b.astype(jnp.float32)], -1)


def gather_items(values, axis):
    me = lax.axis_index(axis)
    for bit in bits_of(axis):
        other = swap(values, axis, bit)
        mine = jnp.bitwise_and(me // bit, 1)
        values = jnp.where(
            mine == 0, jnp.concatenate([values, other]), jnp.concatenate([other, values])
        )
    return values


def per_device(
    frames,
    cotangent,
    section,
    prompt_len,
    section_embed,
    ada_proj,
    ada_bias,
    w_qkv,
    w_out,
    w_up,
    w_down,
):
    _, row_count, width = frames.shape
    frames, cotangent = frames[0], cotangent[0]
    seq_size = lax.axis_size("seq")
    item_size = lax.axis_size("items")
    seq_me, item_me = lax.axis_index("seq"), lax.axis_index("items")
    side = jnp.bitwise_and(item_me, 1).astype(jnp.int32).reshape(1)
    turns = list(range(1, seq_size))
    fetch = lambda values, turn: lax.ppermute(
        values, "seq", [((i + turn) % seq_size, i) for i in range(seq_size)]
    )
    give = lambda values, turn: lax.ppermute(
        values, "seq", [(i, (i + turn) % seq_size) for i in range(seq_size)]
    )
    others = [fetch(frames, turn) for turn in turns]
    sources = jnp.stack([(seq_me + turn) % seq_size for turn in [0] + turns])
    limits = jnp.where(sources == 0, prompt_len[0], row_count).astype(jnp.int32)

    section_count = section_embed.shape[0]
    onehot = (section[:, None] == jnp.arange(section_count, dtype=jnp.int32)[None, :]).astype(
        jnp.float32
    )
    cond = jnp.dot(onehot, section_embed, precision=HIGHEST)
    modul = jnp.dot(cond, ada_proj.astype(jnp.float32), precision=HIGHEST) + ada_bias[None, :]
    scale_one, shift_one, scale_two, shift_two = jnp.split(modul, 4, axis=-1)
    inputs = frames.astype(jnp.float32)
    normed_one, inv_one = normalize(inputs)
    modulate = lambda normed: (normed * (1.0 + scale_one) + shift_one).astype(jnp.bfloat16)
    attn_in = modulate(normed_one)
    qkv = project(attn_in, w_qkv).astype(jnp.bfloat16)
    rest = jnp.concatenate(others) if len(others) > 1 else others[0]
    normed_rest, _ = normalize(rest.astype(jnp.float32))
    attn_rest = modulate(normed_rest)
    kv_rest = project(attn_rest, w_qkv[:, width:]).astype(jnp.bfloat16)
    att, lse = attend(limits, qkv, kv_rest, width)
    mid = inputs + project(att, w_out)
    normed_two, inv_two = normalize(mid)
    ffn_in = (normed_two * (1.0 + scale_two) + shift_two).astype(jnp.bfloat16)
    upper = project(ffn_in, w_up)
    act = gelu_exact(upper).astype(jnp.bfloat16)
    out_frames = (mid + project(act, w_down)).astype(jnp.bfloat16)

    grad_out = cotangent.astype(jnp.float32)
    down_pieces = outer(side, [act], [[(0, cotangent)]], item_size, 256)
    grad_upper = (back_project(cotangent, w_down) * gelu_slope(upper)).astype(jnp.bfloat16)
    up_pieces = outer(side, [ffn_in], [[(0, grad_upper)]], item_size, 512)
    grad_ffn_in = back_project(grad_upper, w_up)
    grad_scale_two = jnp.sum(grad_ffn_in * normed_two, 0)
    grad_shift_two = jnp.sum(grad_ffn_in, 0)
    grad_mid = grad_out + norm_back(grad_ffn_in * (1.0 + scale_two), normed_two, inv_two)
    grad_mid_low = grad_mid.astype(jnp.bfloat16)
    out_pieces = outer(side, [att], [[(0, grad_mid_low)]], item_size, 512)
    grad_att = back_project(grad_mid_low, w_out).astype(jnp.bfloat16)
    grad_query, grad_key, grad_value, key_rest, value_rest = attend_back(
        limits, qkv, kv_rest, grad_att, att, lse
    )
    qkv_pieces = outer(
        side,
        [attn_in, attn_rest],
        [
            [(0, grad_query)],
            [(0, grad_key), (1, key_rest)],
            [(0, grad_value), (1, value_rest)],
        ],
        item_size,
        512,
    )
    w_key, w_value = w_qkv[:, width : 2 * width], w_qkv[:, 2 * width :]
    share = back_project(key_rest, w_key) + back_project(value_rest, w_value)
    grad_rest = [
        give(share[i * row_count : (i + 1) * row_count].astype(jnp.bfloat16), turn)
        for i, turn in enumerate(turns)
    ]
    partial = (
        back_project(grad_query, w_qkv[:, :width])
        + back_project(grad_key, w_key)
        + back_project(grad_value, w_value)
    )
    grad_scale_one = jnp.sum(partial * normed_one, 0) + jnp.sum(share * normed_rest, 0)
    grad_shift_one = jnp.sum(partial, 0) + jnp.sum(share, 0)
    grad_attn_in = partial
    for got in grad_rest:
        grad_attn_in = grad_attn_in + got.astype(jnp.float32)
    frames_grad = (
        grad_mid + norm_back(grad_attn_in * (1.0 + scale_one), normed_one, inv_one)
    ).astype(jnp.bfloat16)

    sum_down = finish(down_pieces, "items", "seq")
    sum_up = finish(up_pieces, "items", "seq")
    sum_out = finish(out_pieces, "items", "seq")
    sum_qkv = finish(qkv_pieces, "items", "seq")

    grad_modul = jnp.concatenate(
        [grad_scale_one, grad_shift_one, grad_scale_two, grad_shift_two]
    )[None, :]
    for bit in bits_of("seq"):
        grad_modul = grad_modul + swap(grad_modul, "seq", bit)
    tagged = jnp.concatenate([grad_modul, jnp.pad(onehot, ((0, 0), (0, 128 - section_count)))], -1)
    tagged = gather_items(tagged, "items")
    modul_all, onehot_all = tagged[:, : 4 * width], tagged[:, 4 * width :][:, :section_count]
    block = width // item_size
    own_embed = lax.dynamic_slice_in_dim(section_embed, item_me * block, block, 1)
    own_cond = jnp.dot(onehot_all, own_embed, precision=HIGHEST)
    sum_ada = lax.dot_general(own_cond, modul_all, (((0,), (0,)), ((), ())), precision=HIGHEST)
    sum_bias = jnp.sum(
        lax.dynamic_slice_in_dim(modul_all, item_me * 4 * block, 4 * block, 1), 0
    )
    own_ada = lax.dynamic_slice_in_dim(ada_proj, item_me * block, block, 0).astype(jnp.float32)
    grad_cond = lax.dot_general(modul_all, own_ada, (((1,), (1,)), ((), ())), precision=HIGHEST)
    sum_embed = lax.dot_general(
        onehot_all, grad_cond, (((0,), (0,)), ((), ())), precision=HIGHEST
    )
    return (
        out_frames[None],
        frames_grad[None],
        sum_embed,
        sum_ada,
        sum_bias,
        sum_qkv,
        sum_out,
        sum_up,
        sum_down,
    )


def solution(mesh):
    in_specs = (
        P("items", "seq", None),
        P("items", "seq", None),
        P("items"),
        P("items"),
        P(),
        P(),
        P(),
        P(),
        P(),
        P(),
        P(),
    )
    out_specs = (
        P("items", "seq", None),
        P("items", "seq", None),
        P(None, "items"),
        P("items", None),
        P("items"),
        P("items", None),
        P("items", None),
        P("items", None),
        P("items", None),
    )
    return jax.shard_map(
        per_device, mesh=mesh, in_specs=in_specs, out_specs=out_specs, check_vma=False
    )
```

```python
import functools

import jax
import jax.numpy as jnp
from jax import lax
from jax.experimental import pallas as pl
from jax.experimental.pallas import tpu as pltpu
from jax.sharding import PartitionSpec as P

HEADS = 16


EPS = 1e-05
NEGATIVE = -1e30
SQRT_HALF = 0.7071067811865476
INV_SQRT_TAU = 0.3989422804014327
HIGHEST = lax.Precision.HIGHEST


def normalize(values):
    mean = jnp.mean(values, -1, keepdims=True)
    centered = values - mean
    inverse = lax.rsqrt(jnp.mean(centered * centered, -1, keepdims=True) + EPS)
    return (centered * inverse, inverse)


def norm_back(grad, normed, inverse):
    first = jnp.mean(grad, -1, keepdims=True)
    second = jnp.mean(grad * normed, -1, keepdims=True)
    return (grad - first - normed * second) * inverse


def gelu_exact(values):
    return 0.5 * values * (1.0 + lax.erf(values * SQRT_HALF))


def gelu_slope(values):
    return (
        0.5 * (1.0 + lax.erf(values * SQRT_HALF))
        + values * jnp.exp(-0.5 * values * values) * INV_SQRT_TAU
    )


def project(left, weight):
    flat = left.reshape(-1, left.shape[-1])
    result = jnp.dot(flat, weight, preferred_element_type=jnp.float32)
    return result.reshape(left.shape[:-1] + (weight.shape[1],))


def back_project(grad, weight):
    flat = grad.reshape(-1, grad.shape[-1])
    result = lax.dot_general(
        flat, weight, (((1,), (1,)), ((), ())), preferred_element_type=jnp.float32
    )
    return result.reshape(grad.shape[:-1] + (weight.shape[0],))


BIG = 1e30

def split3(x):
    hi = x.astype(jnp.bfloat16).astype(jnp.float32)
    rest = x - hi
    mid = rest.astype(jnp.bfloat16).astype(jnp.float32)
    return hi, mid, rest - mid

def dot(a, b, ca, cb):
    return lax.dot_general(a, b, (((ca,), (cb,)), ((), ())), preferred_element_type=jnp.float32)


def fwd_kernel(rows, blocks, lim_ref, q_ref, ko_ref, vo_ref, kt_ref, vt_ref, o_ref, lse_ref):
    lane = lax.broadcasted_iota(jnp.int32, (1, 128), 1)
    low = lane < 64
    row = lax.broadcasted_iota(jnp.int32, (rows, 1), 0)
    q = q_ref[...].astype(jnp.float32) * 0.125
    outs, lses = [], []
    for h in range(2):
        own = low if h == 0 else jnp.logical_not(low)
        first = 64 * (1 - h)
        qa = jnp.where(own, q, jnp.where(lane == first, 1.0, 0.0)).astype(jnp.bfloat16)
        scores, values = [], []
        for j in range(blocks):
            k = ko_ref[...] if j == 0 else kt_ref[pl.ds((j - 1) * rows, rows), :]
            v = vo_ref[...] if j == 0 else vt_ref[pl.ds((j - 1) * rows, rows), :]
            bias = jnp.where(row < lim_ref[j], 0.0, -BIG)
            ka = jnp.where(own, k.astype(jnp.float32), jnp.where(lane == first, bias, 0.0)).astype(jnp.bfloat16)
            va = jnp.where(own, v.astype(jnp.float32), 1.0).astype(jnp.bfloat16)
            scores.append(dot(qa, ka, 1, 1))
            values.append(va)
        top = functools.reduce(jnp.maximum, [jnp.max(s, -1, keepdims=True) for s in scores])
        total = None
        for s, va in zip(scores, values):
            p = jnp.exp(s - top).astype(jnp.bfloat16)
            part = dot(p, va, 1, 0)
            total = part if total is None else total + part
        outs.append(total / pltpu.roll(total, 64, 1))
        lses.append(top + jnp.log(total))
    o_ref[...] = jnp.where(low, outs[0], outs[1]).astype(o_ref.dtype)
    lse_ref[...] = jnp.where(low, lses[1], lses[0])


def bwd_kernel(rows, blocks, lim_ref, q_ref, ko_ref, vo_ref, kt_ref, vt_ref, do_ref, o_ref, lse_ref,
               dq_ref, dko_ref, dvo_ref, dkt_ref, dvt_ref):
    lane = lax.broadcasted_iota(jnp.int32, (1, 128), 1)
    low = lane < 64
    row = lax.broadcasted_iota(jnp.int32, (rows, 1), 0)
    q = q_ref[...].astype(jnp.float32) * 0.125
    qs = q.astype(jnp.bfloat16)
    do_low = do_ref[...]
    do = do_low.astype(jnp.float32)
    prod = do * o_ref[...].astype(jnp.float32)
    lh, lm, ll = split3(lse_ref[...])
    heads = []
    for h in range(2):
        own = low if h == 0 else jnp.logical_not(low)
        f = 64 * (1 - h)
        delta = jnp.sum(jnp.where(own, prod, 0.0), -1, keepdims=True)
        dh, dm, dl = split3(delta)
        qa = jnp.where(own, q, jnp.where(lane == f, 1.0, jnp.where(lane == f + 1, -lh, jnp.where(lane == f + 2, -lm, jnp.where(lane == f + 3, -ll, 0.0))))).astype(jnp.bfloat16)
        doa = jnp.where(own, do, jnp.where(lane == f, -dh, jnp.where(lane == f + 1, -dm, jnp.where(lane == f + 2, -dl, 0.0)))).astype(jnp.bfloat16)
        kone = jnp.where((lane > f) & (lane <= f + 3), 1.0, 0.0)
        vone = jnp.where((lane >= f) & (lane < f + 3), 1.0, 0.0)
        dq = None
        res = []
        for j in range(blocks):
            k = ko_ref[...] if j == 0 else kt_ref[pl.ds((j - 1) * rows, rows), :]
            v = vo_ref[...] if j == 0 else vt_ref[pl.ds((j - 1) * rows, rows), :]
            bias = jnp.where(row < lim_ref[j], 0.0, -BIG)
            ka = jnp.where(own, k.astype(jnp.float32), jnp.where(lane == f, bias, kone)).astype(jnp.bfloat16)
            va = jnp.where(own, v.astype(jnp.float32), vone).astype(jnp.bfloat16)
            pt = jnp.exp(dot(ka, qa, 1, 1))
            dpt = dot(va, doa, 1, 1)
            dst = (pt * dpt).astype(jnp.bfloat16)
            dv = dot(pt.astype(jnp.bfloat16), do_low, 1, 0)
            dk = dot(dst, qs, 1, 0)
            part = dot(dst, k, 0, 0)
            dq = part if dq is None else dq + part
            res.append((dk, dv))
        heads.append((dq, res))
    dq_ref[...] = (jnp.where(low, heads[0][0], heads[1][0]) * 0.125).astype(dq_ref.dtype)
    for j in range(blocks):
        dk = jnp.where(low, heads[0][1][j][0], heads[1][1][j][0]).astype(dko_ref.dtype)
        dv = jnp.where(low, heads[0][1][j][1], heads[1][1][j][1]).astype(dko_ref.dtype)
        if j == 0:
            dko_ref[...] = dk
            dvo_ref[...] = dv
        else:
            dkt_ref[pl.ds((j - 1) * rows, rows), :] = dk
            dvt_ref[pl.ds((j - 1) * rows, rows), :] = dv


def specs_of(rows, others, width):
    pairs = width // 128
    place = lambda count, skip: pl.BlockSpec((count, 128), lambda i, lim: (0, i + skip))
    inputs = [place(rows, 0), place(rows, pairs), place(rows, 2 * pairs), place(others, 0), place(others, pairs)]
    return inputs, place(rows, 0), place(others, 0)


def attend(lim, qkv, kv_rest, width):
    rows, others = qkv.shape[0], kv_rest.shape[0]
    blocks = 1 + others // rows
    inputs, own, oth = specs_of(rows, others, width)
    keys = rows + others
    return pl.pallas_call(
        functools.partial(fwd_kernel, rows, blocks),
        grid_spec=pltpu.PrefetchScalarGridSpec(num_scalar_prefetch=1, grid=(width // 128,),
            in_specs=inputs, out_specs=[own, own]),
        out_shape=[jax.ShapeDtypeStruct((rows, width), jnp.bfloat16), jax.ShapeDtypeStruct((rows, width), jnp.float32)],
        compiler_params=pltpu.CompilerParams(vmem_limit_bytes=56 << 20),
        cost_estimate=pl.CostEstimate(flops=16 * rows * keys * width, transcendentals=rows * keys * width // 64,
            bytes_accessed=2 * width * (2 * rows + 2 * keys) + 4 * rows * width),
    )(lim, qkv, qkv, qkv, kv_rest, kv_rest)


def attend_back(lim, qkv, kv_rest, do, o, lse):
    (rows, width), others = do.shape, kv_rest.shape[0]
    blocks = 1 + others // rows
    inputs, own, oth = specs_of(rows, others, width)
    keys = rows + others
    s = lambda n: jax.ShapeDtypeStruct((n, width), jnp.bfloat16)
    return pl.pallas_call(
        functools.partial(bwd_kernel, rows, blocks),
        grid_spec=pltpu.PrefetchScalarGridSpec(num_scalar_prefetch=1, grid=(width // 128,),
            in_specs=inputs + [own, own, own], out_specs=[own, own, own, oth, oth]),
        out_shape=[s(rows), s(rows), s(rows), s(others), s(others)],
        compiler_params=pltpu.CompilerParams(vmem_limit_bytes=56 << 20),
        cost_estimate=pl.CostEstimate(flops=40 * rows * keys * width, transcendentals=rows * keys * width // 64,
            bytes_accessed=2 * width * (4 * rows + 4 * keys) + 4 * rows * width),
    )(lim, qkv, qkv, qkv, kv_rest, kv_rest, do, o, lse)


def outer_sum(left, right):
    return lax.dot_general(
        left, right, (((0,), (0,)), ((), ())), preferred_element_type=jnp.float32
    )


def outer_kernel(plan, halves, first_tiles, side_ref, *refs):
    lefts, plan_rights, outs, turned = refs[: plan[0]], refs[plan[0] : plan[1]], refs[plan[1] : plan[1] + 4], refs[plan[1] + 4 :]
    step = pl.program_id(0)

    @pl.when(step == 0)
    def _():
        for left, flip in zip(lefts, turned):
            flip[...] = left[...].T

    at = 0
    place = 0
    for tiles, terms in plan[2]:
        rights = plan_rights[place : place + len(terms)]
        place += len(terms)

        @pl.when((step >= at) & (step < at + tiles))
        def _(rights=rights, terms=terms):
            total = None
            for which, right in zip(terms, rights):
                part = dot(turned[which][...], right[...], 1, 0)
                total = part if total is None else total + part
            rows, columns = total.shape
            split = total.astype(jnp.bfloat16).reshape(halves, 2, rows // (2 * halves), columns)
            even = side_ref[0] == 0
            keep = jnp.where(even, split[:, 0], split[:, 1])
            send = jnp.where(even, split[:, 1], split[:, 0])

            @pl.when(step < first_tiles)
            def _():
                outs[0][...] = send
                outs[1][...] = keep

            @pl.when(step >= first_tiles)
            def _():
                outs[2][...] = send
                outs[3][...] = keep

        at += tiles


def outer(side, lefts, segments, parts, tile):
    rows = lefts[0].shape[1]
    halves = parts // 2
    block = rows // parts
    width = sum(segment[0][1].shape[1] for segment in segments)
    steps = width // tile
    first_tiles = steps // 2
    in_specs = [pl.BlockSpec(left.shape, lambda i, s: (0, 0)) for left in lefts]
    operands = list(lefts)
    plan = []
    at = 0
    flops = 0
    for segment in segments:
        tiles = segment[0][1].shape[1] // tile
        for which, right in segment:
            in_specs.append(
                pl.BlockSpec(
                    (right.shape[0], tile),
                    lambda i, s, at=at, tiles=tiles: (0, jnp.clip(i - at, 0, tiles - 1)),
                )
            )
            operands.append(right)
            flops += 2 * rows * right.shape[0] * right.shape[1]
        plan.append((tiles, tuple(which for which, _ in segment)))
        at += tiles
    first = pl.BlockSpec((halves, block, tile), lambda i, s: (0, 0, jnp.minimum(i, first_tiles - 1)))
    second = pl.BlockSpec((halves, block, tile), lambda i, s: (0, 0, jnp.maximum(i - first_tiles, 0)))
    shape = lambda count: jax.ShapeDtypeStruct((halves, block, count * tile), jnp.bfloat16)
    moved = sum(2 * operand.size for operand in operands) + 2 * rows * width
    return pl.pallas_call(
        functools.partial(
            outer_kernel, (len(lefts), len(operands), tuple(plan)), halves, first_tiles
        ),
        grid_spec=pltpu.PrefetchScalarGridSpec(
            num_scalar_prefetch=1,
            grid=(steps,),
            in_specs=in_specs,
            out_specs=[first, first, second, second],
            scratch_shapes=[pltpu.VMEM(left.shape[::-1], jnp.bfloat16) for left in lefts],
        ),
        out_shape=[shape(first_tiles)] * 2 + [shape(steps - first_tiles)] * 2,
        compiler_params=pltpu.CompilerParams(vmem_limit_bytes=58 << 20),
        cost_estimate=pl.CostEstimate(flops=flops, transcendentals=0, bytes_accessed=moved),
    )(side, *operands)


def swap(values, axis, bit):
    size = lax.axis_size(axis)
    return lax.ppermute(values, axis, [(i, i ^ bit) for i in range(size)])


def bits_of(axis):
    size = lax.axis_size(axis)
    return [1 << place for place in range(size.bit_length() - 1)]


def add_low(left, right):
    return (left.astype(jnp.float32) + right.astype(jnp.float32)).astype(jnp.bfloat16)


def half_of(values, dim, which):
    return lax.dynamic_index_in_dim(values, which, dim, keepdims=False)


def reduce_rows(keep, got, axis):
    me = lax.axis_index(axis)
    for bit in bits_of(axis)[1:]:
        mine = jnp.bitwise_and(me // bit, 1)
        shape = keep.shape
        view = (shape[0] // 2, 2) + shape[1:]
        keep, got = keep.reshape(view), got.reshape(view)
        send = add_low(half_of(keep, 1, 1 - mine), half_of(got, 1, 1 - mine))
        keep = add_low(half_of(keep, 1, mine), half_of(got, 1, mine))
        got = swap(send, axis, bit)
    return keep, got


def finish(pieces, rows_axis, seq_axis):
    send_a, keep_a, send_b, keep_b = pieces
    got_a = swap(send_a, rows_axis, 1)
    got_b = swap(send_b, rows_axis, 1)
    keep_a, got_a = reduce_rows(keep_a, got_a, rows_axis)
    total_a = (keep_a.astype(jnp.float32) + got_a.astype(jnp.float32))[0]
    for bit in bits_of(seq_axis):
        low = total_a.astype(jnp.bfloat16)
        total_a = low.astype(jnp.float32) + swap(low, seq_axis, bit).astype(jnp.float32)
    me = lax.axis_index(seq_axis)
    for bit in bits_of(seq_axis):
        mine = jnp.bitwise_and(me // bit, 1)
        width = keep_b.shape[-1] // 2
        cut = lambda values, which: lax.dynamic_slice_in_dim(values, which * width, width, 2)
        send = add_low(cut(keep_b, 1 - mine), cut(got_b, 1 - mine))
        keep_b = add_low(cut(keep_b, mine), cut(got_b, mine))
        got_b = swap(send, seq_axis, bit)
    keep_b, got_b = reduce_rows(keep_b, got_b, rows_axis)
    total_b = add_low(keep_b, got_b)[0]
    for bit in reversed(bits_of(seq_axis)):
        mine = jnp.bitwise_and(me // bit, 1)
        other = swap(total_b, seq_axis, bit)
        total_b = jnp.where(
            mine == 0,
            jnp.concatenate([total_b, other], -1),
            jnp.concatenate([other, total_b], -1),
        )
    return jnp.concatenate([total_a, total_b.astype(jnp.float32)], -1)


def gather_items(values, axis):
    me = lax.axis_index(axis)
    for bit in bits_of(axis):
        other = swap(values, axis, bit)
        mine = jnp.bitwise_and(me // bit, 1)
        values = jnp.where(
            mine == 0, jnp.concatenate([values, other]), jnp.concatenate([other, values])
        )
    return values


LAG = 2
STAGES = 6
MESH = pl.DeviceIdType.MESH


def sum_kernel(units, plan, left_count, right_count, *refs):
    lefts = refs[:left_count]
    rights = refs[left_count : left_count + right_count]
    vector = refs[left_count + right_count]
    rest = refs[left_count + right_count + 1 :]
    outs, gathered_out, rest = rest[: len(plan)], rest[len(plan)], rest[len(plan) + 1 :]
    turned, rest = rest[:left_count], rest[left_count:]
    (send0, recv0, keep0, send_y, recv_y, send_x, recv_x) = rest[:7]
    (send_z, recv_z, send_w, recv_w, keep_a, keep_b, last_a, last_b) = rest[7:15]
    (gathered, got_vector, out_sem, in_sem, vec_out, vec_in) = rest[15:]
    tick = pl.program_id(0)
    item, seq = lax.axis_index("items"), lax.axis_index("seq")
    bit = lambda value, place: jnp.bitwise_and(value // (1 << place), 1)
    core, y, z0, z1, x = bit(item, 0), bit(item, 1), bit(item, 2), bit(item, 3), seq
    flip = lambda place: item + (1 - 2 * bit(item, place)) * (1 << place)
    partners = {
        "core": (flip(0), seq),
        "y": (flip(1), seq),
        "z0": (flip(2), seq),
        "z1": (flip(3), seq),
        "x": (item, 1 - seq),
    }

    @pl.when(tick == 0)
    def _():
        barrier = pltpu.get_barrier_semaphore()
        for partner in partners.values():
            pl.semaphore_signal(barrier, inc=1, device_id=partner, device_id_type=MESH)
        pl.semaphore_wait(barrier, len(partners))

    def copy(kind, number, unit, source, target, to):
        slot, landing = unit % 2, unit % 4
        return pltpu.make_async_remote_copy(
            src_ref=source.at[slot],
            dst_ref=target.at[landing],
            send_sem=out_sem.at[number, slot],
            recv_sem=in_sem.at[number, landing],
            device_id=partners[to],
            device_id_type=MESH,
        )

    wide = lambda values: values.astype(jnp.float32)
    low = lambda values: values.astype(jnp.bfloat16)

    def choose(values, axis, which):
        first = lax.index_in_dim(values, 0, axis, keepdims=False)
        second = lax.index_in_dim(values, 1, axis, keepdims=False)
        mine = jnp.where(which == 0, first, second)
        other = jnp.where(which == 0, second, first)
        return mine, other

    names = [
        ("d", send0, recv0, "core"),
        ("ay", send_y[0], recv_y[0], "y"),
        ("az", send_z[0], recv_z[0], "z0"),
        ("aw", send_w[0], recv_w[0], "z1"),
        ("ax", send_x[0], recv_x[0], "x"),
        ("bx", send_x[1], recv_x[1], "x"),
        ("by", send_y[1], recv_y[1], "y"),
        ("bz", send_z[1], recv_z[1], "z0"),
        ("bw", send_w[1], recv_w[1], "z1"),
        ("bg", send_x[2], recv_x[2], "x"),
    ]
    table = {name: (i, source, target, to) for i, (name, source, target, to) in enumerate(names)}

    def post(name, unit, values):
        number, source, target, to = table[name]
        source[unit % 2] = low(values)
        copy(name, number, unit, source, target, to).start()

    def take(name, unit):
        number, source, target, to = table[name]
        copy(name, number, unit, source, target, to).wait()
        return wide(target[unit % 4])

    def stage_final(unit, offset):
        other = take("bg", unit)
        mine = last_b[unit % 2]
        top = jnp.where(x == 0, mine, other)
        bottom = jnp.where(x == 0, other, mine)
        block = jnp.concatenate(
            [last_a[unit % 2], jnp.concatenate([top, bottom], 0)], 1
        )
        at = 0
        for (count, _, _), out in zip(plan, outs):

            @pl.when((unit >= at) & (unit < at + count))
            def _(out=out):
                out[...] = block

            at += count

    def stage_five(unit):
        last_a[unit % 2] = keep_a[3][unit % 2] + take("ax", unit)
        total = low(keep_b[3][unit % 2] + take("bw", unit))
        last_b[unit % 2] = wide(total)
        post("bg", unit, total)

    def stage_four(unit):
        total = low(keep_a[2][unit % 2] + take("aw", unit))
        keep_a[3][unit % 2] = wide(total)
        post("ax", unit, total)
        mine, other = choose(keep_b[2][unit % 2] + take("bz", unit), 0, z1)
        keep_b[3][unit % 2] = mine
        post("bw", unit, other)

    def stage_three(unit):
        mine, other = choose(keep_a[1][unit % 2] + take("az", unit), 0, z1)
        keep_a[2][unit % 2] = mine
        post("aw", unit, other)
        total = keep_b[1][unit % 2] + take("by", unit)
        mine, other = choose(total.reshape(2, 2, 32, 128), 1, z0)
        keep_b[2][unit % 2] = mine
        post("bz", unit, other)

    def stage_two(unit):
        total = keep_a[0][unit % 2] + take("ay", unit)
        mine, other = choose(total.reshape(2, 2, 64, 128), 1, z0)
        keep_a[1][unit % 2] = mine
        post("az", unit, other)
        total = keep_b[0][unit % 2] + take("bx", unit)
        mine, other = choose(total.reshape(4, 2, 32, 128), 1, y)
        keep_b[1][unit % 2] = mine
        post("by", unit, other)

    def stage_one(unit):
        total = keep0[unit % 2] + take("d", unit)
        mine, other = choose(total[:, :, :128].reshape(4, 2, 64, 128), 1, y)
        keep_a[0][unit % 2] = mine
        post("ay", unit, other)
        mine, other = choose(total[:, :, 128:].reshape(8, 2, 32, 128), 1, x)
        keep_b[0][unit % 2] = mine
        post("bx", unit, other)

    def stage_zero(unit):
        at = 0
        for count, terms, turns in plan:

            @pl.when((unit >= at) & (unit < at + count))
            def _(at=at, terms=terms, turns=turns):
                for which, start in turns:

                    @pl.when(unit == at + start)
                    def _(which=which):
                        turned[which][...] = lefts[which][...].T

                place = 0
                for segment, pairs in terms:

                    @pl.when((unit >= at + place) & (unit < at + place + segment))
                    def _(pairs=pairs):
                        total = None
                        for which, right in pairs:
                            part = dot(turned[which][...], rights[right][...], 1, 0)
                            total = part if total is None else total + part
                        mine, other = choose(total.reshape(8, 2, 64, 256), 1, core)
                        keep0[unit % 2] = mine
                        post("d", unit, other)

                    place += segment

            at += count

    steps = [stage_zero, stage_one, stage_two, stage_three, stage_four, stage_five, stage_final]
    for number in range(STAGES, -1, -1):
        unit = tick - LAG * number

        @pl.when((unit >= 0) & (unit < units))
        def _(number=number, unit=unit):
            if number == STAGES:
                stage_final(unit, 0)
            else:
                steps[number](unit)

    def vec_copy(number, source, target, to):
        return pltpu.make_async_remote_copy(
            src_ref=source,
            dst_ref=target,
            send_sem=vec_out.at[number],
            recv_sem=vec_in.at[number],
            device_id=partners[to],
            device_id_type=MESH,
        )

    first = vec_copy(0, vector, got_vector, "x")
    hops = []
    for number, to in enumerate(("core", "y", "z0", "z1")):
        count = 1 << number
        run = gathered.at[pl.ds((item // count) * count, count)]
        hops.append(vec_copy(number + 1, run, run, to))

    @pl.when(tick == 0)
    def _():
        first.start()

    @pl.when(tick == LAG)
    def _():
        first.wait()
        heights = lax.broadcasted_iota(jnp.int32, vector.shape, 0)
        gathered[item] = vector[...] + jnp.where(heights < vector.shape[0] - 8, got_vector[...], 0.0)
        hops[0].start()

    for number in range(4):

        @pl.when(tick == LAG * (number + 2))
        def _(number=number):
            hops[number].wait()
            if number < 3:
                hops[number + 1].start()
            else:
                gathered_out[...] = gathered[...]


def sum_weights(weights, lefts, vector):
    tile = 256
    rows = lefts[0].shape[1]
    operands, in_specs, plan, out_specs, out_shape = [], [], [], [], []
    for left in lefts:
        in_specs.append(
            pl.BlockSpec(left.shape, lambda i: (0, 0), pipeline_mode=pl.Buffered(1))
        )
    seen = set()
    at = 0
    flops = 0
    for weight in weights:
        terms, turns = [], []
        place = 0
        for segment in weight:
            count = segment[0][1].shape[1] // tile
            pairs = []
            for which, right in segment:
                if which not in seen:
                    seen.add(which)
                    turns.append((which, place))
                pairs.append((which, len(operands)))
                operands.append(right)
                flops += 2 * rows * right.shape[0] * right.shape[1]
                in_specs.append(
                    pl.BlockSpec(
                        (right.shape[0], tile),
                        lambda i, start=at + place, count=count: (
                            0,
                            jnp.clip(i - start, 0, count - 1),
                        ),
                    )
                )
            terms.append((count, tuple(pairs)))
            place += count
        plan.append((place, tuple(terms), tuple(turns)))
        out_specs.append(
            pl.BlockSpec(
                (64, tile),
                lambda i, start=at, count=place: (
                    0,
                    jnp.clip(i - LAG * STAGES - start, 0, count - 1),
                ),
            )
        )
        out_shape.append(jax.ShapeDtypeStruct((64, place * tile), jnp.float32))
        at += place
    units = at
    in_specs.append(pl.BlockSpec(vector.shape, lambda i: (0, 0)))
    out_specs.append(pl.BlockSpec((16,) + vector.shape, lambda i: (0, 0, 0)))
    out_shape.append(jax.ShapeDtypeStruct((16,) + vector.shape, jnp.float32))
    low = lambda *shape: pltpu.VMEM(shape, jnp.bfloat16)
    full = lambda *shape: pltpu.VMEM(shape, jnp.float32)
    scratch = [low(*left.shape[::-1]) for left in lefts]
    scratch += [low(2, 8, 64, 256), low(4, 8, 64, 256), full(2, 8, 64, 256)]
    scratch += [
        (low(2, 4, 64, 128), low(2, 4, 32, 128)),
        (low(4, 4, 64, 128), low(4, 4, 32, 128)),
        (low(2, 64, 128), low(2, 8, 32, 128), low(2, 32, 128)),
        (low(4, 64, 128), low(4, 8, 32, 128), low(4, 32, 128)),
        (low(2, 2, 64, 128), low(2, 2, 32, 128)),
        (low(4, 2, 64, 128), low(4, 2, 32, 128)),
        (low(2, 64, 128), low(2, 32, 128)),
        (low(4, 64, 128), low(4, 32, 128)),
        (full(2, 4, 64, 128), full(2, 2, 64, 128), full(2, 64, 128), full(2, 64, 128)),
        (full(2, 8, 32, 128), full(2, 4, 32, 128), full(2, 2, 32, 128), full(2, 32, 128)),
        full(2, 64, 128),
        full(2, 32, 128),
        full(16, *vector.shape),
        full(*vector.shape),
        pltpu.SemaphoreType.DMA((10, 2)),
        pltpu.SemaphoreType.DMA((10, 4)),
        pltpu.SemaphoreType.DMA((5,)),
        pltpu.SemaphoreType.DMA((5,)),
    ]
    moved = sum(2 * a.size for a in operands) + sum(2 * a.size for a in lefts)
    return pl.pallas_call(
        functools.partial(sum_kernel, units, tuple(plan), len(lefts), len(operands)),
        grid=(units + LAG * STAGES,),
        in_specs=in_specs,
        out_specs=out_specs,
        out_shape=out_shape,
        scratch_shapes=scratch,
        compiler_params=pltpu.CompilerParams(
            vmem_limit_bytes=58 << 20, collective_id=0, has_side_effects=True
        ),
        cost_estimate=pl.CostEstimate(flops=flops, transcendentals=0, bytes_accessed=moved),
    )(*lefts, *operands, vector)


def per_device(
    frames,
    cotangent,
    section,
    prompt_len,
    section_embed,
    ada_proj,
    ada_bias,
    w_qkv,
    w_out,
    w_up,
    w_down,
):
    _, row_count, width = frames.shape
    frames, cotangent = frames[0], cotangent[0]
    seq_size = lax.axis_size("seq")
    item_size = lax.axis_size("items")
    seq_me, item_me = lax.axis_index("seq"), lax.axis_index("items")
    side = jnp.bitwise_and(item_me, 1).astype(jnp.int32).reshape(1)
    turns = list(range(1, seq_size))
    fetch = lambda values, turn: lax.ppermute(
        values, "seq", [((i + turn) % seq_size, i) for i in range(seq_size)]
    )
    give = lambda values, turn: lax.ppermute(
        values, "seq", [(i, (i + turn) % seq_size) for i in range(seq_size)]
    )
    others = [fetch(frames, turn) for turn in turns]
    sources = jnp.stack([(seq_me + turn) % seq_size for turn in [0] + turns])
    limits = jnp.where(sources == 0, prompt_len[0], row_count).astype(jnp.int32)

    section_count = section_embed.shape[0]
    onehot = (section[:, None] == jnp.arange(section_count, dtype=jnp.int32)[None, :]).astype(
        jnp.float32
    )
    cond = jnp.dot(onehot, section_embed, precision=HIGHEST)
    modul = jnp.dot(cond, ada_proj.astype(jnp.float32), precision=HIGHEST) + ada_bias[None, :]
    scale_one, shift_one, scale_two, shift_two = jnp.split(modul, 4, axis=-1)
    inputs = frames.astype(jnp.float32)
    normed_one, inv_one = normalize(inputs)
    modulate = lambda normed: (normed * (1.0 + scale_one) + shift_one).astype(jnp.bfloat16)
    attn_in = modulate(normed_one)
    qkv = project(attn_in, w_qkv).astype(jnp.bfloat16)
    rest = jnp.concatenate(others) if len(others) > 1 else others[0]
    normed_rest, _ = normalize(rest.astype(jnp.float32))
    attn_rest = modulate(normed_rest)
    kv_rest = project(attn_rest, w_qkv[:, width:]).astype(jnp.bfloat16)
    att, lse = attend(limits, qkv, kv_rest, width)
    mid = inputs + project(att, w_out)
    normed_two, inv_two = normalize(mid)
    ffn_in = (normed_two * (1.0 + scale_two) + shift_two).astype(jnp.bfloat16)
    upper = project(ffn_in, w_up)
    act = gelu_exact(upper).astype(jnp.bfloat16)
    out_frames = (mid + project(act, w_down)).astype(jnp.bfloat16)

    grad_out = cotangent.astype(jnp.float32)
    fused = seq_size == 2 and item_size == 16 and width == 1024
    if fused:
        sum_down = lax.psum_scatter(
            outer_sum(act, cotangent).astype(jnp.bfloat16),
            "items",
            scatter_dimension=0,
            tiled=True,
        )
    else:
        down_pieces = outer(side, [act], [[(0, cotangent)]], item_size, 256)
    grad_upper = (back_project(cotangent, w_down) * gelu_slope(upper)).astype(jnp.bfloat16)
    grad_ffn_in = back_project(grad_upper, w_up)
    grad_scale_two = jnp.sum(grad_ffn_in * normed_two, 0)
    grad_shift_two = jnp.sum(grad_ffn_in, 0)
    grad_mid = grad_out + norm_back(grad_ffn_in * (1.0 + scale_two), normed_two, inv_two)
    grad_mid_low = grad_mid.astype(jnp.bfloat16)
    grad_att = back_project(grad_mid_low, w_out).astype(jnp.bfloat16)
    grad_query, grad_key, grad_value, key_rest, value_rest = attend_back(
        limits, qkv, kv_rest, grad_att, att, lse
    )
    up_terms = [[(0, grad_upper)]]
    out_terms = [[(1, grad_mid_low)]]
    qkv_terms = [
        [(2, grad_query)],
        [(2, grad_key), (3, key_rest)],
        [(2, grad_value), (3, value_rest)],
    ]
    w_key, w_value = w_qkv[:, width : 2 * width], w_qkv[:, 2 * width :]
    share = back_project(key_rest, w_key) + back_project(value_rest, w_value)
    grad_rest = [
        give(share[i * row_count : (i + 1) * row_count].astype(jnp.bfloat16), turn)
        for i, turn in enumerate(turns)
    ]
    partial = (
        back_project(grad_query, w_qkv[:, :width])
        + back_project(grad_key, w_key)
        + back_project(grad_value, w_value)
    )
    grad_scale_one = jnp.sum(partial * normed_one, 0) + jnp.sum(share * normed_rest, 0)
    grad_shift_one = jnp.sum(partial, 0) + jnp.sum(share, 0)
    grad_attn_in = partial
    for got in grad_rest:
        grad_attn_in = grad_attn_in + got.astype(jnp.float32)
    frames_grad = (
        grad_mid + norm_back(grad_attn_in * (1.0 + scale_one), normed_one, inv_one)
    ).astype(jnp.bfloat16)

    grad_modul = jnp.concatenate(
        [grad_scale_one, grad_shift_one, grad_scale_two, grad_shift_two]
    )[None, :]
    if fused:
        vector = jnp.concatenate(
            [
                grad_modul.reshape(4 * width // 128, 128),
                jnp.pad(onehot, ((0, 7), (0, 128 - section_count))),
            ]
        )
        sum_up, sum_out, sum_qkv, tagged = sum_weights(
            [up_terms, out_terms, qkv_terms], [ffn_in, att, attn_in, attn_rest], vector
        )
        tagged = tagged[:, : 4 * width // 128 + 1].reshape(item_size, 4 * width + 128)
        sum_down = sum_down.astype(jnp.float32) + swap(sum_down, "seq", 1).astype(jnp.float32)
    else:
        shift = lambda terms, by: [[(i - by, right) for i, right in run] for run in terms]
        sum_down = finish(down_pieces, "items", "seq")
        sum_up = finish(outer(side, [ffn_in], up_terms, item_size, 512), "items", "seq")
        sum_out = finish(
            outer(side, [att], shift(out_terms, 1), item_size, 512), "items", "seq"
        )
        sum_qkv = finish(
            outer(side, [attn_in, attn_rest], shift(qkv_terms, 2), item_size, 512),
            "items",
            "seq",
        )
        for bit in bits_of("seq"):
            grad_modul = grad_modul + swap(grad_modul, "seq", bit)
        tagged = jnp.concatenate(
            [grad_modul, jnp.pad(onehot, ((0, 0), (0, 128 - section_count)))], -1
        )
        tagged = gather_items(tagged, "items")
    modul_all, onehot_all = tagged[:, : 4 * width], tagged[:, 4 * width :][:, :section_count]
    block = width // item_size
    own_embed = lax.dynamic_slice_in_dim(section_embed, item_me * block, block, 1)
    own_cond = jnp.dot(onehot_all, own_embed, precision=HIGHEST)
    sum_ada = lax.dot_general(own_cond, modul_all, (((0,), (0,)), ((), ())), precision=HIGHEST)
    sum_bias = jnp.sum(
        lax.dynamic_slice_in_dim(modul_all, item_me * 4 * block, 4 * block, 1), 0
    )
    own_ada = lax.dynamic_slice_in_dim(ada_proj, item_me * block, block, 0).astype(jnp.float32)
    grad_cond = lax.dot_general(modul_all, own_ada, (((1,), (1,)), ((), ())), precision=HIGHEST)
    sum_embed = lax.dot_general(
        onehot_all, grad_cond, (((0,), (0,)), ((), ())), precision=HIGHEST
    )
    return (
        out_frames[None],
        frames_grad[None],
        sum_embed,
        sum_ada,
        sum_bias,
        sum_qkv,
        sum_out,
        sum_up,
        sum_down,
    )


def solution(mesh):
    in_specs = (
        P("items", "seq", None),
        P("items", "seq", None),
        P("items"),
        P("items"),
        P(),
        P(),
        P(),
        P(),
        P(),
        P(),
        P(),
    )
    out_specs = (
        P("items", "seq", None),
        P("items", "seq", None),
        P(None, "items"),
        P("items", None),
        P("items"),
        P("items", None),
        P("items", None),
        P("items", None),
        P("items", None),
    )
    return jax.shard_map(
        per_device, mesh=mesh, in_specs=in_specs, out_specs=out_specs, check_vma=False
    )
```

```python
import functools

import jax
import jax.numpy as jnp
from jax import lax
from jax.experimental import pallas as pl
from jax.experimental.pallas import tpu as pltpu
from jax.sharding import PartitionSpec as P

HEADS = 16


EPS = 1e-05
NEGATIVE = -1e30
SQRT_HALF = 0.7071067811865476
INV_SQRT_TAU = 0.3989422804014327
HIGHEST = lax.Precision.HIGHEST


def normalize(values):
    mean = jnp.mean(values, -1, keepdims=True)
    centered = values - mean
    inverse = lax.rsqrt(jnp.mean(centered * centered, -1, keepdims=True) + EPS)
    return (centered * inverse, inverse)


def norm_back(grad, normed, inverse):
    first = jnp.mean(grad, -1, keepdims=True)
    second = jnp.mean(grad * normed, -1, keepdims=True)
    return (grad - first - normed * second) * inverse


def gelu_exact(values):
    return 0.5 * values * (1.0 + lax.erf(values * SQRT_HALF))


def gelu_slope(values):
    return (
        0.5 * (1.0 + lax.erf(values * SQRT_HALF))
        + values * jnp.exp(-0.5 * values * values) * INV_SQRT_TAU
    )


def project(left, weight):
    flat = left.reshape(-1, left.shape[-1])
    result = jnp.dot(flat, weight, preferred_element_type=jnp.float32)
    return result.reshape(left.shape[:-1] + (weight.shape[1],))


def back_project(grad, weight):
    flat = grad.reshape(-1, grad.shape[-1])
    result = lax.dot_general(
        flat, weight, (((1,), (1,)), ((), ())), preferred_element_type=jnp.float32
    )
    return result.reshape(grad.shape[:-1] + (weight.shape[0],))


BIG = 1e30

def split3(x):
    hi = x.astype(jnp.bfloat16).astype(jnp.float32)
    rest = x - hi
    mid = rest.astype(jnp.bfloat16).astype(jnp.float32)
    return hi, mid, rest - mid

def dot(a, b, ca, cb):
    return lax.dot_general(a, b, (((ca,), (cb,)), ((), ())), preferred_element_type=jnp.float32)


def fwd_kernel(rows, blocks, lim_ref, q_ref, ko_ref, vo_ref, kt_ref, vt_ref, o_ref, lse_ref):
    lane = lax.broadcasted_iota(jnp.int32, (1, 128), 1)
    low = lane < 64
    row = lax.broadcasted_iota(jnp.int32, (rows, 1), 0)
    q = q_ref[...].astype(jnp.float32) * 0.125
    outs, lses = [], []
    for h in range(2):
        own = low if h == 0 else jnp.logical_not(low)
        first = 64 * (1 - h)
        qa = jnp.where(own, q, jnp.where(lane == first, 1.0, 0.0)).astype(jnp.bfloat16)
        scores, values = [], []
        for j in range(blocks):
            k = ko_ref[...] if j == 0 else kt_ref[pl.ds((j - 1) * rows, rows), :]
            v = vo_ref[...] if j == 0 else vt_ref[pl.ds((j - 1) * rows, rows), :]
            bias = jnp.where(row < lim_ref[j], 0.0, -BIG)
            ka = jnp.where(own, k.astype(jnp.float32), jnp.where(lane == first, bias, 0.0)).astype(jnp.bfloat16)
            va = jnp.where(own, v.astype(jnp.float32), 1.0).astype(jnp.bfloat16)
            scores.append(dot(qa, ka, 1, 1))
            values.append(va)
        top = functools.reduce(jnp.maximum, [jnp.max(s, -1, keepdims=True) for s in scores])
        total = None
        for s, va in zip(scores, values):
            p = jnp.exp(s - top).astype(jnp.bfloat16)
            part = dot(p, va, 1, 0)
            total = part if total is None else total + part
        outs.append(total / pltpu.roll(total, 64, 1))
        lses.append(top + jnp.log(total))
    o_ref[...] = jnp.where(low, outs[0], outs[1]).astype(o_ref.dtype)
    lse_ref[...] = jnp.where(low, lses[1], lses[0])


def bwd_kernel(rows, blocks, lim_ref, q_ref, ko_ref, vo_ref, kt_ref, vt_ref, do_ref, o_ref, lse_ref,
               dq_ref, dko_ref, dvo_ref, dkt_ref, dvt_ref):
    lane = lax.broadcasted_iota(jnp.int32, (1, 128), 1)
    low = lane < 64
    row = lax.broadcasted_iota(jnp.int32, (rows, 1), 0)
    q = q_ref[...].astype(jnp.float32) * 0.125
    qs = q.astype(jnp.bfloat16)
    do_low = do_ref[...]
    do = do_low.astype(jnp.float32)
    prod = do * o_ref[...].astype(jnp.float32)
    lh, lm, ll = split3(lse_ref[...])
    heads = []
    for h in range(2):
        own = low if h == 0 else jnp.logical_not(low)
        f = 64 * (1 - h)
        delta = jnp.sum(jnp.where(own, prod, 0.0), -1, keepdims=True)
        dh, dm, dl = split3(delta)
        qa = jnp.where(own, q, jnp.where(lane == f, 1.0, jnp.where(lane == f + 1, -lh, jnp.where(lane == f + 2, -lm, jnp.where(lane == f + 3, -ll, 0.0))))).astype(jnp.bfloat16)
        doa = jnp.where(own, do, jnp.where(lane == f, -dh, jnp.where(lane == f + 1, -dm, jnp.where(lane == f + 2, -dl, 0.0)))).astype(jnp.bfloat16)
        kone = jnp.where((lane > f) & (lane <= f + 3), 1.0, 0.0)
        vone = jnp.where((lane >= f) & (lane < f + 3), 1.0, 0.0)
        dq = None
        res = []
        for j in range(blocks):
            k = ko_ref[...] if j == 0 else kt_ref[pl.ds((j - 1) * rows, rows), :]
            v = vo_ref[...] if j == 0 else vt_ref[pl.ds((j - 1) * rows, rows), :]
            bias = jnp.where(row < lim_ref[j], 0.0, -BIG)
            ka = jnp.where(own, k.astype(jnp.float32), jnp.where(lane == f, bias, kone)).astype(jnp.bfloat16)
            va = jnp.where(own, v.astype(jnp.float32), vone).astype(jnp.bfloat16)
            pt = jnp.exp(dot(ka, qa, 1, 1))
            dpt = dot(va, doa, 1, 1)
            dst = (pt * dpt).astype(jnp.bfloat16)
            dv = dot(pt.astype(jnp.bfloat16), do_low, 1, 0)
            dk = dot(dst, qs, 1, 0)
            part = dot(dst, k, 0, 0)
            dq = part if dq is None else dq + part
            res.append((dk, dv))
        heads.append((dq, res))
    dq_ref[...] = (jnp.where(low, heads[0][0], heads[1][0]) * 0.125).astype(dq_ref.dtype)
    for j in range(blocks):
        dk = jnp.where(low, heads[0][1][j][0], heads[1][1][j][0]).astype(dko_ref.dtype)
        dv = jnp.where(low, heads[0][1][j][1], heads[1][1][j][1]).astype(dko_ref.dtype)
        if j == 0:
            dko_ref[...] = dk
            dvo_ref[...] = dv
        else:
            dkt_ref[pl.ds((j - 1) * rows, rows), :] = dk
            dvt_ref[pl.ds((j - 1) * rows, rows), :] = dv


def specs_of(rows, others, width):
    pairs = width // 128
    place = lambda count, skip: pl.BlockSpec((count, 128), lambda i, lim: (0, i + skip))
    inputs = [place(rows, 0), place(rows, pairs), place(rows, 2 * pairs), place(others, 0), place(others, pairs)]
    return inputs, place(rows, 0), place(others, 0)


def attend(lim, qkv, kv_rest, width):
    rows, others = qkv.shape[0], kv_rest.shape[0]
    blocks = 1 + others // rows
    inputs, own, oth = specs_of(rows, others, width)
    keys = rows + others
    return pl.pallas_call(
        functools.partial(fwd_kernel, rows, blocks),
        grid_spec=pltpu.PrefetchScalarGridSpec(num_scalar_prefetch=1, grid=(width // 128,),
            in_specs=inputs, out_specs=[own, own]),
        out_shape=[jax.ShapeDtypeStruct((rows, width), jnp.bfloat16), jax.ShapeDtypeStruct((rows, width), jnp.float32)],
        compiler_params=pltpu.CompilerParams(vmem_limit_bytes=56 << 20),
        cost_estimate=pl.CostEstimate(flops=16 * rows * keys * width, transcendentals=rows * keys * width // 64,
            bytes_accessed=2 * width * (2 * rows + 2 * keys) + 4 * rows * width),
    )(lim, qkv, qkv, qkv, kv_rest, kv_rest)


def attend_back(lim, qkv, kv_rest, do, o, lse):
    (rows, width), others = do.shape, kv_rest.shape[0]
    blocks = 1 + others // rows
    inputs, own, oth = specs_of(rows, others, width)
    keys = rows + others
    s = lambda n: jax.ShapeDtypeStruct((n, width), jnp.bfloat16)
    return pl.pallas_call(
        functools.partial(bwd_kernel, rows, blocks),
        grid_spec=pltpu.PrefetchScalarGridSpec(num_scalar_prefetch=1, grid=(width // 128,),
            in_specs=inputs + [own, own, own], out_specs=[own, own, own, oth, oth]),
        out_shape=[s(rows), s(rows), s(rows), s(others), s(others)],
        compiler_params=pltpu.CompilerParams(vmem_limit_bytes=56 << 20),
        cost_estimate=pl.CostEstimate(flops=40 * rows * keys * width, transcendentals=rows * keys * width // 64,
            bytes_accessed=2 * width * (4 * rows + 4 * keys) + 4 * rows * width),
    )(lim, qkv, qkv, qkv, kv_rest, kv_rest, do, o, lse)


def outer_sum(left, right):
    return lax.dot_general(
        left, right, (((0,), (0,)), ((), ())), preferred_element_type=jnp.float32
    )


def outer_kernel(plan, halves, first_tiles, side_ref, *refs):
    lefts, plan_rights, outs, turned = refs[: plan[0]], refs[plan[0] : plan[1]], refs[plan[1] : plan[1] + 4], refs[plan[1] + 4 :]
    step = pl.program_id(0)

    @pl.when(step == 0)
    def _():
        for left, flip in zip(lefts, turned):
            flip[...] = left[...].T

    at = 0
    place = 0
    for tiles, terms in plan[2]:
        rights = plan_rights[place : place + len(terms)]
        place += len(terms)

        @pl.when((step >= at) & (step < at + tiles))
        def _(rights=rights, terms=terms):
            total = None
            for which, right in zip(terms, rights):
                part = dot(turned[which][...], right[...], 1, 0)
                total = part if total is None else total + part
            rows, columns = total.shape
            split = total.astype(jnp.bfloat16).reshape(halves, 2, rows // (2 * halves), columns)
            even = side_ref[0] == 0
            keep = jnp.where(even, split[:, 0], split[:, 1])
            send = jnp.where(even, split[:, 1], split[:, 0])

            @pl.when(step < first_tiles)
            def _():
                outs[0][...] = send
                outs[1][...] = keep

            @pl.when(step >= first_tiles)
            def _():
                outs[2][...] = send
                outs[3][...] = keep

        at += tiles


def outer(side, lefts, segments, parts, tile):
    rows = lefts[0].shape[1]
    halves = parts // 2
    block = rows // parts
    width = sum(segment[0][1].shape[1] for segment in segments)
    steps = width // tile
    first_tiles = steps // 2
    in_specs = [pl.BlockSpec(left.shape, lambda i, s: (0, 0)) for left in lefts]
    operands = list(lefts)
    plan = []
    at = 0
    flops = 0
    for segment in segments:
        tiles = segment[0][1].shape[1] // tile
        for which, right in segment:
            in_specs.append(
                pl.BlockSpec(
                    (right.shape[0], tile),
                    lambda i, s, at=at, tiles=tiles: (0, jnp.clip(i - at, 0, tiles - 1)),
                )
            )
            operands.append(right)
            flops += 2 * rows * right.shape[0] * right.shape[1]
        plan.append((tiles, tuple(which for which, _ in segment)))
        at += tiles
    first = pl.BlockSpec((halves, block, tile), lambda i, s: (0, 0, jnp.minimum(i, first_tiles - 1)))
    second = pl.BlockSpec((halves, block, tile), lambda i, s: (0, 0, jnp.maximum(i - first_tiles, 0)))
    shape = lambda count: jax.ShapeDtypeStruct((halves, block, count * tile), jnp.bfloat16)
    moved = sum(2 * operand.size for operand in operands) + 2 * rows * width
    return pl.pallas_call(
        functools.partial(
            outer_kernel, (len(lefts), len(operands), tuple(plan)), halves, first_tiles
        ),
        grid_spec=pltpu.PrefetchScalarGridSpec(
            num_scalar_prefetch=1,
            grid=(steps,),
            in_specs=in_specs,
            out_specs=[first, first, second, second],
            scratch_shapes=[pltpu.VMEM(left.shape[::-1], jnp.bfloat16) for left in lefts],
        ),
        out_shape=[shape(first_tiles)] * 2 + [shape(steps - first_tiles)] * 2,
        compiler_params=pltpu.CompilerParams(vmem_limit_bytes=58 << 20),
        cost_estimate=pl.CostEstimate(flops=flops, transcendentals=0, bytes_accessed=moved),
    )(side, *operands)


def swap(values, axis, bit):
    size = lax.axis_size(axis)
    return lax.ppermute(values, axis, [(i, i ^ bit) for i in range(size)])


def bits_of(axis):
    size = lax.axis_size(axis)
    return [1 << place for place in range(size.bit_length() - 1)]


def add_low(left, right):
    return (left.astype(jnp.float32) + right.astype(jnp.float32)).astype(jnp.bfloat16)


def half_of(values, dim, which):
    return lax.dynamic_index_in_dim(values, which, dim, keepdims=False)


def reduce_rows(keep, got, axis):
    me = lax.axis_index(axis)
    for bit in bits_of(axis)[1:]:
        mine = jnp.bitwise_and(me // bit, 1)
        shape = keep.shape
        view = (shape[0] // 2, 2) + shape[1:]
        keep, got = keep.reshape(view), got.reshape(view)
        send = add_low(half_of(keep, 1, 1 - mine), half_of(got, 1, 1 - mine))
        keep = add_low(half_of(keep, 1, mine), half_of(got, 1, mine))
        got = swap(send, axis, bit)
    return keep, got


def finish(pieces, rows_axis, seq_axis):
    send_a, keep_a, send_b, keep_b = pieces
    got_a = swap(send_a, rows_axis, 1)
    got_b = swap(send_b, rows_axis, 1)
    keep_a, got_a = reduce_rows(keep_a, got_a, rows_axis)
    total_a = (keep_a.astype(jnp.float32) + got_a.astype(jnp.float32))[0]
    for bit in bits_of(seq_axis):
        low = total_a.astype(jnp.bfloat16)
        total_a = low.astype(jnp.float32) + swap(low, seq_axis, bit).astype(jnp.float32)
    me = lax.axis_index(seq_axis)
    for bit in bits_of(seq_axis):
        mine = jnp.bitwise_and(me // bit, 1)
        width = keep_b.shape[-1] // 2
        cut = lambda values, which: lax.dynamic_slice_in_dim(values, which * width, width, 2)
        send = add_low(cut(keep_b, 1 - mine), cut(got_b, 1 - mine))
        keep_b = add_low(cut(keep_b, mine), cut(got_b, mine))
        got_b = swap(send, seq_axis, bit)
    keep_b, got_b = reduce_rows(keep_b, got_b, rows_axis)
    total_b = add_low(keep_b, got_b)[0]
    for bit in reversed(bits_of(seq_axis)):
        mine = jnp.bitwise_and(me // bit, 1)
        other = swap(total_b, seq_axis, bit)
        total_b = jnp.where(
            mine == 0,
            jnp.concatenate([total_b, other], -1),
            jnp.concatenate([other, total_b], -1),
        )
    return jnp.concatenate([total_a, total_b.astype(jnp.float32)], -1)


def gather_items(values, axis):
    me = lax.axis_index(axis)
    for bit in bits_of(axis):
        other = swap(values, axis, bit)
        mine = jnp.bitwise_and(me // bit, 1)
        values = jnp.where(
            mine == 0, jnp.concatenate([values, other]), jnp.concatenate([other, values])
        )
    return values


LAG = 2
CHUNK = 16
STAGES = 6
MESH = pl.DeviceIdType.MESH


def sum_kernel(units, plan, left_count, right_count, *refs):
    lefts = refs[:left_count]
    rights = refs[left_count : left_count + right_count]
    vector, give_ref = refs[left_count + right_count : left_count + right_count + 2]
    rest = refs[left_count + right_count + 2 :]
    outs, gathered_out, got_ref = rest[: len(plan)], rest[len(plan)], rest[len(plan) + 1]
    rest = rest[len(plan) + 2 :]
    turned, rest = rest[:left_count], rest[left_count:]
    (send0, recv0, keep0, send_y, recv_y, send_x, recv_x) = rest[:7]
    (send_z, recv_z, send_w, recv_w, keep_a, keep_b, last_a, last_b) = rest[7:15]
    (gathered, got_vector, out_sem, in_sem, vec_out, vec_in, give_out, give_in) = rest[15:]
    tick = pl.program_id(0)
    item, seq = lax.axis_index("items"), lax.axis_index("seq")
    bit = lambda value, place: jnp.bitwise_and(value // (1 << place), 1)
    core, y, z0, z1, x = bit(item, 0), bit(item, 1), bit(item, 2), bit(item, 3), seq
    flip = lambda place: item + (1 - 2 * bit(item, place)) * (1 << place)
    partners = {
        "core": (flip(0), seq),
        "y": (flip(1), seq),
        "z0": (flip(2), seq),
        "z1": (flip(3), seq),
        "x": (item, 1 - seq),
    }

    @pl.when(tick == 0)
    def _():
        barrier = pltpu.get_barrier_semaphore()
        for partner in partners.values():
            pl.semaphore_signal(barrier, inc=1, device_id=partner, device_id_type=MESH)
        pl.semaphore_wait(barrier, len(partners))

    def copy(kind, number, unit, source, target, to):
        slot, landing = unit % 2, unit % 4
        return pltpu.make_async_remote_copy(
            src_ref=source.at[slot],
            dst_ref=target.at[landing],
            send_sem=out_sem.at[number, slot],
            recv_sem=in_sem.at[number, landing],
            device_id=partners[to],
            device_id_type=MESH,
        )

    wide = lambda values: values.astype(jnp.float32)
    low = lambda values: values.astype(jnp.bfloat16)

    def choose(values, axis, which):
        first = lax.index_in_dim(values, 0, axis, keepdims=False)
        second = lax.index_in_dim(values, 1, axis, keepdims=False)
        mine = jnp.where(which == 0, first, second)
        other = jnp.where(which == 0, second, first)
        return mine, other

    names = [
        ("d", send0, recv0, "core"),
        ("ay", send_y[0], recv_y[0], "y"),
        ("az", send_z[0], recv_z[0], "z0"),
        ("aw", send_w[0], recv_w[0], "z1"),
        ("ax", send_x[0], recv_x[0], "x"),
        ("bx", send_x[1], recv_x[1], "x"),
        ("by", send_y[1], recv_y[1], "y"),
        ("bz", send_z[1], recv_z[1], "z0"),
        ("bw", send_w[1], recv_w[1], "z1"),
        ("bg", send_x[2], recv_x[2], "x"),
    ]
    table = {name: (i, source, target, to) for i, (name, source, target, to) in enumerate(names)}

    def post(name, unit, values):
        number, source, target, to = table[name]
        source[unit % 2] = low(values)
        copy(name, number, unit, source, target, to).start()

    def take(name, unit):
        number, source, target, to = table[name]
        copy(name, number, unit, source, target, to).wait()
        return wide(target[unit % 4])

    def stage_final(unit, offset):
        other = take("bg", unit)
        mine = last_b[unit % 2]
        top = jnp.where(x == 0, mine, other)
        bottom = jnp.where(x == 0, other, mine)
        block = jnp.concatenate(
            [last_a[unit % 2], jnp.concatenate([top, bottom], 0)], 1
        )
        at = 0
        for (count, _, _), out in zip(plan, outs):

            @pl.when((unit >= at) & (unit < at + count))
            def _(out=out):
                out[...] = block

            at += count

    def stage_five(unit):
        last_a[unit % 2] = keep_a[3][unit % 2] + take("ax", unit)
        total = low(keep_b[3][unit % 2] + take("bw", unit))
        last_b[unit % 2] = wide(total)
        post("bg", unit, total)

    def stage_four(unit):
        total = low(keep_a[2][unit % 2] + take("aw", unit))
        keep_a[3][unit % 2] = wide(total)
        post("ax", unit, total)
        mine, other = choose(keep_b[2][unit % 2] + take("bz", unit), 0, z1)
        keep_b[3][unit % 2] = mine
        post("bw", unit, other)

    def stage_three(unit):
        mine, other = choose(keep_a[1][unit % 2] + take("az", unit), 0, z1)
        keep_a[2][unit % 2] = mine
        post("aw", unit, other)
        total = keep_b[1][unit % 2] + take("by", unit)
        mine, other = choose(total.reshape(2, 2, 32, 128), 1, z0)
        keep_b[2][unit % 2] = mine
        post("bz", unit, other)

    def stage_two(unit):
        total = keep_a[0][unit % 2] + take("ay", unit)
        mine, other = choose(total.reshape(2, 2, 64, 128), 1, z0)
        keep_a[1][unit % 2] = mine
        post("az", unit, other)
        total = keep_b[0][unit % 2] + take("bx", unit)
        mine, other = choose(total.reshape(4, 2, 32, 128), 1, y)
        keep_b[1][unit % 2] = mine
        post("by", unit, other)

    def stage_one(unit):
        total = keep0[unit % 2] + take("d", unit)
        mine, other = choose(total[:, :, :128].reshape(4, 2, 64, 128), 1, y)
        keep_a[0][unit % 2] = mine
        post("ay", unit, other)
        mine, other = choose(total[:, :, 128:].reshape(8, 2, 32, 128), 1, x)
        keep_b[0][unit % 2] = mine
        post("bx", unit, other)

    def stage_zero(unit):
        at = 0
        for count, terms, turns in plan:

            @pl.when((unit >= at) & (unit < at + count))
            def _(at=at, terms=terms, turns=turns):
                for which, start in turns:

                    @pl.when(unit == at + start)
                    def _(which=which):
                        turned[which][...] = lefts[which][...].T

                place = 0
                for segment, pairs in terms:

                    @pl.when((unit >= at + place) & (unit < at + place + segment))
                    def _(pairs=pairs):
                        total = None
                        for which, right in pairs:
                            part = dot(turned[which][...], rights[right][...], 1, 0)
                            total = part if total is None else total + part
                        mine, other = choose(total.reshape(8, 2, 64, 256), 1, core)
                        keep0[unit % 2] = mine
                        post("d", unit, other)

                    place += segment

            at += count

    steps = [stage_zero, stage_one, stage_two, stage_three, stage_four, stage_five, stage_final]
    for number in range(STAGES, -1, -1):
        unit = tick - LAG * number

        @pl.when((unit >= 0) & (unit < units))
        def _(number=number, unit=unit):
            if number == STAGES:
                stage_final(unit, 0)
            else:
                steps[number](unit)

    def give_copy(source, target):
        return pltpu.make_async_remote_copy(
            src_ref=source,
            dst_ref=target,
            send_sem=give_out.at[0],
            recv_sem=give_in.at[0],
            device_id=partners["x"],
            device_id_type=MESH,
        )

    @pl.when(tick < give_ref.shape[0] // CHUNK)
    def _():
        run = pl.ds(pl.multiple_of(tick * CHUNK, CHUNK), CHUNK)
        give_copy(give_ref.at[run], got_ref.at[run]).start()

    @pl.when(tick == pl.num_programs(0) - 1)
    def _():
        give_copy(give_ref, got_ref).wait()

    def vec_copy(number, source, target, to):
        return pltpu.make_async_remote_copy(
            src_ref=source,
            dst_ref=target,
            send_sem=vec_out.at[number],
            recv_sem=vec_in.at[number],
            device_id=partners[to],
            device_id_type=MESH,
        )

    first = vec_copy(0, vector, got_vector, "x")
    hops = []
    for number, to in enumerate(("core", "y", "z0", "z1")):
        count = 1 << number
        run = gathered.at[pl.ds((item // count) * count, count)]
        hops.append(vec_copy(number + 1, run, run, to))

    @pl.when(tick == 0)
    def _():
        first.start()

    @pl.when(tick == LAG)
    def _():
        first.wait()
        heights = lax.broadcasted_iota(jnp.int32, vector.shape, 0)
        gathered[item] = vector[...] + jnp.where(heights < vector.shape[0] - 8, got_vector[...], 0.0)
        hops[0].start()

    for number in range(4):

        @pl.when(tick == LAG * (number + 2))
        def _(number=number):
            hops[number].wait()
            if number < 3:
                hops[number + 1].start()
            else:
                gathered_out[...] = gathered[...]


def sum_weights(weights, lefts, vector, share):
    tile = 256
    rows = lefts[0].shape[1]
    operands, in_specs, plan, out_specs, out_shape = [], [], [], [], []
    for left in lefts:
        in_specs.append(
            pl.BlockSpec(left.shape, lambda i: (0, 0), pipeline_mode=pl.Buffered(1))
        )
    seen = set()
    at = 0
    flops = 0
    for weight in weights:
        terms, turns = [], []
        place = 0
        for segment in weight:
            count = segment[0][1].shape[1] // tile
            pairs = []
            for which, right in segment:
                if which not in seen:
                    seen.add(which)
                    turns.append((which, place))
                pairs.append((which, len(operands)))
                operands.append(right)
                flops += 2 * rows * right.shape[0] * right.shape[1]
                in_specs.append(
                    pl.BlockSpec(
                        (right.shape[0], tile),
                        lambda i, start=at + place, count=count: (
                            0,
                            jnp.clip(i - start, 0, count - 1),
                        ),
                    )
                )
            terms.append((count, tuple(pairs)))
            place += count
        plan.append((place, tuple(terms), tuple(turns)))
        out_specs.append(
            pl.BlockSpec(
                (64, tile),
                lambda i, start=at, count=place: (
                    0,
                    jnp.clip(i - LAG * STAGES - start, 0, count - 1),
                ),
            )
        )
        out_shape.append(jax.ShapeDtypeStruct((64, place * tile), jnp.float32))
        at += place
    units = at
    in_specs.append(pl.BlockSpec(vector.shape, lambda i: (0, 0)))
    out_specs.append(pl.BlockSpec((16,) + vector.shape, lambda i: (0, 0, 0)))
    out_shape.append(jax.ShapeDtypeStruct((16,) + vector.shape, jnp.float32))
    in_specs.append(pl.BlockSpec(memory_space=pl.ANY))
    out_specs.append(pl.BlockSpec(memory_space=pl.ANY))
    out_shape.append(jax.ShapeDtypeStruct(share.shape, share.dtype))
    low = lambda *shape: pltpu.VMEM(shape, jnp.bfloat16)
    full = lambda *shape: pltpu.VMEM(shape, jnp.float32)
    scratch = [low(*left.shape[::-1]) for left in lefts]
    scratch += [low(2, 8, 64, 256), low(4, 8, 64, 256), full(2, 8, 64, 256)]
    scratch += [
        (low(2, 4, 64, 128), low(2, 4, 32, 128)),
        (low(4, 4, 64, 128), low(4, 4, 32, 128)),
        (low(2, 64, 128), low(2, 8, 32, 128), low(2, 32, 128)),
        (low(4, 64, 128), low(4, 8, 32, 128), low(4, 32, 128)),
        (low(2, 2, 64, 128), low(2, 2, 32, 128)),
        (low(4, 2, 64, 128), low(4, 2, 32, 128)),
        (low(2, 64, 128), low(2, 32, 128)),
        (low(4, 64, 128), low(4, 32, 128)),
        (full(2, 4, 64, 128), full(2, 2, 64, 128), full(2, 64, 128), full(2, 64, 128)),
        (full(2, 8, 32, 128), full(2, 4, 32, 128), full(2, 2, 32, 128), full(2, 32, 128)),
        full(2, 64, 128),
        full(2, 32, 128),
        full(16, *vector.shape),
        full(*vector.shape),
        pltpu.SemaphoreType.DMA((10, 2)),
        pltpu.SemaphoreType.DMA((10, 4)),
        pltpu.SemaphoreType.DMA((5,)),
        pltpu.SemaphoreType.DMA((5,)),
        pltpu.SemaphoreType.DMA((1,)),
        pltpu.SemaphoreType.DMA((1,)),
    ]
    moved = sum(2 * a.size for a in operands) + sum(2 * a.size for a in lefts)
    return pl.pallas_call(
        functools.partial(sum_kernel, units, tuple(plan), len(lefts), len(operands)),
        grid=(units + LAG * STAGES,),
        in_specs=in_specs,
        out_specs=out_specs,
        out_shape=out_shape,
        scratch_shapes=scratch,
        compiler_params=pltpu.CompilerParams(
            vmem_limit_bytes=58 << 20, collective_id=0, has_side_effects=True
        ),
        cost_estimate=pl.CostEstimate(flops=flops, transcendentals=0, bytes_accessed=moved),
    )(*lefts, *operands, vector, share)


def per_device(
    frames,
    cotangent,
    section,
    prompt_len,
    section_embed,
    ada_proj,
    ada_bias,
    w_qkv,
    w_out,
    w_up,
    w_down,
):
    _, row_count, width = frames.shape
    frames, cotangent = frames[0], cotangent[0]
    seq_size = lax.axis_size("seq")
    item_size = lax.axis_size("items")
    seq_me, item_me = lax.axis_index("seq"), lax.axis_index("items")
    side = jnp.bitwise_and(item_me, 1).astype(jnp.int32).reshape(1)
    turns = list(range(1, seq_size))
    fetch = lambda values, turn: lax.ppermute(
        values, "seq", [((i + turn) % seq_size, i) for i in range(seq_size)]
    )
    give = lambda values, turn: lax.ppermute(
        values, "seq", [(i, (i + turn) % seq_size) for i in range(seq_size)]
    )
    others = [fetch(frames, turn) for turn in turns]
    sources = jnp.stack([(seq_me + turn) % seq_size for turn in [0] + turns])
    limits = jnp.where(sources == 0, prompt_len[0], row_count).astype(jnp.int32)

    section_count = section_embed.shape[0]
    onehot = (section[:, None] == jnp.arange(section_count, dtype=jnp.int32)[None, :]).astype(
        jnp.float32
    )
    cond = jnp.dot(onehot, section_embed, precision=HIGHEST)
    modul = jnp.dot(cond, ada_proj.astype(jnp.float32), precision=HIGHEST) + ada_bias[None, :]
    scale_one, shift_one, scale_two, shift_two = jnp.split(modul, 4, axis=-1)
    inputs = frames.astype(jnp.float32)
    normed_one, inv_one = normalize(inputs)
    modulate = lambda normed: (normed * (1.0 + scale_one) + shift_one).astype(jnp.bfloat16)
    attn_in = modulate(normed_one)
    qkv = project(attn_in, w_qkv).astype(jnp.bfloat16)
    grad_act = back_project(cotangent, w_down).astype(jnp.bfloat16)
    others, qkv, grad_act = lax.optimization_barrier((others, qkv, grad_act))
    rest = jnp.concatenate(others) if len(others) > 1 else others[0]
    normed_rest, _ = normalize(rest.astype(jnp.float32))
    attn_rest = modulate(normed_rest)
    kv_rest = project(attn_rest, w_qkv[:, width:]).astype(jnp.bfloat16)
    att, lse = attend(limits, qkv, kv_rest, width)
    mid = inputs + project(att, w_out)
    normed_two, inv_two = normalize(mid)
    ffn_in = (normed_two * (1.0 + scale_two) + shift_two).astype(jnp.bfloat16)
    upper = project(ffn_in, w_up)
    act = gelu_exact(upper).astype(jnp.bfloat16)
    grad_upper = (grad_act.astype(jnp.float32) * gelu_slope(upper)).astype(jnp.bfloat16)
    out_frames = (mid + project(act, w_down)).astype(jnp.bfloat16)

    grad_out = cotangent.astype(jnp.float32)
    fused = seq_size == 2 and item_size == 16 and width == 1024
    if fused:
        sum_down = lax.psum_scatter(
            outer_sum(act, cotangent).astype(jnp.bfloat16),
            "items",
            scatter_dimension=0,
            tiled=True,
        )
    else:
        down_pieces = outer(side, [act], [[(0, cotangent)]], item_size, 256)
    grad_ffn_in = back_project(grad_upper, w_up)
    grad_scale_two = jnp.sum(grad_ffn_in * normed_two, 0)
    grad_shift_two = jnp.sum(grad_ffn_in, 0)
    grad_mid = grad_out + norm_back(grad_ffn_in * (1.0 + scale_two), normed_two, inv_two)
    grad_mid_low = grad_mid.astype(jnp.bfloat16)
    grad_att = back_project(grad_mid_low, w_out).astype(jnp.bfloat16)
    grad_query, grad_key, grad_value, key_rest, value_rest = attend_back(
        limits, qkv, kv_rest, grad_att, att, lse
    )
    up_terms = [[(0, grad_upper)]]
    out_terms = [[(1, grad_mid_low)]]
    qkv_terms = [
        [(2, grad_query)],
        [(2, grad_key), (3, key_rest)],
        [(2, grad_value), (3, value_rest)],
    ]
    w_key, w_value = w_qkv[:, width : 2 * width], w_qkv[:, 2 * width :]
    share = back_project(key_rest, w_key) + back_project(value_rest, w_value)
    share_low = share.astype(jnp.bfloat16)
    partial = (
        back_project(grad_query, w_qkv[:, :width])
        + back_project(grad_key, w_key)
        + back_project(grad_value, w_value)
    )
    grad_scale_one = jnp.sum(partial * normed_one, 0) + jnp.sum(share * normed_rest, 0)
    grad_shift_one = jnp.sum(partial, 0) + jnp.sum(share, 0)
    grad_modul = jnp.concatenate(
        [grad_scale_one, grad_shift_one, grad_scale_two, grad_shift_two]
    )[None, :]
    if fused:
        vector = jnp.concatenate(
            [
                grad_modul.reshape(4 * width // 128, 128),
                jnp.pad(onehot, ((0, 7), (0, 128 - section_count))),
            ]
        )
        sum_up, sum_out, sum_qkv, tagged, got_share = sum_weights(
            [up_terms, out_terms, qkv_terms],
            [ffn_in, att, attn_in, attn_rest],
            vector,
            share_low,
        )
        grad_rest = [got_share]
        tagged = tagged[:, : 4 * width // 128 + 1].reshape(item_size, 4 * width + 128)
        sum_down = sum_down.astype(jnp.float32) + swap(sum_down, "seq", 1).astype(jnp.float32)
    else:
        grad_rest = [
            give(share_low[i * row_count : (i + 1) * row_count], turn)
            for i, turn in enumerate(turns)
        ]
        shift = lambda terms, by: [[(i - by, right) for i, right in run] for run in terms]
        sum_down = finish(down_pieces, "items", "seq")
        sum_up = finish(outer(side, [ffn_in], up_terms, item_size, 512), "items", "seq")
        sum_out = finish(
            outer(side, [att], shift(out_terms, 1), item_size, 512), "items", "seq"
        )
        sum_qkv = finish(
            outer(side, [attn_in, attn_rest], shift(qkv_terms, 2), item_size, 512),
            "items",
            "seq",
        )
        for bit in bits_of("seq"):
            grad_modul = grad_modul + swap(grad_modul, "seq", bit)
        tagged = jnp.concatenate(
            [grad_modul, jnp.pad(onehot, ((0, 0), (0, 128 - section_count)))], -1
        )
        tagged = gather_items(tagged, "items")
    grad_attn_in = partial
    for got in grad_rest:
        grad_attn_in = grad_attn_in + got.astype(jnp.float32)
    frames_grad = (
        grad_mid + norm_back(grad_attn_in * (1.0 + scale_one), normed_one, inv_one)
    ).astype(jnp.bfloat16)

    modul_all, onehot_all = tagged[:, : 4 * width], tagged[:, 4 * width :][:, :section_count]
    block = width // item_size
    own_embed = lax.dynamic_slice_in_dim(section_embed, item_me * block, block, 1)
    own_cond = jnp.dot(onehot_all, own_embed, precision=HIGHEST)
    sum_ada = lax.dot_general(own_cond, modul_all, (((0,), (0,)), ((), ())), precision=HIGHEST)
    sum_bias = jnp.sum(
        lax.dynamic_slice_in_dim(modul_all, item_me * 4 * block, 4 * block, 1), 0
    )
    own_ada = lax.dynamic_slice_in_dim(ada_proj, item_me * block, block, 0).astype(jnp.float32)
    grad_cond = lax.dot_general(modul_all, own_ada, (((1,), (1,)), ((), ())), precision=HIGHEST)
    sum_embed = lax.dot_general(
        onehot_all, grad_cond, (((0,), (0,)), ((), ())), precision=HIGHEST
    )
    return (
        out_frames[None],
        frames_grad[None],
        sum_embed,
        sum_ada,
        sum_bias,
        sum_qkv,
        sum_out,
        sum_up,
        sum_down,
    )


def solution(mesh):
    in_specs = (
        P("items", "seq", None),
        P("items", "seq", None),
        P("items"),
        P("items"),
        P(),
        P(),
        P(),
        P(),
        P(),
        P(),
        P(),
    )
    out_specs = (
        P("items", "seq", None),
        P("items", "seq", None),
        P(None, "items"),
        P("items", None),
        P("items"),
        P("items", None),
        P("items", None),
        P("items", None),
        P("items", None),
    )
    return jax.shard_map(
        per_device, mesh=mesh, in_specs=in_specs, out_specs=out_specs, check_vma=False
    )
```

```python
import functools

import jax
import jax.numpy as jnp
from jax import lax
from jax.experimental import pallas as pl
from jax.experimental.pallas import tpu as pltpu
from jax.sharding import PartitionSpec as P

HEADS = 16


EPS = 1e-05
NEGATIVE = -1e30
SQRT_HALF = 0.7071067811865476
INV_SQRT_TAU = 0.3989422804014327
HIGHEST = lax.Precision.HIGHEST


def normalize(values):
    mean = jnp.mean(values, -1, keepdims=True)
    centered = values - mean
    inverse = lax.rsqrt(jnp.mean(centered * centered, -1, keepdims=True) + EPS)
    return (centered * inverse, inverse)


def norm_back(grad, normed, inverse):
    first = jnp.mean(grad, -1, keepdims=True)
    second = jnp.mean(grad * normed, -1, keepdims=True)
    return (grad - first - normed * second) * inverse


def gelu_exact(values):
    return 0.5 * values * (1.0 + lax.erf(values * SQRT_HALF))


def gelu_slope(values):
    return (
        0.5 * (1.0 + lax.erf(values * SQRT_HALF))
        + values * jnp.exp(-0.5 * values * values) * INV_SQRT_TAU
    )


def project(left, weight):
    flat = left.reshape(-1, left.shape[-1])
    result = jnp.dot(flat, weight, preferred_element_type=jnp.float32)
    return result.reshape(left.shape[:-1] + (weight.shape[1],))


def back_project(grad, weight):
    flat = grad.reshape(-1, grad.shape[-1])
    result = lax.dot_general(
        flat, weight, (((1,), (1,)), ((), ())), preferred_element_type=jnp.float32
    )
    return result.reshape(grad.shape[:-1] + (weight.shape[0],))


BIG = 1e30

def split3(x):
    hi = x.astype(jnp.bfloat16).astype(jnp.float32)
    rest = x - hi
    mid = rest.astype(jnp.bfloat16).astype(jnp.float32)
    return hi, mid, rest - mid

def dot(a, b, ca, cb):
    return lax.dot_general(a, b, (((ca,), (cb,)), ((), ())), preferred_element_type=jnp.float32)


def fwd_kernel(rows, blocks, lim_ref, q_ref, ko_ref, vo_ref, kt_ref, vt_ref, o_ref, lse_ref):
    lane = lax.broadcasted_iota(jnp.int32, (1, 128), 1)
    low = lane < 64
    row = lax.broadcasted_iota(jnp.int32, (rows, 1), 0)
    q = q_ref[...].astype(jnp.float32) * 0.125
    outs, lses = [], []
    for h in range(2):
        own = low if h == 0 else jnp.logical_not(low)
        first = 64 * (1 - h)
        qa = jnp.where(own, q, jnp.where(lane == first, 1.0, 0.0)).astype(jnp.bfloat16)
        scores, values = [], []
        for j in range(blocks):
            k = ko_ref[...] if j == 0 else kt_ref[pl.ds((j - 1) * rows, rows), :]
            v = vo_ref[...] if j == 0 else vt_ref[pl.ds((j - 1) * rows, rows), :]
            bias = jnp.where(row < lim_ref[j], 0.0, -BIG)
            ka = jnp.where(own, k.astype(jnp.float32), jnp.where(lane == first, bias, 0.0)).astype(jnp.bfloat16)
            va = jnp.where(own, v.astype(jnp.float32), 1.0).astype(jnp.bfloat16)
            scores.append(dot(qa, ka, 1, 1))
            values.append(va)
        top = functools.reduce(jnp.maximum, [jnp.max(s, -1, keepdims=True) for s in scores])
        total = None
        for s, va in zip(scores, values):
            p = jnp.exp(s - top).astype(jnp.bfloat16)
            part = dot(p, va, 1, 0)
            total = part if total is None else total + part
        outs.append(total / pltpu.roll(total, 64, 1))
        lses.append(top + jnp.log(total))
    o_ref[...] = jnp.where(low, outs[0], outs[1]).astype(o_ref.dtype)
    lse_ref[...] = jnp.where(low, lses[1], lses[0])


def bwd_kernel(rows, blocks, lim_ref, q_ref, ko_ref, vo_ref, kt_ref, vt_ref, do_ref, o_ref, lse_ref,
               dq_ref, dko_ref, dvo_ref, dkt_ref, dvt_ref):
    lane = lax.broadcasted_iota(jnp.int32, (1, 128), 1)
    low = lane < 64
    row = lax.broadcasted_iota(jnp.int32, (rows, 1), 0)
    q = q_ref[...].astype(jnp.float32) * 0.125
    qs = q.astype(jnp.bfloat16)
    do_low = do_ref[...]
    do = do_low.astype(jnp.float32)
    prod = do * o_ref[...].astype(jnp.float32)
    lh, lm, ll = split3(lse_ref[...])
    heads = []
    for h in range(2):
        own = low if h == 0 else jnp.logical_not(low)
        f = 64 * (1 - h)
        delta = jnp.sum(jnp.where(own, prod, 0.0), -1, keepdims=True)
        dh, dm, dl = split3(delta)
        qa = jnp.where(own, q, jnp.where(lane == f, 1.0, jnp.where(lane == f + 1, -lh, jnp.where(lane == f + 2, -lm, jnp.where(lane == f + 3, -ll, 0.0))))).astype(jnp.bfloat16)
        doa = jnp.where(own, do, jnp.where(lane == f, -dh, jnp.where(lane == f + 1, -dm, jnp.where(lane == f + 2, -dl, 0.0)))).astype(jnp.bfloat16)
        kone = jnp.where((lane > f) & (lane <= f + 3), 1.0, 0.0)
        vone = jnp.where((lane >= f) & (lane < f + 3), 1.0, 0.0)
        dq = None
        res = []
        for j in range(blocks):
            k = ko_ref[...] if j == 0 else kt_ref[pl.ds((j - 1) * rows, rows), :]
            v = vo_ref[...] if j == 0 else vt_ref[pl.ds((j - 1) * rows, rows), :]
            bias = jnp.where(row < lim_ref[j], 0.0, -BIG)
            ka = jnp.where(own, k.astype(jnp.float32), jnp.where(lane == f, bias, kone)).astype(jnp.bfloat16)
            va = jnp.where(own, v.astype(jnp.float32), vone).astype(jnp.bfloat16)
            pt = jnp.exp(dot(ka, qa, 1, 1))
            dpt = dot(va, doa, 1, 1)
            dst = (pt * dpt).astype(jnp.bfloat16)
            dv = dot(pt.astype(jnp.bfloat16), do_low, 1, 0)
            dk = dot(dst, qs, 1, 0)
            part = dot(dst, k, 0, 0)
            dq = part if dq is None else dq + part
            res.append((dk, dv))
        heads.append((dq, res))
    dq_ref[...] = (jnp.where(low, heads[0][0], heads[1][0]) * 0.125).astype(dq_ref.dtype)
    for j in range(blocks):
        dk = jnp.where(low, heads[0][1][j][0], heads[1][1][j][0]).astype(dko_ref.dtype)
        dv = jnp.where(low, heads[0][1][j][1], heads[1][1][j][1]).astype(dko_ref.dtype)
        if j == 0:
            dko_ref[...] = dk
            dvo_ref[...] = dv
        else:
            dkt_ref[pl.ds((j - 1) * rows, rows), :] = dk
            dvt_ref[pl.ds((j - 1) * rows, rows), :] = dv


def specs_of(rows, others, width):
    pairs = width // 128
    place = lambda count, skip: pl.BlockSpec((count, 128), lambda i, lim: (0, i + skip))
    inputs = [place(rows, 0), place(rows, pairs), place(rows, 2 * pairs), place(others, 0), place(others, pairs)]
    return inputs, place(rows, 0), place(others, 0)


def attend(lim, qkv, kv_rest, width):
    rows, others = qkv.shape[0], kv_rest.shape[0]
    blocks = 1 + others // rows
    inputs, own, oth = specs_of(rows, others, width)
    keys = rows + others
    return pl.pallas_call(
        functools.partial(fwd_kernel, rows, blocks),
        grid_spec=pltpu.PrefetchScalarGridSpec(num_scalar_prefetch=1, grid=(width // 128,),
            in_specs=inputs, out_specs=[own, own]),
        out_shape=[jax.ShapeDtypeStruct((rows, width), jnp.bfloat16), jax.ShapeDtypeStruct((rows, width), jnp.float32)],
        compiler_params=pltpu.CompilerParams(vmem_limit_bytes=56 << 20),
        cost_estimate=pl.CostEstimate(flops=16 * rows * keys * width, transcendentals=rows * keys * width // 64,
            bytes_accessed=2 * width * (2 * rows + 2 * keys) + 4 * rows * width),
    )(lim, qkv, qkv, qkv, kv_rest, kv_rest)


def attend_back(lim, qkv, kv_rest, do, o, lse):
    (rows, width), others = do.shape, kv_rest.shape[0]
    blocks = 1 + others // rows
    inputs, own, oth = specs_of(rows, others, width)
    keys = rows + others
    s = lambda n: jax.ShapeDtypeStruct((n, width), jnp.bfloat16)
    return pl.pallas_call(
        functools.partial(bwd_kernel, rows, blocks),
        grid_spec=pltpu.PrefetchScalarGridSpec(num_scalar_prefetch=1, grid=(width // 128,),
            in_specs=inputs + [own, own, own], out_specs=[own, own, own, oth, oth]),
        out_shape=[s(rows), s(rows), s(rows), s(others), s(others)],
        compiler_params=pltpu.CompilerParams(vmem_limit_bytes=56 << 20),
        cost_estimate=pl.CostEstimate(flops=40 * rows * keys * width, transcendentals=rows * keys * width // 64,
            bytes_accessed=2 * width * (4 * rows + 4 * keys) + 4 * rows * width),
    )(lim, qkv, qkv, qkv, kv_rest, kv_rest, do, o, lse)


def outer_sum(left, right):
    return lax.dot_general(
        left, right, (((0,), (0,)), ((), ())), preferred_element_type=jnp.float32
    )


def outer_kernel(plan, halves, first_tiles, side_ref, *refs):
    lefts, plan_rights, outs, turned = refs[: plan[0]], refs[plan[0] : plan[1]], refs[plan[1] : plan[1] + 4], refs[plan[1] + 4 :]
    step = pl.program_id(0)

    @pl.when(step == 0)
    def _():
        for left, flip in zip(lefts, turned):
            flip[...] = left[...].T

    at = 0
    place = 0
    for tiles, terms in plan[2]:
        rights = plan_rights[place : place + len(terms)]
        place += len(terms)

        @pl.when((step >= at) & (step < at + tiles))
        def _(rights=rights, terms=terms):
            total = None
            for which, right in zip(terms, rights):
                part = dot(turned[which][...], right[...], 1, 0)
                total = part if total is None else total + part
            rows, columns = total.shape
            split = total.astype(jnp.bfloat16).reshape(halves, 2, rows // (2 * halves), columns)
            even = side_ref[0] == 0
            keep = jnp.where(even, split[:, 0], split[:, 1])
            send = jnp.where(even, split[:, 1], split[:, 0])

            @pl.when(step < first_tiles)
            def _():
                outs[0][...] = send
                outs[1][...] = keep

            @pl.when(step >= first_tiles)
            def _():
                outs[2][...] = send
                outs[3][...] = keep

        at += tiles


def outer(side, lefts, segments, parts, tile):
    rows = lefts[0].shape[1]
    halves = parts // 2
    block = rows // parts
    width = sum(segment[0][1].shape[1] for segment in segments)
    steps = width // tile
    first_tiles = steps // 2
    in_specs = [pl.BlockSpec(left.shape, lambda i, s: (0, 0)) for left in lefts]
    operands = list(lefts)
    plan = []
    at = 0
    flops = 0
    for segment in segments:
        tiles = segment[0][1].shape[1] // tile
        for which, right in segment:
            in_specs.append(
                pl.BlockSpec(
                    (right.shape[0], tile),
                    lambda i, s, at=at, tiles=tiles: (0, jnp.clip(i - at, 0, tiles - 1)),
                )
            )
            operands.append(right)
            flops += 2 * rows * right.shape[0] * right.shape[1]
        plan.append((tiles, tuple(which for which, _ in segment)))
        at += tiles
    first = pl.BlockSpec((halves, block, tile), lambda i, s: (0, 0, jnp.minimum(i, first_tiles - 1)))
    second = pl.BlockSpec((halves, block, tile), lambda i, s: (0, 0, jnp.maximum(i - first_tiles, 0)))
    shape = lambda count: jax.ShapeDtypeStruct((halves, block, count * tile), jnp.bfloat16)
    moved = sum(2 * operand.size for operand in operands) + 2 * rows * width
    return pl.pallas_call(
        functools.partial(
            outer_kernel, (len(lefts), len(operands), tuple(plan)), halves, first_tiles
        ),
        grid_spec=pltpu.PrefetchScalarGridSpec(
            num_scalar_prefetch=1,
            grid=(steps,),
            in_specs=in_specs,
            out_specs=[first, first, second, second],
            scratch_shapes=[pltpu.VMEM(left.shape[::-1], jnp.bfloat16) for left in lefts],
        ),
        out_shape=[shape(first_tiles)] * 2 + [shape(steps - first_tiles)] * 2,
        compiler_params=pltpu.CompilerParams(vmem_limit_bytes=58 << 20),
        cost_estimate=pl.CostEstimate(flops=flops, transcendentals=0, bytes_accessed=moved),
    )(side, *operands)


def swap(values, axis, bit):
    size = lax.axis_size(axis)
    return lax.ppermute(values, axis, [(i, i ^ bit) for i in range(size)])


def bits_of(axis):
    size = lax.axis_size(axis)
    return [1 << place for place in range(size.bit_length() - 1)]


def add_low(left, right):
    return (left.astype(jnp.float32) + right.astype(jnp.float32)).astype(jnp.bfloat16)


def half_of(values, dim, which):
    return lax.dynamic_index_in_dim(values, which, dim, keepdims=False)


def reduce_rows(keep, got, axis):
    me = lax.axis_index(axis)
    for bit in bits_of(axis)[1:]:
        mine = jnp.bitwise_and(me // bit, 1)
        shape = keep.shape
        view = (shape[0] // 2, 2) + shape[1:]
        keep, got = keep.reshape(view), got.reshape(view)
        send = add_low(half_of(keep, 1, 1 - mine), half_of(got, 1, 1 - mine))
        keep = add_low(half_of(keep, 1, mine), half_of(got, 1, mine))
        got = swap(send, axis, bit)
    return keep, got


def finish(pieces, rows_axis, seq_axis):
    send_a, keep_a, send_b, keep_b = pieces
    got_a = swap(send_a, rows_axis, 1)
    got_b = swap(send_b, rows_axis, 1)
    keep_a, got_a = reduce_rows(keep_a, got_a, rows_axis)
    total_a = (keep_a.astype(jnp.float32) + got_a.astype(jnp.float32))[0]
    for bit in bits_of(seq_axis):
        low = total_a.astype(jnp.bfloat16)
        total_a = low.astype(jnp.float32) + swap(low, seq_axis, bit).astype(jnp.float32)
    me = lax.axis_index(seq_axis)
    for bit in bits_of(seq_axis):
        mine = jnp.bitwise_and(me // bit, 1)
        width = keep_b.shape[-1] // 2
        cut = lambda values, which: lax.dynamic_slice_in_dim(values, which * width, width, 2)
        send = add_low(cut(keep_b, 1 - mine), cut(got_b, 1 - mine))
        keep_b = add_low(cut(keep_b, mine), cut(got_b, mine))
        got_b = swap(send, seq_axis, bit)
    keep_b, got_b = reduce_rows(keep_b, got_b, rows_axis)
    total_b = add_low(keep_b, got_b)[0]
    for bit in reversed(bits_of(seq_axis)):
        mine = jnp.bitwise_and(me // bit, 1)
        other = swap(total_b, seq_axis, bit)
        total_b = jnp.where(
            mine == 0,
            jnp.concatenate([total_b, other], -1),
            jnp.concatenate([other, total_b], -1),
        )
    return jnp.concatenate([total_a, total_b.astype(jnp.float32)], -1)


def gather_items(values, axis):
    me = lax.axis_index(axis)
    for bit in bits_of(axis):
        other = swap(values, axis, bit)
        mine = jnp.bitwise_and(me // bit, 1)
        values = jnp.where(
            mine == 0, jnp.concatenate([values, other]), jnp.concatenate([other, values])
        )
    return values


LAG = 2
MESH = pl.DeviceIdType.MESH


def attention_step(step, lim_ref, q_ref, ko_ref, vo_ref, kt_ref, vt_ref, do_ref, o_ref, lse_ref,
                   dq_ref, dko_ref, dvo_ref, dkt_ref, dvt_ref, qa_ref, doa_ref, dq_sum):
    rows = q_ref.shape[0]
    head, j = (step // 2) % 2, step % 2
    lane = lax.broadcasted_iota(jnp.int32, (1, 128), 1)
    own = (lane // 64) == head
    f = 64 * (1 - head)

    @pl.when(j == 0)
    def _():
        q = q_ref[...].astype(jnp.float32) * 0.125
        do = do_ref[...].astype(jnp.float32)
        prod = do * o_ref[...].astype(jnp.float32)
        lh, lm, ll = split3(lse_ref[...])
        delta = jnp.sum(jnp.where(own, prod, 0.0), -1, keepdims=True)
        dh, dm, dl = split3(delta)
        qa_ref[...] = jnp.where(own, q, jnp.where(lane == f, 1.0, jnp.where(lane == f + 1, -lh, jnp.where(lane == f + 2, -lm, jnp.where(lane == f + 3, -ll, 0.0))))).astype(jnp.bfloat16)
        doa_ref[...] = jnp.where(own, do, jnp.where(lane == f, -dh, jnp.where(lane == f + 1, -dm, jnp.where(lane == f + 2, -dl, 0.0)))).astype(jnp.bfloat16)

    row = lax.broadcasted_iota(jnp.int32, (rows, 1), 0)
    wide = lambda ref: ref[...].astype(jnp.float32)
    k = jnp.where(j == 0, wide(ko_ref), wide(kt_ref))
    v = jnp.where(j == 0, wide(vo_ref), wide(vt_ref))
    kone = jnp.where((lane > f) & (lane <= f + 3), 1.0, 0.0)
    vone = jnp.where((lane >= f) & (lane < f + 3), 1.0, 0.0)
    bias = jnp.where(row < lim_ref[j], 0.0, -BIG)
    ka = jnp.where(own, k, jnp.where(lane == f, bias, kone)).astype(jnp.bfloat16)
    va = jnp.where(own, v, vone).astype(jnp.bfloat16)
    qa, doa = qa_ref[...], doa_ref[...]
    pt = jnp.exp(dot(ka, qa, 1, 1))
    dpt = dot(va, doa, 1, 1)
    dst = (pt * dpt).astype(jnp.bfloat16)
    dv = dot(pt.astype(jnp.bfloat16), doa, 1, 0)
    dk = dot(dst, qa, 1, 0)
    part = dot(dst, ka, 0, 0)

    def put(ref, values):
        @pl.when(head == 0)
        def _():
            ref[...] = values.astype(ref.dtype)

        @pl.when(head == 1)
        def _():
            ref[...] = jnp.where(lane < 64, wide(ref), values).astype(ref.dtype)

    @pl.when(j == 0)
    def _():
        dq_sum[...] = part
        put(dko_ref, dk)
        put(dvo_ref, dv)

    @pl.when(j == 1)
    def _():
        put(dq_ref, (dq_sum[...] + part) * 0.125)
        put(dkt_ref, dk)
        put(dvt_ref, dv)


def sum_kernel(units, plan, layout, sides, *refs):
    at = 0
    parts = {}
    for name, count in layout:
        parts[name] = refs[at : at + count]
        at += count
    lefts, rights, outs, turned = (parts[name] for name in ("lefts", "rights", "outs", "turned"))
    send, recv, keep = parts["send"], parts["recv"], parts["keep"]
    out_sem, in_sem = parts["sems"]
    stages = 4 + sides
    cut = 256 // sides
    tick = pl.program_id(0)
    item, seq = lax.axis_index("items"), lax.axis_index("seq")
    bit = lambda value, place: jnp.bitwise_and(value // (1 << place), 1)
    core, y, z0, z1, x = bit(item, 0), bit(item, 1), bit(item, 2), bit(item, 3), seq
    flip = lambda place: item + (1 - 2 * bit(item, place)) * (1 << place)
    partners = {
        "core": (flip(0), seq),
        "y": (flip(1), seq),
        "z0": (flip(2), seq),
        "z1": (flip(3), seq),
        "x": (item, 1 - seq),
    }

    @pl.when(tick == 0)
    def _():
        barrier = pltpu.get_barrier_semaphore()
        for partner in partners.values():
            pl.semaphore_signal(barrier, inc=1, device_id=partner, device_id_type=MESH)
        pl.semaphore_wait(barrier, len(partners))

    wide = lambda values: values.astype(jnp.float32)
    low = lambda values: values.astype(jnp.bfloat16)

    def choose(values, axis, which):
        first = lax.index_in_dim(values, 0, axis, keepdims=False)
        second = lax.index_in_dim(values, 1, axis, keepdims=False)
        mine = jnp.where(which == 0, first, second)
        other = jnp.where(which == 0, second, first)
        return mine, other

    table = {name: (i, to) for i, (name, to, _) in enumerate(HOPS[sides])}

    def copy(name, unit):
        number, to = table[name]
        slot, landing = unit % 2, unit % 4
        return pltpu.make_async_remote_copy(
            src_ref=send[number].at[slot],
            dst_ref=recv[number].at[landing],
            send_sem=out_sem.at[number, slot],
            recv_sem=in_sem.at[number, landing],
            device_id=partners[to],
            device_id_type=MESH,
        )

    def post(name, unit, mine, other):
        number, _ = table[name]
        keep[number][unit % 2] = mine
        send[number][unit % 2] = low(other)
        copy(name, unit).start()

    def take(name, unit):
        number, _ = table[name]
        copy(name, unit).wait()
        return keep[number][unit % 2] + wide(recv[number][unit % 4])

    def stage_zero(unit):
        at = 0
        for count, terms, turns in plan:

            @pl.when((unit >= at) & (unit < at + count))
            def _(at=at, terms=terms, turns=turns):
                for which, start in turns:

                    @pl.when(unit == at + start)
                    def _(which=which):
                        turned[which][...] = lefts[which][...].T

                place = 0
                for segment, pairs in terms:

                    @pl.when((unit >= at + place) & (unit < at + place + segment))
                    def _(pairs=pairs):
                        total = None
                        for which, right in pairs:
                            part = dot(turned[which][...], rights[right][...], 1, 0)
                            total = part if total is None else total + part
                        post("d", unit, *choose(total.reshape(8, 2, 64, 256), 1, core))

                    place += segment

            at += count

    def stage_one(unit):
        total = take("d", unit)
        post("ay", unit, *choose(total[:, :, :cut].reshape(4, 2, 64, cut), 1, y))
        if sides == 2:
            post("bx", unit, *choose(total[:, :, cut:].reshape(8, 2, 32, cut), 1, x))

    def stage_two(unit):
        post("az", unit, *choose(take("ay", unit).reshape(2, 2, 64, cut), 1, z0))
        if sides == 2:
            post("by", unit, *choose(take("bx", unit).reshape(4, 2, 32, cut), 1, y))

    def stage_three(unit):
        post("aw", unit, *choose(take("az", unit), 0, z1))
        if sides == 2:
            post("bz", unit, *choose(take("by", unit).reshape(2, 2, 32, cut), 1, z0))

    def stage_four(unit):
        total = low(take("aw", unit))
        post("ax", unit, wide(total), total)
        if sides == 2:
            post("bw", unit, *choose(take("bz", unit), 0, z1))

    def stage_five(unit):
        parts["last"][0][unit % 2] = take("ax", unit)
        total = low(take("bw", unit))
        post("bg", unit, wide(total), total)

    def stage_final(unit):
        if sides == 1:
            block = take("ax", unit)
        else:
            number, _ = table["bg"]
            copy("bg", unit).wait()
            other = wide(recv[number][unit % 4])
            mine = keep[number][unit % 2]
            top = jnp.where(x == 0, mine, other)
            bottom = jnp.where(x == 0, other, mine)
            block = jnp.concatenate(
                [parts["last"][0][unit % 2], jnp.concatenate([top, bottom], 0)], 1
            )
        at = 0
        for (count, _, _), out in zip(plan, outs):

            @pl.when((unit >= at) & (unit < at + count))
            def _(out=out):
                out[...] = block

            at += count

    steps = [stage_zero, stage_one, stage_two, stage_three, stage_four, stage_five][:stages]
    steps.append(stage_final)
    for number in range(stages, -1, -1):
        unit = tick - LAG * number

        @pl.when((unit >= 0) & (unit < units))
        def _(number=number, unit=unit):
            steps[number](unit)

    if parts["attention"]:

        @pl.when(tick < ATTENTION_STEPS)
        def _():
            attention_step(tick, *parts["attention"], *parts["grads"], *parts["held"])

    if parts["vector"]:
        vector, gathered_out = parts["vector"][0], parts["gathered"][0]
        gathered, got_vector, vec_out, vec_in = parts["gather"]
        give_ref, got_ref = parts["give"][0], parts["got"][0]
        give_out, give_in = parts["give_sems"]
        ticks = pl.num_programs(0)
        chunk = give_ref.shape[0] // GIVES

        def other_copy(source, target, out, into, to):
            return pltpu.make_async_remote_copy(
                src_ref=source,
                dst_ref=target,
                send_sem=out,
                recv_sem=into,
                device_id=partners[to],
                device_id_type=MESH,
            )

        give_copy = lambda source, target: other_copy(
            source, target, give_out.at[0], give_in.at[0], "x"
        )

        @pl.when(tick < GIVES)
        def _():
            run = pl.ds(pl.multiple_of(tick * chunk, chunk), chunk)
            give_copy(give_ref.at[run], got_ref.at[run]).start()

        @pl.when(tick == ticks - 1)
        def _():
            give_copy(give_ref, got_ref).wait()

        first = other_copy(vector, got_vector, vec_out.at[0], vec_in.at[0], "x")
        hops = []
        for number, to in enumerate(("core", "y", "z0", "z1")):
            count = 1 << number
            run = gathered.at[pl.ds((item // count) * count, count)]
            hops.append(other_copy(run, run, vec_out.at[number + 1], vec_in.at[number + 1], to))

        @pl.when(tick == 0)
        def _():
            first.start()

        @pl.when(tick == LAG)
        def _():
            first.wait()
            heights = lax.broadcasted_iota(jnp.int32, vector.shape, 0)
            gathered[item] = vector[...] + jnp.where(
                heights < vector.shape[0] - 8, got_vector[...], 0.0
            )
            hops[0].start()

        for number in range(4):

            @pl.when(tick == LAG * (number + 2))
            def _(number=number):
                hops[number].wait()
                if number < 3:
                    hops[number + 1].start()
                else:
                    gathered_out[...] = gathered[...]


ATTENTION_STEPS = 32
GIVES = 20
HOPS = {
    1: [
        ("d", "core", (8, 64, 256)),
        ("ay", "y", (4, 64, 256)),
        ("az", "z0", (2, 64, 256)),
        ("aw", "z1", (64, 256)),
        ("ax", "x", (64, 256)),
    ],
    2: [
        ("d", "core", (8, 64, 256)),
        ("ay", "y", (4, 64, 128)),
        ("az", "z0", (2, 64, 128)),
        ("aw", "z1", (64, 128)),
        ("ax", "x", (64, 128)),
        ("bx", "x", (8, 32, 128)),
        ("by", "y", (4, 32, 128)),
        ("bz", "z0", (2, 32, 128)),
        ("bw", "z1", (32, 128)),
        ("bg", "x", (32, 128)),
    ],
}


def sum_weights(weights, lefts, sides, vector=None, share=None, attention=None):
    tile = 256
    stages = 4 + sides
    rows = lefts[0].shape[1]
    low = lambda *shape: pltpu.VMEM(shape, jnp.bfloat16)
    full = lambda *shape: pltpu.VMEM(shape, jnp.float32)
    units = sum(segment[0][1].shape[1] for weight in weights for segment in weight) // tile
    inputs, outputs, scratch = [], [], []
    for left in lefts:
        spec = pl.BlockSpec(left.shape, lambda i: (0, 0), pipeline_mode=pl.Buffered(1))
        inputs.append(("lefts", left, spec))
        scratch.append(("turned", low(*left.shape[::-1])))
    seen, plan = set(), []
    at = flops = rights = 0
    for weight in weights:
        terms, turns = [], []
        place = 0
        for segment in weight:
            count = segment[0][1].shape[1] // tile
            pairs = []
            for which, right in segment:
                if which not in seen:
                    seen.add(which)
                    turns.append((which, place))
                pairs.append((which, rights))
                rights += 1
                flops += 2 * rows * right.shape[0] * right.shape[1]
                spec = pl.BlockSpec(
                    (right.shape[0], tile),
                    lambda i, start=at + place, count=count: (
                        0,
                        jnp.clip(i - start, 0, count - 1),
                    ),
                )
                inputs.append(("rights", right, spec))
            terms.append((count, tuple(pairs)))
            place += count
        plan.append((place, tuple(terms), tuple(turns)))
        spec = pl.BlockSpec(
            (64, tile),
            lambda i, start=at, count=place: (
                0,
                jnp.clip(i - LAG * stages - start, 0, count - 1),
            ),
        )
        outputs.append(("outs", jax.ShapeDtypeStruct((64, place * tile), jnp.float32), spec))
        at += place
    hops = HOPS[sides]
    for _, _, shape in hops:
        scratch.append(("send", low(2, *shape)))
        scratch.append(("recv", low(4, *shape)))
        scratch.append(("keep", full(2, *shape)))
    scratch.append(("last", full(2, 64, 128)))
    scratch.append(("sems", pltpu.SemaphoreType.DMA((len(hops), 2))))
    scratch.append(("sems", pltpu.SemaphoreType.DMA((len(hops), 4))))
    transcendentals = 0
    if vector is not None:
        anywhere = pl.BlockSpec(memory_space=pl.ANY)
        inputs.append(("vector", vector, pl.BlockSpec(vector.shape, lambda i: (0, 0))))
        inputs.append(("give", share, anywhere))
        shape = (16,) + vector.shape
        outputs.append(("gathered", jax.ShapeDtypeStruct(shape, jnp.float32), pl.BlockSpec(shape, lambda i: (0, 0, 0))))
        outputs.append(("got", jax.ShapeDtypeStruct(share.shape, share.dtype), anywhere))
        scratch += [("gather", full(*shape)), ("gather", full(*vector.shape))]
        scratch += [("gather", pltpu.SemaphoreType.DMA((5,)))] * 2
        scratch += [("give_sems", pltpu.SemaphoreType.DMA((1,)))] * 2
    if attention is not None:
        lim, qkv, kv_rest, do, o, lse = attention
        count, width = do.shape
        pairs = width // 128
        place = lambda skip: pl.BlockSpec(
            (count, 128), lambda i: (0, jnp.minimum(i // 4, pairs - 1) + skip)
        )
        inputs.append(("attention", lim, pl.BlockSpec(memory_space=pltpu.SMEM)))
        for operand, skip in (
            (qkv, 0),
            (qkv, pairs),
            (qkv, 2 * pairs),
            (kv_rest, 0),
            (kv_rest, pairs),
            (do, 0),
            (o, 0),
            (lse, 0),
        ):
            inputs.append(("attention", operand, place(skip)))
        for _ in range(5):
            outputs.append(("grads", jax.ShapeDtypeStruct(do.shape, jnp.bfloat16), place(0)))
        scratch += [("held", low(count, 128)), ("held", low(count, 128)), ("held", full(count, 128))]
        flops += 40 * count * 2 * count * width
        transcendentals += count * 2 * count * width // 64
    groups = (
        ("lefts", "rights", "vector", "give", "attention"),
        ("outs", "gathered", "got", "grads"),
        ("turned", "send", "recv", "keep", "last", "sems", "gather", "give_sems", "held"),
    )
    layout, ordered = [], []
    for names, entries in zip(groups, (inputs, outputs, scratch)):
        found = [[entry[1:] for entry in entries if entry[0] == name] for name in names]
        layout += [(name, len(run)) for name, run in zip(names, found)]
        ordered.append([entry for run in found for entry in run])
    operands = [operand for operand, _ in ordered[0]]
    results = pl.pallas_call(
        functools.partial(sum_kernel, units, tuple(plan), tuple(layout), sides),
        grid=(units + LAG * stages,),
        in_specs=[spec for _, spec in ordered[0]],
        out_specs=[spec for _, spec in ordered[1]],
        out_shape=[shape for shape, _ in ordered[1]],
        scratch_shapes=[shape for shape, in ordered[2]],
        compiler_params=pltpu.CompilerParams(
            vmem_limit_bytes=58 << 20, collective_id=sides - 1, has_side_effects=True
        ),
        cost_estimate=pl.CostEstimate(
            flops=flops,
            transcendentals=transcendentals,
            bytes_accessed=sum(2 * operand.size for operand in operands),
        ),
    )(*operands)
    return results


def per_device(
    frames,
    cotangent,
    section,
    prompt_len,
    section_embed,
    ada_proj,
    ada_bias,
    w_qkv,
    w_out,
    w_up,
    w_down,
):
    _, row_count, width = frames.shape
    frames, cotangent = frames[0], cotangent[0]
    seq_size = lax.axis_size("seq")
    item_size = lax.axis_size("items")
    seq_me, item_me = lax.axis_index("seq"), lax.axis_index("items")
    side = jnp.bitwise_and(item_me, 1).astype(jnp.int32).reshape(1)
    turns = list(range(1, seq_size))
    fetch = lambda values, turn: lax.ppermute(
        values, "seq", [((i + turn) % seq_size, i) for i in range(seq_size)]
    )
    give = lambda values, turn: lax.ppermute(
        values, "seq", [(i, (i + turn) % seq_size) for i in range(seq_size)]
    )
    others = [fetch(frames, turn) for turn in turns]
    sources = jnp.stack([(seq_me + turn) % seq_size for turn in [0] + turns])
    limits = jnp.where(sources == 0, prompt_len[0], row_count).astype(jnp.int32)

    section_count = section_embed.shape[0]
    onehot = (section[:, None] == jnp.arange(section_count, dtype=jnp.int32)[None, :]).astype(
        jnp.float32
    )
    cond = jnp.dot(onehot, section_embed, precision=HIGHEST)
    modul = jnp.dot(cond, ada_proj.astype(jnp.float32), precision=HIGHEST) + ada_bias[None, :]
    scale_one, shift_one, scale_two, shift_two = jnp.split(modul, 4, axis=-1)
    inputs = frames.astype(jnp.float32)
    normed_one, inv_one = normalize(inputs)
    modulate = lambda normed: (normed * (1.0 + scale_one) + shift_one).astype(jnp.bfloat16)
    attn_in = modulate(normed_one)
    qkv = project(attn_in, w_qkv).astype(jnp.bfloat16)
    grad_act = back_project(cotangent, w_down).astype(jnp.bfloat16)
    others, qkv, grad_act = lax.optimization_barrier((others, qkv, grad_act))
    rest = jnp.concatenate(others) if len(others) > 1 else others[0]
    normed_rest, _ = normalize(rest.astype(jnp.float32))
    attn_rest = modulate(normed_rest)
    kv_rest = project(attn_rest, w_qkv[:, width:]).astype(jnp.bfloat16)
    att, lse = attend(limits, qkv, kv_rest, width)
    mid = inputs + project(att, w_out)
    normed_two, inv_two = normalize(mid)
    ffn_in = (normed_two * (1.0 + scale_two) + shift_two).astype(jnp.bfloat16)
    upper = project(ffn_in, w_up)
    act = gelu_exact(upper).astype(jnp.bfloat16)
    grad_upper = (grad_act.astype(jnp.float32) * gelu_slope(upper)).astype(jnp.bfloat16)
    out_frames = (mid + project(act, w_down)).astype(jnp.bfloat16)

    grad_out = cotangent.astype(jnp.float32)
    fused = seq_size == 2 and item_size == 16 and width == 1024
    if fused:
        sum_down = lax.psum_scatter(
            outer_sum(act, cotangent).astype(jnp.bfloat16),
            "items",
            scatter_dimension=0,
            tiled=True,
        )
    else:
        down_pieces = outer(side, [act], [[(0, cotangent)]], item_size, 256)
    grad_ffn_in = lax.optimization_barrier(back_project(grad_upper, w_up))
    grad_scale_two = jnp.sum(grad_ffn_in * normed_two, 0)
    grad_shift_two = jnp.sum(grad_ffn_in, 0)
    grad_mid = grad_out + norm_back(grad_ffn_in * (1.0 + scale_two), normed_two, inv_two)
    grad_mid_low = grad_mid.astype(jnp.bfloat16)
    grad_att = back_project(grad_mid_low, w_out).astype(jnp.bfloat16)
    up_terms = [[(0, grad_upper)]]
    out_terms = [[(1, grad_mid_low)]]
    if fused:
        sum_up, sum_out, grad_query, grad_key, grad_value, key_rest, value_rest = sum_weights(
            [up_terms, out_terms],
            [ffn_in, att],
            2,
            attention=(limits, qkv, kv_rest, grad_att, att, lse),
        )
    else:
        grad_query, grad_key, grad_value, key_rest, value_rest = attend_back(
            limits, qkv, kv_rest, grad_att, att, lse
        )
    qkv_terms = [
        [(0, grad_query)],
        [(0, grad_key), (1, key_rest)],
        [(0, grad_value), (1, value_rest)],
    ]
    w_key, w_value = w_qkv[:, width : 2 * width], w_qkv[:, 2 * width :]
    share = back_project(key_rest, w_key) + back_project(value_rest, w_value)
    partial = (
        back_project(grad_query, w_qkv[:, :width])
        + back_project(grad_key, w_key)
        + back_project(grad_value, w_value)
    )
    partial, share = lax.optimization_barrier((partial, share))
    share_low = share.astype(jnp.bfloat16)
    grad_scale_one = jnp.sum(partial * normed_one, 0) + jnp.sum(share * normed_rest, 0)
    grad_shift_one = jnp.sum(partial, 0) + jnp.sum(share, 0)
    grad_modul = jnp.concatenate(
        [grad_scale_one, grad_shift_one, grad_scale_two, grad_shift_two]
    )[None, :]
    if fused:
        vector = jnp.concatenate(
            [
                grad_modul.reshape(4 * width // 128, 128),
                jnp.pad(onehot, ((0, 7), (0, 128 - section_count))),
            ]
        )
        sum_qkv, tagged, got_share = sum_weights(
            [qkv_terms], [attn_in, attn_rest], 1, vector=vector, share=share_low
        )
        grad_rest = [got_share]
        tagged = tagged[:, : 4 * width // 128 + 1].reshape(item_size, 4 * width + 128)
        sum_down = sum_down.astype(jnp.float32) + swap(sum_down, "seq", 1).astype(jnp.float32)
    else:
        grad_rest = [
            give(share_low[i * row_count : (i + 1) * row_count], turn)
            for i, turn in enumerate(turns)
        ]
        shift = lambda terms, by: [[(i - by, right) for i, right in run] for run in terms]
        sum_down = finish(down_pieces, "items", "seq")
        sum_up = finish(outer(side, [ffn_in], up_terms, item_size, 512), "items", "seq")
        sum_out = finish(
            outer(side, [att], shift(out_terms, 1), item_size, 512), "items", "seq"
        )
        sum_qkv = finish(
            outer(side, [attn_in, attn_rest], qkv_terms, item_size, 512),
            "items",
            "seq",
        )
        for bit in bits_of("seq"):
            grad_modul = grad_modul + swap(grad_modul, "seq", bit)
        tagged = jnp.concatenate(
            [grad_modul, jnp.pad(onehot, ((0, 0), (0, 128 - section_count)))], -1
        )
        tagged = gather_items(tagged, "items")
    grad_attn_in = partial
    for got in grad_rest:
        grad_attn_in = grad_attn_in + got.astype(jnp.float32)
    frames_grad = (
        grad_mid + norm_back(grad_attn_in * (1.0 + scale_one), normed_one, inv_one)
    ).astype(jnp.bfloat16)

    modul_all, onehot_all = tagged[:, : 4 * width], tagged[:, 4 * width :][:, :section_count]
    block = width // item_size
    own_embed = lax.dynamic_slice_in_dim(section_embed, item_me * block, block, 1)
    own_cond = jnp.dot(onehot_all, own_embed, precision=HIGHEST)
    sum_ada = lax.dot_general(own_cond, modul_all, (((0,), (0,)), ((), ())), precision=HIGHEST)
    sum_bias = jnp.sum(
        lax.dynamic_slice_in_dim(modul_all, item_me * 4 * block, 4 * block, 1), 0
    )
    own_ada = lax.dynamic_slice_in_dim(ada_proj, item_me * block, block, 0).astype(jnp.float32)
    grad_cond = lax.dot_general(modul_all, own_ada, (((1,), (1,)), ((), ())), precision=HIGHEST)
    sum_embed = lax.dot_general(
        onehot_all, grad_cond, (((0,), (0,)), ((), ())), precision=HIGHEST
    )
    return (
        out_frames[None],
        frames_grad[None],
        sum_embed,
        sum_ada,
        sum_bias,
        sum_qkv,
        sum_out,
        sum_up,
        sum_down,
    )


def solution(mesh):
    in_specs = (
        P("items", "seq", None),
        P("items", "seq", None),
        P("items"),
        P("items"),
        P(),
        P(),
        P(),
        P(),
        P(),
        P(),
        P(),
    )
    out_specs = (
        P("items", "seq", None),
        P("items", "seq", None),
        P(None, "items"),
        P("items", None),
        P("items"),
        P("items", None),
        P("items", None),
        P("items", None),
        P("items", None),
    )
    return jax.shard_map(
        per_device, mesh=mesh, in_specs=in_specs, out_specs=out_specs, check_vma=False
    )
```

```python
import functools

import jax
import jax.numpy as jnp
from jax import lax
from jax.experimental import pallas as pl
from jax.experimental.pallas import tpu as pltpu
from jax.sharding import PartitionSpec as P

HEADS = 16


EPS = 1e-05
NEGATIVE = -1e30
SQRT_HALF = 0.7071067811865476
INV_SQRT_TAU = 0.3989422804014327
HIGHEST = lax.Precision.HIGHEST


def normalize(values):
    mean = jnp.mean(values, -1, keepdims=True)
    centered = values - mean
    inverse = lax.rsqrt(jnp.mean(centered * centered, -1, keepdims=True) + EPS)
    return (centered * inverse, inverse)


def norm_back(grad, normed, inverse):
    first = jnp.mean(grad, -1, keepdims=True)
    second = jnp.mean(grad * normed, -1, keepdims=True)
    return (grad - first - normed * second) * inverse


def gelu_exact(values):
    return 0.5 * values * (1.0 + lax.erf(values * SQRT_HALF))


def gelu_slope(values):
    return (
        0.5 * (1.0 + lax.erf(values * SQRT_HALF))
        + values * jnp.exp(-0.5 * values * values) * INV_SQRT_TAU
    )


def project(left, weight):
    flat = left.reshape(-1, left.shape[-1])
    result = jnp.dot(flat, weight, preferred_element_type=jnp.float32)
    return result.reshape(left.shape[:-1] + (weight.shape[1],))


def back_project(grad, weight):
    flat = grad.reshape(-1, grad.shape[-1])
    result = lax.dot_general(
        flat, weight, (((1,), (1,)), ((), ())), preferred_element_type=jnp.float32
    )
    return result.reshape(grad.shape[:-1] + (weight.shape[0],))


BIG = 1e30

def split3(x):
    hi = x.astype(jnp.bfloat16).astype(jnp.float32)
    rest = x - hi
    mid = rest.astype(jnp.bfloat16).astype(jnp.float32)
    return hi, mid, rest - mid

def dot(a, b, ca, cb):
    return lax.dot_general(a, b, (((ca,), (cb,)), ((), ())), preferred_element_type=jnp.float32)


def fwd_kernel(rows, blocks, lim_ref, q_ref, ko_ref, vo_ref, kt_ref, vt_ref, o_ref, lse_ref):
    lane = lax.broadcasted_iota(jnp.int32, (1, 128), 1)
    low = lane < 64
    row = lax.broadcasted_iota(jnp.int32, (rows, 1), 0)
    q = q_ref[...].astype(jnp.float32) * 0.125
    outs, lses = [], []
    for h in range(2):
        own = low if h == 0 else jnp.logical_not(low)
        first = 64 * (1 - h)
        qa = jnp.where(own, q, jnp.where(lane == first, 1.0, 0.0)).astype(jnp.bfloat16)
        scores, values = [], []
        for j in range(blocks):
            k = ko_ref[...] if j == 0 else kt_ref[pl.ds((j - 1) * rows, rows), :]
            v = vo_ref[...] if j == 0 else vt_ref[pl.ds((j - 1) * rows, rows), :]
            bias = jnp.where(row < lim_ref[j], 0.0, -BIG)
            ka = jnp.where(own, k.astype(jnp.float32), jnp.where(lane == first, bias, 0.0)).astype(jnp.bfloat16)
            va = jnp.where(own, v.astype(jnp.float32), 1.0).astype(jnp.bfloat16)
            scores.append(dot(qa, ka, 1, 1))
            values.append(va)
        top = functools.reduce(jnp.maximum, [jnp.max(s, -1, keepdims=True) for s in scores])
        total = None
        for s, va in zip(scores, values):
            p = jnp.exp(s - top).astype(jnp.bfloat16)
            part = dot(p, va, 1, 0)
            total = part if total is None else total + part
        outs.append(total / pltpu.roll(total, 64, 1))
        lses.append(top + jnp.log(total))
    o_ref[...] = jnp.where(low, outs[0], outs[1]).astype(o_ref.dtype)
    lse_ref[...] = jnp.where(low, lses[1], lses[0])


def bwd_kernel(rows, blocks, lim_ref, q_ref, ko_ref, vo_ref, kt_ref, vt_ref, do_ref, o_ref, lse_ref,
               dq_ref, dko_ref, dvo_ref, dkt_ref, dvt_ref):
    lane = lax.broadcasted_iota(jnp.int32, (1, 128), 1)
    low = lane < 64
    row = lax.broadcasted_iota(jnp.int32, (rows, 1), 0)
    q = q_ref[...].astype(jnp.float32) * 0.125
    qs = q.astype(jnp.bfloat16)
    do_low = do_ref[...]
    do = do_low.astype(jnp.float32)
    prod = do * o_ref[...].astype(jnp.float32)
    lh, lm, ll = split3(lse_ref[...])
    heads = []
    for h in range(2):
        own = low if h == 0 else jnp.logical_not(low)
        f = 64 * (1 - h)
        delta = jnp.sum(jnp.where(own, prod, 0.0), -1, keepdims=True)
        dh, dm, dl = split3(delta)
        qa = jnp.where(own, q, jnp.where(lane == f, 1.0, jnp.where(lane == f + 1, -lh, jnp.where(lane == f + 2, -lm, jnp.where(lane == f + 3, -ll, 0.0))))).astype(jnp.bfloat16)
        doa = jnp.where(own, do, jnp.where(lane == f, -dh, jnp.where(lane == f + 1, -dm, jnp.where(lane == f + 2, -dl, 0.0)))).astype(jnp.bfloat16)
        kone = jnp.where((lane > f) & (lane <= f + 3), 1.0, 0.0)
        vone = jnp.where((lane >= f) & (lane < f + 3), 1.0, 0.0)
        dq = None
        res = []
        for j in range(blocks):
            k = ko_ref[...] if j == 0 else kt_ref[pl.ds((j - 1) * rows, rows), :]
            v = vo_ref[...] if j == 0 else vt_ref[pl.ds((j - 1) * rows, rows), :]
            bias = jnp.where(row < lim_ref[j], 0.0, -BIG)
            ka = jnp.where(own, k.astype(jnp.float32), jnp.where(lane == f, bias, kone)).astype(jnp.bfloat16)
            va = jnp.where(own, v.astype(jnp.float32), vone).astype(jnp.bfloat16)
            pt = jnp.exp(dot(ka, qa, 1, 1))
            dpt = dot(va, doa, 1, 1)
            dst = (pt * dpt).astype(jnp.bfloat16)
            dv = dot(pt.astype(jnp.bfloat16), do_low, 1, 0)
            dk = dot(dst, qs, 1, 0)
            part = dot(dst, k, 0, 0)
            dq = part if dq is None else dq + part
            res.append((dk, dv))
        heads.append((dq, res))
    dq_ref[...] = (jnp.where(low, heads[0][0], heads[1][0]) * 0.125).astype(dq_ref.dtype)
    for j in range(blocks):
        dk = jnp.where(low, heads[0][1][j][0], heads[1][1][j][0]).astype(dko_ref.dtype)
        dv = jnp.where(low, heads[0][1][j][1], heads[1][1][j][1]).astype(dko_ref.dtype)
        if j == 0:
            dko_ref[...] = dk
            dvo_ref[...] = dv
        else:
            dkt_ref[pl.ds((j - 1) * rows, rows), :] = dk
            dvt_ref[pl.ds((j - 1) * rows, rows), :] = dv


def specs_of(rows, others, width):
    pairs = width // 128
    place = lambda count, skip: pl.BlockSpec((count, 128), lambda i, lim: (0, i + skip))
    inputs = [place(rows, 0), place(rows, pairs), place(rows, 2 * pairs), place(others, 0), place(others, pairs)]
    return inputs, place(rows, 0), place(others, 0)


def attend(lim, qkv, kv_rest, width):
    rows, others = qkv.shape[0], kv_rest.shape[0]
    blocks = 1 + others // rows
    inputs, own, oth = specs_of(rows, others, width)
    keys = rows + others
    return pl.pallas_call(
        functools.partial(fwd_kernel, rows, blocks),
        grid_spec=pltpu.PrefetchScalarGridSpec(num_scalar_prefetch=1, grid=(width // 128,),
            in_specs=inputs, out_specs=[own, own]),
        out_shape=[jax.ShapeDtypeStruct((rows, width), jnp.bfloat16), jax.ShapeDtypeStruct((rows, width), jnp.float32)],
        compiler_params=pltpu.CompilerParams(vmem_limit_bytes=56 << 20),
        cost_estimate=pl.CostEstimate(flops=16 * rows * keys * width, transcendentals=rows * keys * width // 64,
            bytes_accessed=2 * width * (2 * rows + 2 * keys) + 4 * rows * width),
    )(lim, qkv, qkv, qkv, kv_rest, kv_rest)


def attend_back(lim, qkv, kv_rest, do, o, lse):
    (rows, width), others = do.shape, kv_rest.shape[0]
    blocks = 1 + others // rows
    inputs, own, oth = specs_of(rows, others, width)
    keys = rows + others
    s = lambda n: jax.ShapeDtypeStruct((n, width), jnp.bfloat16)
    return pl.pallas_call(
        functools.partial(bwd_kernel, rows, blocks),
        grid_spec=pltpu.PrefetchScalarGridSpec(num_scalar_prefetch=1, grid=(width // 128,),
            in_specs=inputs + [own, own, own], out_specs=[own, own, own, oth, oth]),
        out_shape=[s(rows), s(rows), s(rows), s(others), s(others)],
        compiler_params=pltpu.CompilerParams(vmem_limit_bytes=56 << 20),
        cost_estimate=pl.CostEstimate(flops=40 * rows * keys * width, transcendentals=rows * keys * width // 64,
            bytes_accessed=2 * width * (4 * rows + 4 * keys) + 4 * rows * width),
    )(lim, qkv, qkv, qkv, kv_rest, kv_rest, do, o, lse)


def outer_kernel(plan, halves, first_tiles, side_ref, *refs):
    lefts, plan_rights, outs, turned = refs[: plan[0]], refs[plan[0] : plan[1]], refs[plan[1] : plan[1] + 4], refs[plan[1] + 4 :]
    step = pl.program_id(0)

    @pl.when(step == 0)
    def _():
        for left, flip in zip(lefts, turned):
            flip[...] = left[...].T

    at = 0
    place = 0
    for tiles, terms in plan[2]:
        rights = plan_rights[place : place + len(terms)]
        place += len(terms)

        @pl.when((step >= at) & (step < at + tiles))
        def _(rights=rights, terms=terms):
            total = None
            for which, right in zip(terms, rights):
                part = dot(turned[which][...], right[...], 1, 0)
                total = part if total is None else total + part
            rows, columns = total.shape
            split = total.astype(jnp.bfloat16).reshape(halves, 2, rows // (2 * halves), columns)
            even = side_ref[0] == 0
            keep = jnp.where(even, split[:, 0], split[:, 1])
            send = jnp.where(even, split[:, 1], split[:, 0])

            @pl.when(step < first_tiles)
            def _():
                outs[0][...] = send
                outs[1][...] = keep

            @pl.when(step >= first_tiles)
            def _():
                outs[2][...] = send
                outs[3][...] = keep

        at += tiles


def outer(side, lefts, segments, parts, tile):
    rows = lefts[0].shape[1]
    halves = parts // 2
    block = rows // parts
    width = sum(segment[0][1].shape[1] for segment in segments)
    steps = width // tile
    first_tiles = steps // 2
    in_specs = [pl.BlockSpec(left.shape, lambda i, s: (0, 0)) for left in lefts]
    operands = list(lefts)
    plan = []
    at = 0
    flops = 0
    for segment in segments:
        tiles = segment[0][1].shape[1] // tile
        for which, right in segment:
            in_specs.append(
                pl.BlockSpec(
                    (right.shape[0], tile),
                    lambda i, s, at=at, tiles=tiles: (0, jnp.clip(i - at, 0, tiles - 1)),
                )
            )
            operands.append(right)
            flops += 2 * rows * right.shape[0] * right.shape[1]
        plan.append((tiles, tuple(which for which, _ in segment)))
        at += tiles
    first = pl.BlockSpec((halves, block, tile), lambda i, s: (0, 0, jnp.minimum(i, first_tiles - 1)))
    second = pl.BlockSpec((halves, block, tile), lambda i, s: (0, 0, jnp.maximum(i - first_tiles, 0)))
    shape = lambda count: jax.ShapeDtypeStruct((halves, block, count * tile), jnp.bfloat16)
    moved = sum(2 * operand.size for operand in operands) + 2 * rows * width
    return pl.pallas_call(
        functools.partial(
            outer_kernel, (len(lefts), len(operands), tuple(plan)), halves, first_tiles
        ),
        grid_spec=pltpu.PrefetchScalarGridSpec(
            num_scalar_prefetch=1,
            grid=(steps,),
            in_specs=in_specs,
            out_specs=[first, first, second, second],
            scratch_shapes=[pltpu.VMEM(left.shape[::-1], jnp.bfloat16) for left in lefts],
        ),
        out_shape=[shape(first_tiles)] * 2 + [shape(steps - first_tiles)] * 2,
        compiler_params=pltpu.CompilerParams(vmem_limit_bytes=58 << 20),
        cost_estimate=pl.CostEstimate(flops=flops, transcendentals=0, bytes_accessed=moved),
    )(side, *operands)


def swap(values, axis, bit):
    size = lax.axis_size(axis)
    return lax.ppermute(values, axis, [(i, i ^ bit) for i in range(size)])


def bits_of(axis):
    size = lax.axis_size(axis)
    return [1 << place for place in range(size.bit_length() - 1)]


def add_low(left, right):
    return (left.astype(jnp.float32) + right.astype(jnp.float32)).astype(jnp.bfloat16)


def half_of(values, dim, which):
    return lax.dynamic_index_in_dim(values, which, dim, keepdims=False)


def reduce_rows(keep, got, axis):
    me = lax.axis_index(axis)
    for bit in bits_of(axis)[1:]:
        mine = jnp.bitwise_and(me // bit, 1)
        shape = keep.shape
        view = (shape[0] // 2, 2) + shape[1:]
        keep, got = keep.reshape(view), got.reshape(view)
        send = add_low(half_of(keep, 1, 1 - mine), half_of(got, 1, 1 - mine))
        keep = add_low(half_of(keep, 1, mine), half_of(got, 1, mine))
        got = swap(send, axis, bit)
    return keep, got


def finish(pieces, rows_axis, seq_axis):
    send_a, keep_a, send_b, keep_b = pieces
    got_a = swap(send_a, rows_axis, 1)
    got_b = swap(send_b, rows_axis, 1)
    keep_a, got_a = reduce_rows(keep_a, got_a, rows_axis)
    total_a = (keep_a.astype(jnp.float32) + got_a.astype(jnp.float32))[0]
    for bit in bits_of(seq_axis):
        low = total_a.astype(jnp.bfloat16)
        total_a = low.astype(jnp.float32) + swap(low, seq_axis, bit).astype(jnp.float32)
    me = lax.axis_index(seq_axis)
    for bit in bits_of(seq_axis):
        mine = jnp.bitwise_and(me // bit, 1)
        width = keep_b.shape[-1] // 2
        cut = lambda values, which: lax.dynamic_slice_in_dim(values, which * width, width, 2)
        send = add_low(cut(keep_b, 1 - mine), cut(got_b, 1 - mine))
        keep_b = add_low(cut(keep_b, mine), cut(got_b, mine))
        got_b = swap(send, seq_axis, bit)
    keep_b, got_b = reduce_rows(keep_b, got_b, rows_axis)
    total_b = add_low(keep_b, got_b)[0]
    for bit in reversed(bits_of(seq_axis)):
        mine = jnp.bitwise_and(me // bit, 1)
        other = swap(total_b, seq_axis, bit)
        total_b = jnp.where(
            mine == 0,
            jnp.concatenate([total_b, other], -1),
            jnp.concatenate([other, total_b], -1),
        )
    return jnp.concatenate([total_a, total_b.astype(jnp.float32)], -1)


def gather_items(values, axis):
    me = lax.axis_index(axis)
    for bit in bits_of(axis):
        other = swap(values, axis, bit)
        mine = jnp.bitwise_and(me // bit, 1)
        values = jnp.where(
            mine == 0, jnp.concatenate([values, other]), jnp.concatenate([other, values])
        )
    return values


LAG = 2
MESH = pl.DeviceIdType.MESH


def attention_step(step, lim_ref, q_ref, ko_ref, vo_ref, kt_ref, vt_ref, do_ref, o_ref, lse_ref,
                   dq_ref, dko_ref, dvo_ref, dkt_ref, dvt_ref, qa_ref, doa_ref, dq_sum):
    rows = q_ref.shape[0]
    head, j = (step // 2) % 2, step % 2
    lane = lax.broadcasted_iota(jnp.int32, (1, 128), 1)
    own = (lane // 64) == head
    f = 64 * (1 - head)

    @pl.when(j == 0)
    def _():
        q = q_ref[...].astype(jnp.float32) * 0.125
        do = do_ref[...].astype(jnp.float32)
        prod = do * o_ref[...].astype(jnp.float32)
        lh, lm, ll = split3(lse_ref[...])
        delta = jnp.sum(jnp.where(own, prod, 0.0), -1, keepdims=True)
        dh, dm, dl = split3(delta)
        qa_ref[...] = jnp.where(own, q, jnp.where(lane == f, 1.0, jnp.where(lane == f + 1, -lh, jnp.where(lane == f + 2, -lm, jnp.where(lane == f + 3, -ll, 0.0))))).astype(jnp.bfloat16)
        doa_ref[...] = jnp.where(own, do, jnp.where(lane == f, -dh, jnp.where(lane == f + 1, -dm, jnp.where(lane == f + 2, -dl, 0.0)))).astype(jnp.bfloat16)

    row = lax.broadcasted_iota(jnp.int32, (rows, 1), 0)
    wide = lambda ref: ref[...].astype(jnp.float32)
    k = jnp.where(j == 0, wide(ko_ref), wide(kt_ref))
    v = jnp.where(j == 0, wide(vo_ref), wide(vt_ref))
    kone = jnp.where((lane > f) & (lane <= f + 3), 1.0, 0.0)
    vone = jnp.where((lane >= f) & (lane < f + 3), 1.0, 0.0)
    bias = jnp.where(row < lim_ref[j], 0.0, -BIG)
    ka = jnp.where(own, k, jnp.where(lane == f, bias, kone)).astype(jnp.bfloat16)
    va = jnp.where(own, v, vone).astype(jnp.bfloat16)
    qa, doa = qa_ref[...], doa_ref[...]
    pt = jnp.exp(dot(ka, qa, 1, 1))
    dpt = dot(va, doa, 1, 1)
    dst = (pt * dpt).astype(jnp.bfloat16)
    dv = dot(pt.astype(jnp.bfloat16), doa, 1, 0)
    dk = dot(dst, qa, 1, 0)
    part = dot(dst, ka, 0, 0)

    def put(ref, values):
        @pl.when(head == 0)
        def _():
            ref[...] = values.astype(ref.dtype)

        @pl.when(head == 1)
        def _():
            ref[...] = jnp.where(lane < 64, wide(ref), values).astype(ref.dtype)

    @pl.when(j == 0)
    def _():
        dq_sum[...] = part
        put(dko_ref, dk)
        put(dvo_ref, dv)

    @pl.when(j == 1)
    def _():
        put(dq_ref, (dq_sum[...] + part) * 0.125)
        put(dkt_ref, dk)
        put(dvt_ref, dv)


def sum_kernel(units, plan, layout, sides, *refs):
    at = 0
    parts = {}
    for name, count in layout:
        parts[name] = refs[at : at + count]
        at += count
    lefts, rights, outs, turned = (parts[name] for name in ("lefts", "rights", "outs", "turned"))
    send, recv, keep = parts["send"], parts["recv"], parts["keep"]
    out_sem, in_sem = parts["sems"]
    stages = 4 + sides
    cut = 256 // sides
    tick = pl.program_id(0)
    item, seq = lax.axis_index("items"), lax.axis_index("seq")
    bit = lambda value, place: jnp.bitwise_and(value // (1 << place), 1)
    core, y, z0, z1, x = bit(item, 0), bit(item, 1), bit(item, 2), bit(item, 3), seq
    flip = lambda place: item + (1 - 2 * bit(item, place)) * (1 << place)
    partners = {
        "core": (flip(0), seq),
        "y": (flip(1), seq),
        "z0": (flip(2), seq),
        "z1": (flip(3), seq),
        "x": (item, 1 - seq),
    }

    @pl.when(tick == 0)
    def _():
        barrier = pltpu.get_barrier_semaphore()
        for partner in partners.values():
            pl.semaphore_signal(barrier, inc=1, device_id=partner, device_id_type=MESH)
        pl.semaphore_wait(barrier, len(partners))

    wide = lambda values: values.astype(jnp.float32)
    low = lambda values: values.astype(jnp.bfloat16)

    def choose(values, axis, which):
        first = lax.index_in_dim(values, 0, axis, keepdims=False)
        second = lax.index_in_dim(values, 1, axis, keepdims=False)
        mine = jnp.where(which == 0, first, second)
        other = jnp.where(which == 0, second, first)
        return mine, other

    table = {name: (i, to) for i, (name, to, _) in enumerate(HOPS[sides])}

    def copy(name, unit):
        number, to = table[name]
        slot, landing = unit % 2, unit % 4
        return pltpu.make_async_remote_copy(
            src_ref=send[number].at[slot],
            dst_ref=recv[number].at[landing],
            send_sem=out_sem.at[number, slot],
            recv_sem=in_sem.at[number, landing],
            device_id=partners[to],
            device_id_type=MESH,
        )

    def post(name, unit, mine, other):
        number, _ = table[name]
        keep[number][unit % 2] = mine
        send[number][unit % 2] = low(other)
        copy(name, unit).start()

    def take(name, unit):
        number, _ = table[name]
        copy(name, unit).wait()
        return keep[number][unit % 2] + wide(recv[number][unit % 4])

    def turn(which, start):
        left, target = lefts[which], turned[which]
        halves = target.shape[0]
        if halves == 1:

            @pl.loop(0, target.shape[1] // 128)
            def _(i):
                run = pl.ds(pl.multiple_of(i * 128, 128), 128)
                target[0, run] = left[:, run].T

        else:

            @pl.loop(0, 16)
            def _(i):
                block = left[:, pl.ds(pl.multiple_of(i * 256 + start * 128, 128), 128)].T
                run = pl.ds(pl.multiple_of(i * 64, 64), 64)
                target[0, run] = block[:64]
                target[1, run] = block[64:]

    def stage_zero(unit):
        at = 0
        for count, terms, turns in plan:

            @pl.when((unit >= at) & (unit < at + count))
            def _(at=at, terms=terms, turns=turns):
                for which, start in turns:

                    @pl.when(unit == at + start)
                    def _(which=which, start=start):
                        turn(which, start // 8)

                place = 0
                for segment, pairs in terms:

                    @pl.when((unit >= at + place) & (unit < at + place + segment))
                    def _(pairs=pairs):
                        total = None
                        for which, right in pairs:
                            half = ((unit - at) // 4) % turned[which].shape[0]
                            part = dot(turned[which][half], rights[right][...], 1, 0)
                            total = part if total is None else total + part
                        post("d", unit, *choose(total.reshape(8, 2, 64, 256), 1, core))

                    place += segment

            at += count

    def stage_one(unit):
        total = take("d", unit)
        post("ay", unit, *choose(total[:, :, :cut].reshape(4, 2, 64, cut), 1, y))
        if sides == 2:
            post("bx", unit, *choose(total[:, :, cut:].reshape(8, 2, 32, cut), 1, x))

    def stage_two(unit):
        post("az", unit, *choose(take("ay", unit).reshape(2, 2, 64, cut), 1, z0))
        if sides == 2:
            post("by", unit, *choose(take("bx", unit).reshape(4, 2, 32, cut), 1, y))

    def stage_three(unit):
        post("aw", unit, *choose(take("az", unit), 0, z1))
        if sides == 2:
            post("bz", unit, *choose(take("by", unit).reshape(2, 2, 32, cut), 1, z0))

    def stage_four(unit):
        total = low(take("aw", unit))
        post("ax", unit, wide(total), total)
        if sides == 2:
            post("bw", unit, *choose(take("bz", unit), 0, z1))

    def stage_five(unit):
        parts["last"][0][unit % 2] = take("ax", unit)
        total = low(take("bw", unit))
        post("bg", unit, wide(total), total)

    def stage_final(unit):
        if sides == 1:
            block = take("ax", unit)
        else:
            number, _ = table["bg"]
            copy("bg", unit).wait()
            other = wide(recv[number][unit % 4])
            mine = keep[number][unit % 2]
            top = jnp.where(x == 0, mine, other)
            bottom = jnp.where(x == 0, other, mine)
            block = jnp.concatenate(
                [parts["last"][0][unit % 2], jnp.concatenate([top, bottom], 0)], 1
            )
        at = 0
        for (count, _, _), out in zip(plan, outs):

            @pl.when((unit >= at) & (unit < at + count))
            def _(out=out):
                out[...] = block

            at += count

    steps = [stage_zero, stage_one, stage_two, stage_three, stage_four, stage_five][:stages]
    steps.append(stage_final)
    for number in range(stages, -1, -1):
        unit = tick - LAG * number

        @pl.when((unit >= 0) & (unit < units))
        def _(number=number, unit=unit):
            steps[number](unit)

    if parts["attention"]:

        @pl.when(tick < ATTENTION_STEPS)
        def _():
            attention_step(tick, *parts["attention"], *parts["grads"], *parts["held"])

    if parts["vector"]:
        vector, gathered_out = parts["vector"][0], parts["gathered"][0]
        gathered, got_vector, vec_out, vec_in = parts["gather"]
        give_ref, got_ref = parts["give"][0], parts["got"][0]
        give_out, give_in = parts["give_sems"]
        ticks = pl.num_programs(0)
        chunk = give_ref.shape[0] // GIVES

        def other_copy(source, target, out, into, to):
            return pltpu.make_async_remote_copy(
                src_ref=source,
                dst_ref=target,
                send_sem=out,
                recv_sem=into,
                device_id=partners[to],
                device_id_type=MESH,
            )

        give_copy = lambda source, target: other_copy(
            source, target, give_out.at[0], give_in.at[0], "x"
        )

        @pl.when(tick < GIVES)
        def _():
            run = pl.ds(pl.multiple_of(tick * chunk, chunk), chunk)
            give_copy(give_ref.at[run], got_ref.at[run]).start()

        @pl.when(tick == ticks - 1)
        def _():
            give_copy(give_ref, got_ref).wait()

        first = other_copy(vector, got_vector, vec_out.at[0], vec_in.at[0], "x")
        hops = []
        for number, to in enumerate(("core", "y", "z0", "z1")):
            count = 1 << number
            run = gathered.at[pl.ds((item // count) * count, count)]
            hops.append(other_copy(run, run, vec_out.at[number + 1], vec_in.at[number + 1], to))

        @pl.when(tick == 0)
        def _():
            first.start()

        @pl.when(tick == LAG)
        def _():
            first.wait()
            heights = lax.broadcasted_iota(jnp.int32, vector.shape, 0)
            gathered[item] = vector[...] + jnp.where(
                heights < vector.shape[0] - 8, got_vector[...], 0.0
            )
            hops[0].start()

        for number in range(4):

            @pl.when(tick == LAG * (number + 2))
            def _(number=number):
                hops[number].wait()
                if number < 3:
                    hops[number + 1].start()
                else:
                    gathered_out[...] = gathered[...]


ATTENTION_STEPS = 32
GIVES = 10
HOPS = {
    1: [
        ("d", "core", (8, 64, 256)),
        ("ay", "y", (4, 64, 256)),
        ("az", "z0", (2, 64, 256)),
        ("aw", "z1", (64, 256)),
        ("ax", "x", (64, 256)),
    ],
    2: [
        ("d", "core", (8, 64, 256)),
        ("ay", "y", (4, 64, 128)),
        ("az", "z0", (2, 64, 128)),
        ("aw", "z1", (64, 128)),
        ("ax", "x", (64, 128)),
        ("bx", "x", (8, 32, 128)),
        ("by", "y", (4, 32, 128)),
        ("bz", "z0", (2, 32, 128)),
        ("bw", "z1", (32, 128)),
        ("bg", "x", (32, 128)),
    ],
}


def sum_weights(weights, lefts, sides, vector=None, share=None, attention=None):
    tile = 256
    stages = 4 + sides
    low = lambda *shape: pltpu.VMEM(shape, jnp.bfloat16)
    full = lambda *shape: pltpu.VMEM(shape, jnp.float32)
    deep = [lefts[weight[0][0][0]].shape[1] // 1024 for weight in weights]
    units = sum(
        segment[0][1].shape[1] * depth // tile
        for weight, depth in zip(weights, deep)
        for segment in weight
    )
    inputs, outputs, scratch = [], [], []
    for left in lefts:
        spec = pl.BlockSpec(left.shape, lambda i: (0, 0), pipeline_mode=pl.Buffered(1))
        inputs.append(("lefts", left, spec))
        scratch.append(("turned", low(1 + left.shape[1] // 2048 // 2, 1024, left.shape[0])))
    seen, plan = set(), []
    at = flops = rights = 0
    for weight, depth in zip(weights, deep):
        terms, turns = [], []
        place = 0
        for segment in weight:
            across = segment[0][1].shape[1] // tile
            count = across * depth
            pairs = []
            for which, right in segment:
                if which not in seen:
                    seen.add(which)
                    turns += [(which, place + more) for more in range(0, count if depth > 1 else 1, 8)]
                pairs.append((which, rights))
                rights += 1
                flops += 2 * 1024 * depth * right.shape[0] * right.shape[1]
                spec = pl.BlockSpec(
                    (right.shape[0], tile),
                    lambda i, start=at + place, count=count, across=across: (
                        0,
                        lax.rem(jnp.clip(i - start, 0, count - 1), across),
                    ),
                )
                inputs.append(("rights", right, spec))
            terms.append((count, tuple(pairs)))
            place += count
        plan.append((place, tuple(terms), tuple(turns)))
        spec = pl.BlockSpec(
            (64, tile),
            lambda i, start=at, count=place, across=place // depth: (
                jnp.clip(i - LAG * stages - start, 0, count - 1) // across,
                lax.rem(jnp.clip(i - LAG * stages - start, 0, count - 1), across),
            ),
        )
        shape = (64 * depth, place // depth * tile)
        outputs.append(("outs", jax.ShapeDtypeStruct(shape, jnp.float32), spec))
        at += place
    hops = HOPS[sides]
    for _, _, shape in hops:
        scratch.append(("send", low(2, *shape)))
        scratch.append(("recv", low(4, *shape)))
        scratch.append(("keep", full(2, *shape)))
    scratch.append(("last", full(2, 64, 128)))
    scratch.append(("sems", pltpu.SemaphoreType.DMA((len(hops), 2))))
    scratch.append(("sems", pltpu.SemaphoreType.DMA((len(hops), 4))))
    transcendentals = 0
    if vector is not None:
        anywhere = pl.BlockSpec(memory_space=pl.ANY)
        inputs.append(("vector", vector, pl.BlockSpec(vector.shape, lambda i: (0, 0))))
        inputs.append(("give", share, anywhere))
        shape = (16,) + vector.shape
        outputs.append(("gathered", jax.ShapeDtypeStruct(shape, jnp.float32), pl.BlockSpec(shape, lambda i: (0, 0, 0))))
        outputs.append(("got", jax.ShapeDtypeStruct(share.shape, share.dtype), anywhere))
        scratch += [("gather", full(*shape)), ("gather", full(*vector.shape))]
        scratch += [("gather", pltpu.SemaphoreType.DMA((5,)))] * 2
        scratch += [("give_sems", pltpu.SemaphoreType.DMA((1,)))] * 2
    if attention is not None:
        lim, qkv, kv_rest, do, o, lse = attention
        count, width = do.shape
        pairs = width // 128
        place = lambda skip: pl.BlockSpec(
            (count, 128), lambda i: (0, jnp.minimum(i // 4, pairs - 1) + skip)
        )
        inputs.append(("attention", lim, pl.BlockSpec(memory_space=pltpu.SMEM)))
        for operand, skip in (
            (qkv, 0),
            (qkv, pairs),
            (qkv, 2 * pairs),
            (kv_rest, 0),
            (kv_rest, pairs),
            (do, 0),
            (o, 0),
            (lse, 0),
        ):
            inputs.append(("attention", operand, place(skip)))
        for _ in range(5):
            outputs.append(("grads", jax.ShapeDtypeStruct(do.shape, jnp.bfloat16), place(0)))
        scratch += [("held", low(count, 128)), ("held", low(count, 128)), ("held", full(count, 128))]
        flops += 40 * count * 2 * count * width
        transcendentals += count * 2 * count * width // 64
    groups = (
        ("lefts", "rights", "vector", "give", "attention"),
        ("outs", "gathered", "got", "grads"),
        ("turned", "send", "recv", "keep", "last", "sems", "gather", "give_sems", "held"),
    )
    layout, ordered = [], []
    for names, entries in zip(groups, (inputs, outputs, scratch)):
        found = [[entry[1:] for entry in entries if entry[0] == name] for name in names]
        layout += [(name, len(run)) for name, run in zip(names, found)]
        ordered.append([entry for run in found for entry in run])
    operands = [operand for operand, _ in ordered[0]]
    results = pl.pallas_call(
        functools.partial(sum_kernel, units, tuple(plan), tuple(layout), sides),
        grid=(units + LAG * stages,),
        in_specs=[spec for _, spec in ordered[0]],
        out_specs=[spec for _, spec in ordered[1]],
        out_shape=[shape for shape, _ in ordered[1]],
        scratch_shapes=[shape for shape, in ordered[2]],
        compiler_params=pltpu.CompilerParams(
            vmem_limit_bytes=58 << 20, collective_id=sides - 1, has_side_effects=True
        ),
        cost_estimate=pl.CostEstimate(
            flops=flops,
            transcendentals=transcendentals,
            bytes_accessed=sum(2 * operand.size for operand in operands),
        ),
    )(*operands)
    return results


def per_device(
    frames,
    cotangent,
    section,
    prompt_len,
    section_embed,
    ada_proj,
    ada_bias,
    w_qkv,
    w_out,
    w_up,
    w_down,
):
    _, row_count, width = frames.shape
    frames, cotangent = frames[0], cotangent[0]
    seq_size = lax.axis_size("seq")
    item_size = lax.axis_size("items")
    seq_me, item_me = lax.axis_index("seq"), lax.axis_index("items")
    side = jnp.bitwise_and(item_me, 1).astype(jnp.int32).reshape(1)
    turns = list(range(1, seq_size))
    fetch = lambda values, turn: lax.ppermute(
        values, "seq", [((i + turn) % seq_size, i) for i in range(seq_size)]
    )
    give = lambda values, turn: lax.ppermute(
        values, "seq", [(i, (i + turn) % seq_size) for i in range(seq_size)]
    )
    others = [fetch(frames, turn) for turn in turns]
    sources = jnp.stack([(seq_me + turn) % seq_size for turn in [0] + turns])
    limits = jnp.where(sources == 0, prompt_len[0], row_count).astype(jnp.int32)

    section_count = section_embed.shape[0]
    onehot = (section[:, None] == jnp.arange(section_count, dtype=jnp.int32)[None, :]).astype(
        jnp.float32
    )
    cond = jnp.dot(onehot, section_embed, precision=HIGHEST)
    modul = jnp.dot(cond, ada_proj.astype(jnp.float32), precision=HIGHEST) + ada_bias[None, :]
    scale_one, shift_one, scale_two, shift_two = jnp.split(modul, 4, axis=-1)
    inputs = frames.astype(jnp.float32)
    normed_one, inv_one = normalize(inputs)
    modulate = lambda normed: (normed * (1.0 + scale_one) + shift_one).astype(jnp.bfloat16)
    attn_in = modulate(normed_one)
    qkv = project(attn_in, w_qkv).astype(jnp.bfloat16)
    grad_act = back_project(cotangent, w_down).astype(jnp.bfloat16)
    others, qkv, grad_act = lax.optimization_barrier((others, qkv, grad_act))
    rest = jnp.concatenate(others) if len(others) > 1 else others[0]
    normed_rest, _ = normalize(rest.astype(jnp.float32))
    attn_rest = modulate(normed_rest)
    kv_rest = project(attn_rest, w_qkv[:, width:]).astype(jnp.bfloat16)
    att, lse = attend(limits, qkv, kv_rest, width)
    mid = inputs + project(att, w_out)
    normed_two, inv_two = normalize(mid)
    ffn_in = (normed_two * (1.0 + scale_two) + shift_two).astype(jnp.bfloat16)
    upper = project(ffn_in, w_up)
    act = gelu_exact(upper).astype(jnp.bfloat16)
    grad_upper = (grad_act.astype(jnp.float32) * gelu_slope(upper)).astype(jnp.bfloat16)
    out_frames = (mid + project(act, w_down)).astype(jnp.bfloat16)

    grad_out = cotangent.astype(jnp.float32)
    fused = seq_size == 2 and item_size == 16 and width == 1024
    grad_upper, out_frames = lax.optimization_barrier((grad_upper, out_frames))
    grad_ffn_in = lax.optimization_barrier(back_project(grad_upper, w_up))
    grad_scale_two = jnp.sum(grad_ffn_in * normed_two, 0)
    grad_shift_two = jnp.sum(grad_ffn_in, 0)
    grad_mid = grad_out + norm_back(grad_ffn_in * (1.0 + scale_two), normed_two, inv_two)
    grad_mid_low = grad_mid.astype(jnp.bfloat16)
    grad_att = back_project(grad_mid_low, w_out).astype(jnp.bfloat16)
    down_terms = [[(0, cotangent)]]
    if fused:
        sum_down, sum_up, sum_out, *grads = sum_weights(
            [down_terms, [[(1, grad_upper)]], [[(2, grad_mid_low)]]],
            [act, ffn_in, att],
            2,
            attention=(limits, qkv, kv_rest, grad_att, att, lse),
        )
        grad_query, grad_key, grad_value, key_rest, value_rest = grads
    else:
        grad_query, grad_key, grad_value, key_rest, value_rest = attend_back(
            limits, qkv, kv_rest, grad_att, att, lse
        )
    qkv_terms = [
        [(0, grad_query)],
        [(0, grad_key), (1, key_rest)],
        [(0, grad_value), (1, value_rest)],
    ]
    w_key, w_value = w_qkv[:, width : 2 * width], w_qkv[:, 2 * width :]
    share = back_project(key_rest, w_key) + back_project(value_rest, w_value)
    partial = (
        back_project(grad_query, w_qkv[:, :width])
        + back_project(grad_key, w_key)
        + back_project(grad_value, w_value)
    )
    partial, share = lax.optimization_barrier((partial, share))
    share_low = share.astype(jnp.bfloat16)
    grad_scale_one = jnp.sum(partial * normed_one, 0) + jnp.sum(share * normed_rest, 0)
    grad_shift_one = jnp.sum(partial, 0) + jnp.sum(share, 0)
    grad_modul = jnp.concatenate(
        [grad_scale_one, grad_shift_one, grad_scale_two, grad_shift_two]
    )[None, :]
    if fused:
        vector = jnp.concatenate(
            [
                grad_modul.reshape(4 * width // 128, 128),
                jnp.pad(onehot, ((0, 7), (0, 128 - section_count))),
            ]
        )
        sum_qkv, tagged, got_share = sum_weights(
            [qkv_terms], [attn_in, attn_rest], 1, vector=vector, share=share_low
        )
        grad_rest = [got_share]
        tagged = tagged[:, : 4 * width // 128 + 1].reshape(item_size, 4 * width + 128)
    else:
        grad_rest = [
            give(share_low[i * row_count : (i + 1) * row_count], turn)
            for i, turn in enumerate(turns)
        ]
        sum_down = finish(outer(side, [act], down_terms, item_size, 256), "items", "seq")
        sum_up = finish(outer(side, [ffn_in], [[(0, grad_upper)]], item_size, 512), "items", "seq")
        sum_out = finish(
            outer(side, [att], [[(0, grad_mid_low)]], item_size, 512), "items", "seq"
        )
        sum_qkv = finish(
            outer(side, [attn_in, attn_rest], qkv_terms, item_size, 512),
            "items",
            "seq",
        )
        for bit in bits_of("seq"):
            grad_modul = grad_modul + swap(grad_modul, "seq", bit)
        tagged = jnp.concatenate(
            [grad_modul, jnp.pad(onehot, ((0, 0), (0, 128 - section_count)))], -1
        )
        tagged = gather_items(tagged, "items")
    grad_attn_in = partial
    for got in grad_rest:
        grad_attn_in = grad_attn_in + got.astype(jnp.float32)
    frames_grad = (
        grad_mid + norm_back(grad_attn_in * (1.0 + scale_one), normed_one, inv_one)
    ).astype(jnp.bfloat16)

    modul_all, onehot_all = tagged[:, : 4 * width], tagged[:, 4 * width :][:, :section_count]
    block = width // item_size
    own_embed = lax.dynamic_slice_in_dim(section_embed, item_me * block, block, 1)
    own_cond = jnp.dot(onehot_all, own_embed, precision=HIGHEST)
    sum_ada = lax.dot_general(own_cond, modul_all, (((0,), (0,)), ((), ())), precision=HIGHEST)
    sum_bias = jnp.sum(
        lax.dynamic_slice_in_dim(modul_all, item_me * 4 * block, 4 * block, 1), 0
    )
    own_ada = lax.dynamic_slice_in_dim(ada_proj, item_me * block, block, 0).astype(jnp.float32)
    grad_cond = lax.dot_general(modul_all, own_ada, (((1,), (1,)), ((), ())), precision=HIGHEST)
    sum_embed = lax.dot_general(
        onehot_all, grad_cond, (((0,), (0,)), ((), ())), precision=HIGHEST
    )
    return (
        out_frames[None],
        frames_grad[None],
        sum_embed,
        sum_ada,
        sum_bias,
        sum_qkv,
        sum_out,
        sum_up,
        sum_down,
    )


def solution(mesh):
    in_specs = (
        P("items", "seq", None),
        P("items", "seq", None),
        P("items"),
        P("items"),
        P(),
        P(),
        P(),
        P(),
        P(),
        P(),
        P(),
    )
    out_specs = (
        P("items", "seq", None),
        P("items", "seq", None),
        P(None, "items"),
        P("items", None),
        P("items"),
        P("items", None),
        P("items", None),
        P("items", None),
        P("items", None),
    )
    return jax.shard_map(
        per_device, mesh=mesh, in_specs=in_specs, out_specs=out_specs, check_vma=False
    )
```

```python
import functools

import jax
import jax.numpy as jnp
from jax import lax
from jax.experimental import pallas as pl
from jax.experimental.pallas import tpu as pltpu
from jax.sharding import PartitionSpec as P

HEADS = 16


EPS = 1e-05
NEGATIVE = -1e30
SQRT_HALF = 0.7071067811865476
INV_SQRT_TAU = 0.3989422804014327
HIGHEST = lax.Precision.HIGHEST


def normalize(values):
    mean = jnp.mean(values, -1, keepdims=True)
    centered = values - mean
    inverse = lax.rsqrt(jnp.mean(centered * centered, -1, keepdims=True) + EPS)
    return (centered * inverse, inverse)


def norm_back(grad, normed, inverse):
    first = jnp.mean(grad, -1, keepdims=True)
    second = jnp.mean(grad * normed, -1, keepdims=True)
    return (grad - first - normed * second) * inverse


def gelu_exact(values):
    return 0.5 * values * (1.0 + lax.erf(values * SQRT_HALF))


def gelu_slope(values):
    return (
        0.5 * (1.0 + lax.erf(values * SQRT_HALF))
        + values * jnp.exp(-0.5 * values * values) * INV_SQRT_TAU
    )


def project(left, weight):
    flat = left.reshape(-1, left.shape[-1])
    result = jnp.dot(flat, weight, preferred_element_type=jnp.float32)
    return result.reshape(left.shape[:-1] + (weight.shape[1],))


def back_project(grad, weight):
    flat = grad.reshape(-1, grad.shape[-1])
    result = lax.dot_general(
        flat, weight, (((1,), (1,)), ((), ())), preferred_element_type=jnp.float32
    )
    return result.reshape(grad.shape[:-1] + (weight.shape[0],))


BIG = 1e30

def split3(x):
    hi = x.astype(jnp.bfloat16).astype(jnp.float32)
    rest = x - hi
    mid = rest.astype(jnp.bfloat16).astype(jnp.float32)
    return hi, mid, rest - mid

def dot(a, b, ca, cb):
    return lax.dot_general(a, b, (((ca,), (cb,)), ((), ())), preferred_element_type=jnp.float32)


def fwd_kernel(rows, blocks, lim_ref, q_ref, ko_ref, vo_ref, kt_ref, vt_ref, o_ref, lse_ref):
    lane = lax.broadcasted_iota(jnp.int32, (1, 128), 1)
    low = lane < 64
    row = lax.broadcasted_iota(jnp.int32, (rows, 1), 0)
    q = q_ref[...].astype(jnp.float32) * 0.125
    outs, lses = [], []
    for h in range(2):
        own = low if h == 0 else jnp.logical_not(low)
        first = 64 * (1 - h)
        qa = jnp.where(own, q, jnp.where(lane == first, 1.0, 0.0)).astype(jnp.bfloat16)
        scores, values = [], []
        for j in range(blocks):
            k = ko_ref[...] if j == 0 else kt_ref[pl.ds((j - 1) * rows, rows), :]
            v = vo_ref[...] if j == 0 else vt_ref[pl.ds((j - 1) * rows, rows), :]
            bias = jnp.where(row < lim_ref[j], 0.0, -BIG)
            ka = jnp.where(own, k.astype(jnp.float32), jnp.where(lane == first, bias, 0.0)).astype(jnp.bfloat16)
            va = jnp.where(own, v.astype(jnp.float32), 1.0).astype(jnp.bfloat16)
            scores.append(dot(qa, ka, 1, 1))
            values.append(va)
        top = functools.reduce(jnp.maximum, [jnp.max(s, -1, keepdims=True) for s in scores])
        total = None
        for s, va in zip(scores, values):
            p = jnp.exp(s - top).astype(jnp.bfloat16)
            part = dot(p, va, 1, 0)
            total = part if total is None else total + part
        outs.append(total / pltpu.roll(total, 64, 1))
        lses.append(top + jnp.log(total))
    o_ref[...] = jnp.where(low, outs[0], outs[1]).astype(o_ref.dtype)
    lse_ref[...] = jnp.where(low, lses[1], lses[0])


def bwd_kernel(rows, blocks, lim_ref, q_ref, ko_ref, vo_ref, kt_ref, vt_ref, do_ref, o_ref, lse_ref,
               dq_ref, dko_ref, dvo_ref, dkt_ref, dvt_ref):
    lane = lax.broadcasted_iota(jnp.int32, (1, 128), 1)
    low = lane < 64
    row = lax.broadcasted_iota(jnp.int32, (rows, 1), 0)
    q = q_ref[...].astype(jnp.float32) * 0.125
    qs = q.astype(jnp.bfloat16)
    do_low = do_ref[...]
    do = do_low.astype(jnp.float32)
    prod = do * o_ref[...].astype(jnp.float32)
    lh, lm, ll = split3(lse_ref[...])
    heads = []
    for h in range(2):
        own = low if h == 0 else jnp.logical_not(low)
        f = 64 * (1 - h)
        delta = jnp.sum(jnp.where(own, prod, 0.0), -1, keepdims=True)
        dh, dm, dl = split3(delta)
        qa = jnp.where(own, q, jnp.where(lane == f, 1.0, jnp.where(lane == f + 1, -lh, jnp.where(lane == f + 2, -lm, jnp.where(lane == f + 3, -ll, 0.0))))).astype(jnp.bfloat16)
        doa = jnp.where(own, do, jnp.where(lane == f, -dh, jnp.where(lane == f + 1, -dm, jnp.where(lane == f + 2, -dl, 0.0)))).astype(jnp.bfloat16)
        kone = jnp.where((lane > f) & (lane <= f + 3), 1.0, 0.0)
        vone = jnp.where((lane >= f) & (lane < f + 3), 1.0, 0.0)
        dq = None
        res = []
        for j in range(blocks):
            k = ko_ref[...] if j == 0 else kt_ref[pl.ds((j - 1) * rows, rows), :]
            v = vo_ref[...] if j == 0 else vt_ref[pl.ds((j - 1) * rows, rows), :]
            bias = jnp.where(row < lim_ref[j], 0.0, -BIG)
            ka = jnp.where(own, k.astype(jnp.float32), jnp.where(lane == f, bias, kone)).astype(jnp.bfloat16)
            va = jnp.where(own, v.astype(jnp.float32), vone).astype(jnp.bfloat16)
            pt = jnp.exp(dot(ka, qa, 1, 1))
            dpt = dot(va, doa, 1, 1)
            dst = (pt * dpt).astype(jnp.bfloat16)
            dv = dot(pt.astype(jnp.bfloat16), do_low, 1, 0)
            dk = dot(dst, qs, 1, 0)
            part = dot(dst, k, 0, 0)
            dq = part if dq is None else dq + part
            res.append((dk, dv))
        heads.append((dq, res))
    dq_ref[...] = (jnp.where(low, heads[0][0], heads[1][0]) * 0.125).astype(dq_ref.dtype)
    for j in range(blocks):
        dk = jnp.where(low, heads[0][1][j][0], heads[1][1][j][0]).astype(dko_ref.dtype)
        dv = jnp.where(low, heads[0][1][j][1], heads[1][1][j][1]).astype(dko_ref.dtype)
        if j == 0:
            dko_ref[...] = dk
            dvo_ref[...] = dv
        else:
            dkt_ref[pl.ds((j - 1) * rows, rows), :] = dk
            dvt_ref[pl.ds((j - 1) * rows, rows), :] = dv


def specs_of(rows, others, width):
    pairs = width // 128
    place = lambda count, skip: pl.BlockSpec((count, 128), lambda i, lim: (0, i + skip))
    inputs = [place(rows, 0), place(rows, pairs), place(rows, 2 * pairs), place(others, 0), place(others, pairs)]
    return inputs, place(rows, 0), place(others, 0)


def attend(lim, qkv, kv_rest, width):
    rows, others = qkv.shape[0], kv_rest.shape[0]
    blocks = 1 + others // rows
    inputs, own, oth = specs_of(rows, others, width)
    keys = rows + others
    return pl.pallas_call(
        functools.partial(fwd_kernel, rows, blocks),
        grid_spec=pltpu.PrefetchScalarGridSpec(num_scalar_prefetch=1, grid=(width // 128,),
            in_specs=inputs, out_specs=[own, own]),
        out_shape=[jax.ShapeDtypeStruct((rows, width), jnp.bfloat16), jax.ShapeDtypeStruct((rows, width), jnp.float32)],
        compiler_params=pltpu.CompilerParams(vmem_limit_bytes=56 << 20),
        cost_estimate=pl.CostEstimate(flops=16 * rows * keys * width, transcendentals=rows * keys * width // 64,
            bytes_accessed=2 * width * (2 * rows + 2 * keys) + 4 * rows * width),
    )(lim, qkv, qkv, qkv, kv_rest, kv_rest)


def attend_back(lim, qkv, kv_rest, do, o, lse):
    (rows, width), others = do.shape, kv_rest.shape[0]
    blocks = 1 + others // rows
    inputs, own, oth = specs_of(rows, others, width)
    keys = rows + others
    s = lambda n: jax.ShapeDtypeStruct((n, width), jnp.bfloat16)
    return pl.pallas_call(
        functools.partial(bwd_kernel, rows, blocks),
        grid_spec=pltpu.PrefetchScalarGridSpec(num_scalar_prefetch=1, grid=(width // 128,),
            in_specs=inputs + [own, own, own], out_specs=[own, own, own, oth, oth]),
        out_shape=[s(rows), s(rows), s(rows), s(others), s(others)],
        compiler_params=pltpu.CompilerParams(vmem_limit_bytes=56 << 20),
        cost_estimate=pl.CostEstimate(flops=40 * rows * keys * width, transcendentals=rows * keys * width // 64,
            bytes_accessed=2 * width * (4 * rows + 4 * keys) + 4 * rows * width),
    )(lim, qkv, qkv, qkv, kv_rest, kv_rest, do, o, lse)


def outer_kernel(plan, halves, first_tiles, side_ref, *refs):
    lefts, plan_rights, outs, turned = refs[: plan[0]], refs[plan[0] : plan[1]], refs[plan[1] : plan[1] + 4], refs[plan[1] + 4 :]
    step = pl.program_id(0)

    @pl.when(step == 0)
    def _():
        for left, flip in zip(lefts, turned):
            flip[...] = left[...].T

    at = 0
    place = 0
    for tiles, terms in plan[2]:
        rights = plan_rights[place : place + len(terms)]
        place += len(terms)

        @pl.when((step >= at) & (step < at + tiles))
        def _(rights=rights, terms=terms):
            total = None
            for which, right in zip(terms, rights):
                part = dot(turned[which][...], right[...], 1, 0)
                total = part if total is None else total + part
            rows, columns = total.shape
            split = total.astype(jnp.bfloat16).reshape(halves, 2, rows // (2 * halves), columns)
            even = side_ref[0] == 0
            keep = jnp.where(even, split[:, 0], split[:, 1])
            send = jnp.where(even, split[:, 1], split[:, 0])

            @pl.when(step < first_tiles)
            def _():
                outs[0][...] = send
                outs[1][...] = keep

            @pl.when(step >= first_tiles)
            def _():
                outs[2][...] = send
                outs[3][...] = keep

        at += tiles


def outer(side, lefts, segments, parts, tile):
    rows = lefts[0].shape[1]
    halves = parts // 2
    block = rows // parts
    width = sum(segment[0][1].shape[1] for segment in segments)
    steps = width // tile
    first_tiles = steps // 2
    in_specs = [pl.BlockSpec(left.shape, lambda i, s: (0, 0)) for left in lefts]
    operands = list(lefts)
    plan = []
    at = 0
    flops = 0
    for segment in segments:
        tiles = segment[0][1].shape[1] // tile
        for which, right in segment:
            in_specs.append(
                pl.BlockSpec(
                    (right.shape[0], tile),
                    lambda i, s, at=at, tiles=tiles: (0, jnp.clip(i - at, 0, tiles - 1)),
                )
            )
            operands.append(right)
            flops += 2 * rows * right.shape[0] * right.shape[1]
        plan.append((tiles, tuple(which for which, _ in segment)))
        at += tiles
    first = pl.BlockSpec((halves, block, tile), lambda i, s: (0, 0, jnp.minimum(i, first_tiles - 1)))
    second = pl.BlockSpec((halves, block, tile), lambda i, s: (0, 0, jnp.maximum(i - first_tiles, 0)))
    shape = lambda count: jax.ShapeDtypeStruct((halves, block, count * tile), jnp.bfloat16)
    moved = sum(2 * operand.size for operand in operands) + 2 * rows * width
    return pl.pallas_call(
        functools.partial(
            outer_kernel, (len(lefts), len(operands), tuple(plan)), halves, first_tiles
        ),
        grid_spec=pltpu.PrefetchScalarGridSpec(
            num_scalar_prefetch=1,
            grid=(steps,),
            in_specs=in_specs,
            out_specs=[first, first, second, second],
            scratch_shapes=[pltpu.VMEM(left.shape[::-1], jnp.bfloat16) for left in lefts],
        ),
        out_shape=[shape(first_tiles)] * 2 + [shape(steps - first_tiles)] * 2,
        compiler_params=pltpu.CompilerParams(vmem_limit_bytes=58 << 20),
        cost_estimate=pl.CostEstimate(flops=flops, transcendentals=0, bytes_accessed=moved),
    )(side, *operands)


def swap(values, axis, bit):
    size = lax.axis_size(axis)
    return lax.ppermute(values, axis, [(i, i ^ bit) for i in range(size)])


def bits_of(axis):
    size = lax.axis_size(axis)
    return [1 << place for place in range(size.bit_length() - 1)]


def add_low(left, right):
    return (left.astype(jnp.float32) + right.astype(jnp.float32)).astype(jnp.bfloat16)


def half_of(values, dim, which):
    return lax.dynamic_index_in_dim(values, which, dim, keepdims=False)


def reduce_rows(keep, got, axis):
    me = lax.axis_index(axis)
    for bit in bits_of(axis)[1:]:
        mine = jnp.bitwise_and(me // bit, 1)
        shape = keep.shape
        view = (shape[0] // 2, 2) + shape[1:]
        keep, got = keep.reshape(view), got.reshape(view)
        send = add_low(half_of(keep, 1, 1 - mine), half_of(got, 1, 1 - mine))
        keep = add_low(half_of(keep, 1, mine), half_of(got, 1, mine))
        got = swap(send, axis, bit)
    return keep, got


def finish(pieces, rows_axis, seq_axis):
    send_a, keep_a, send_b, keep_b = pieces
    got_a = swap(send_a, rows_axis, 1)
    got_b = swap(send_b, rows_axis, 1)
    keep_a, got_a = reduce_rows(keep_a, got_a, rows_axis)
    total_a = (keep_a.astype(jnp.float32) + got_a.astype(jnp.float32))[0]
    for bit in bits_of(seq_axis):
        low = total_a.astype(jnp.bfloat16)
        total_a = low.astype(jnp.float32) + swap(low, seq_axis, bit).astype(jnp.float32)
    me = lax.axis_index(seq_axis)
    for bit in bits_of(seq_axis):
        mine = jnp.bitwise_and(me // bit, 1)
        width = keep_b.shape[-1] // 2
        cut = lambda values, which: lax.dynamic_slice_in_dim(values, which * width, width, 2)
        send = add_low(cut(keep_b, 1 - mine), cut(got_b, 1 - mine))
        keep_b = add_low(cut(keep_b, mine), cut(got_b, mine))
        got_b = swap(send, seq_axis, bit)
    keep_b, got_b = reduce_rows(keep_b, got_b, rows_axis)
    total_b = add_low(keep_b, got_b)[0]
    for bit in reversed(bits_of(seq_axis)):
        mine = jnp.bitwise_and(me // bit, 1)
        other = swap(total_b, seq_axis, bit)
        total_b = jnp.where(
            mine == 0,
            jnp.concatenate([total_b, other], -1),
            jnp.concatenate([other, total_b], -1),
        )
    return jnp.concatenate([total_a, total_b.astype(jnp.float32)], -1)


def gather_items(values, axis):
    me = lax.axis_index(axis)
    for bit in bits_of(axis):
        other = swap(values, axis, bit)
        mine = jnp.bitwise_and(me // bit, 1)
        values = jnp.where(
            mine == 0, jnp.concatenate([values, other]), jnp.concatenate([other, values])
        )
    return values


LAG = 2
MESH = pl.DeviceIdType.MESH


def attention_step(step, lim_ref, q_ref, ko_ref, vo_ref, kt_ref, vt_ref, do_ref, o_ref, lse_ref,
                   grads, qa_ref, doa_ref, dq_sum):
    rows = q_ref.shape[0]
    j = step % 2
    lanes = pl.ds(pl.multiple_of((step // 2) * 128, 128), 128)
    lane = lax.broadcasted_iota(jnp.int32, (1, 128), 1)
    low = lane < 64
    wide = lambda ref: ref[...].astype(jnp.float32)

    @pl.when(j == 0)
    def _():
        q = wide(q_ref) * 0.125
        do = wide(do_ref)
        prod = do * wide(o_ref)
        lh, lm, ll = split3(lse_ref[...])
        for h in range(2):
            own = low if h == 0 else jnp.logical_not(low)
            f = 64 * (1 - h)
            delta = jnp.sum(jnp.where(own, prod, 0.0), -1, keepdims=True)
            dh, dm, dl = split3(delta)
            qa_ref[h] = jnp.where(own, q, jnp.where(lane == f, 1.0, jnp.where(lane == f + 1, -lh, jnp.where(lane == f + 2, -lm, jnp.where(lane == f + 3, -ll, 0.0))))).astype(jnp.bfloat16)
            doa_ref[h] = jnp.where(own, do, jnp.where(lane == f, -dh, jnp.where(lane == f + 1, -dm, jnp.where(lane == f + 2, -dl, 0.0)))).astype(jnp.bfloat16)

    row = lax.broadcasted_iota(jnp.int32, (rows, 1), 0)
    k = jnp.where(j == 0, wide(ko_ref), wide(kt_ref))
    v = jnp.where(j == 0, wide(vo_ref), wide(vt_ref))
    bias = jnp.where(row < lim_ref[j], 0.0, -BIG)
    heads = []
    for h in range(2):
        own = low if h == 0 else jnp.logical_not(low)
        f = 64 * (1 - h)
        kone = jnp.where((lane > f) & (lane <= f + 3), 1.0, 0.0)
        vone = jnp.where((lane >= f) & (lane < f + 3), 1.0, 0.0)
        ka = jnp.where(own, k, jnp.where(lane == f, bias, kone)).astype(jnp.bfloat16)
        va = jnp.where(own, v, vone).astype(jnp.bfloat16)
        qa, doa = qa_ref[h], doa_ref[h]
        pt = jnp.exp(dot(ka, qa, 1, 1))
        dpt = dot(va, doa, 1, 1)
        dst = (pt * dpt).astype(jnp.bfloat16)
        dv = dot(pt.astype(jnp.bfloat16), doa, 1, 0)
        dk = dot(dst, qa, 1, 0)
        heads.append((dot(dst, ka, 0, 0), dk, dv))
    part, dk, dv = (jnp.where(low, first, second) for first, second in zip(*heads))

    @pl.when(j == 0)
    def _():
        dq_sum[...] = part
        grads[1, :, lanes] = dk.astype(jnp.bfloat16)
        grads[2, :, lanes] = dv.astype(jnp.bfloat16)

    @pl.when(j == 1)
    def _():
        grads[0, :, lanes] = ((dq_sum[...] + part) * 0.125).astype(jnp.bfloat16)
        grads[3, :, lanes] = dk.astype(jnp.bfloat16)
        grads[4, :, lanes] = dv.astype(jnp.bfloat16)


def sum_kernel(units, plan, layout, sides, *refs):
    at = 0
    parts = {}
    for name, count in layout:
        parts[name] = refs[at : at + count]
        at += count
    lefts, rights, outs = (parts[name] for name in ("lefts", "rights", "outs"))
    turned, grads = parts["turned"][0], parts["held"][0]
    send, recv, keep = parts["send"], parts["recv"], parts["keep"]
    out_sem, in_sem = parts["sems"]
    stages = 4 + sides
    cut = 256 // sides
    tick = pl.program_id(0)
    item, seq = lax.axis_index("items"), lax.axis_index("seq")
    bit = lambda value, place: jnp.bitwise_and(value // (1 << place), 1)
    x = seq
    flip = lambda place: item + (1 - 2 * bit(item, place)) * (1 << place)
    partners = {
        "core": (flip(0), seq),
        "y": (flip(1), seq),
        "z0": (flip(2), seq),
        "z1": (flip(3), seq),
        "x": (item, 1 - seq),
    }

    @pl.when(tick == 0)
    def _():
        barrier = pltpu.get_barrier_semaphore()
        for partner in partners.values():
            pl.semaphore_signal(barrier, inc=1, device_id=partner, device_id_type=MESH)
        pl.semaphore_wait(barrier, len(partners))

    wide = lambda values: values.astype(jnp.float32)
    low = lambda values: values.astype(jnp.bfloat16)

    def choose(values, axis, which):
        first = lax.index_in_dim(values, 0, axis, keepdims=False)
        second = lax.index_in_dim(values, 1, axis, keepdims=False)
        mine = jnp.where(which == 0, first, second)
        other = jnp.where(which == 0, second, first)
        return mine, other

    table = {name: (i, to) for i, (name, to, _) in enumerate(HOPS[sides])}

    def copy(name, unit):
        number, to = table[name]
        slot, landing = unit % LAG, unit % (2 * LAG)
        return pltpu.make_async_remote_copy(
            src_ref=send[number].at[slot],
            dst_ref=recv[number].at[landing],
            send_sem=out_sem.at[number, slot],
            recv_sem=in_sem.at[number, landing],
            device_id=partners[to],
            device_id_type=MESH,
        )

    def post(name, unit, mine, other):
        number, _ = table[name]
        keep[number][unit % LAG] = mine
        send[number][unit % LAG] = low(other)
        copy(name, unit).start()

    def take(name, unit):
        number, _ = table[name]
        copy(name, unit).wait()
        return keep[number][unit % LAG] + wide(recv[number][unit % (2 * LAG)])

    def place_of(block):
        differs = [lax.rem(bit(block, place) + bit(item, place), 2) for place in range(4)]
        place = differs[0] * 8 + differs[1] * 4 + differs[2] * 2 + differs[3]
        return pl.ds(pl.multiple_of(place * 64, 64), 64)

    def turn(which, start):
        left = lefts[which]

        @pl.loop(0, 16 if left.shape[1] > 1024 else 8)
        def _(i):
            if left.shape[1] > 1024:
                block = left[:, pl.ds(pl.multiple_of(i * 256 + start * 128, 128), 128)].T
                turned[0, place_of(i)] = block[:64]
                turned[1, place_of(i)] = block[64:]
            else:
                block = left[:, pl.ds(pl.multiple_of(i * 128, 128), 128)].T
                turned[slot_of(which), place_of(2 * i)] = block[:64]
                turned[slot_of(which), place_of(2 * i + 1)] = block[64:]

    def stage_zero(unit):
        at = 0
        for count, terms, turns in plan:

            @pl.when((unit >= at) & (unit < at + count))
            def _(at=at, terms=terms, turns=turns):
                for which, start in turns:

                    @pl.when(unit == at + start)
                    def _(which=which, start=start):
                        turn(which, start // 8)

                place = 0
                for segment, pairs in terms:

                    @pl.when((unit >= at + place) & (unit < at + place + segment))
                    def _(pairs=pairs, place=place):
                        def product(run):
                            total = None
                            for which, right in pairs:
                                deep = lefts[which].shape[1] > 1024
                                half = ((unit - at) // 4) % 2 if deep else slot_of(which)
                                if right < HELD:
                                    values = rights[right][...]
                                else:
                                    local = unit - at - place
                                    column = pl.multiple_of((local % 4) * 256, 256)
                                    values = grads[right - HELD + local // 4, :, pl.ds(column, 256)]
                                part = dot(turned[half, run], values, 1, 0)
                                total = part if total is None else total + part
                            return total.reshape(8, 64, 256)

                        send[0][unit % LAG] = low(product(slice(512, 1024)))
                        copy("d", unit).start()
                        keep[0][unit % LAG] = product(slice(0, 512))

                    place += segment

            at += count

    def halves(values):
        count = values.shape[0] // 2
        return values[:count], values[count:]

    def stage_one(unit):
        total = take("d", unit)
        post("ay", unit, *halves(total[:, :, :cut]))
        if sides == 2:
            post("bx", unit, *choose(total[:, :, cut:].reshape(8, 2, 32, cut), 1, x))

    def stage_two(unit):
        post("az", unit, *halves(take("ay", unit)))
        if sides == 2:
            post("by", unit, *halves(take("bx", unit)))

    def stage_three(unit):
        total = take("az", unit)
        post("aw", unit, total[0], total[1])
        if sides == 2:
            post("bz", unit, *halves(take("by", unit)))

    def stage_four(unit):
        total = low(take("aw", unit))
        post("ax", unit, wide(total), total)
        if sides == 2:
            rest = take("bz", unit)
            post("bw", unit, rest[0], rest[1])

    def stage_five(unit):
        parts["last"][0][unit % LAG] = take("ax", unit)
        total = low(take("bw", unit))
        post("bg", unit, wide(total), total)

    def stage_final(unit):
        if sides == 1:
            block = take("ax", unit)
        else:
            number, _ = table["bg"]
            copy("bg", unit).wait()
            other = wide(recv[number][unit % (2 * LAG)])
            mine = keep[number][unit % LAG]
            top = jnp.where(x == 0, mine, other)
            bottom = jnp.where(x == 0, other, mine)
            block = jnp.concatenate(
                [parts["last"][0][unit % LAG], jnp.concatenate([top, bottom], 0)], 1
            )
        at = 0
        for (count, _, _), out in zip(plan, outs):

            @pl.when((unit >= at) & (unit < at + count))
            def _(out=out):
                out[...] = block

            at += count

    steps = [stage_zero, stage_one, stage_two, stage_three, stage_four, stage_five][:stages]
    steps.append(stage_final)
    for number in range(stages, -1, -1):
        unit = tick - LAG * number

        @pl.when((unit >= 0) & (unit < units))
        def _(number=number, unit=unit):
            steps[number](unit)

    @pl.when((tick < 2 * ATTENTION_STEPS) & (lax.rem(tick, 2) == 0))
    def _():
        attention_step(tick // 2, *parts["attention"], *parts["held"])

    vector, weight, normed, normed_rest = parts["project"]
    partial_out, got_ref, gathered_out, frames_out = parts["results"]
    gathered, got_vector, own_vector, give_ref = parts["gather"]
    vec_out, vec_in, give_out, give_in = parts["gather_sems"]

    @pl.when(tick == 0)
    def _():
        own_vector[...] = vector[...]

    @pl.when((tick >= SHARE) & (tick < SHARE + 8) & (lax.rem(tick, 2) == 0))
    def _():
        column = (tick - SHARE) // 2
        query, key, value = (weight[:, which * 1024 : (which + 1) * 1024] for which in range(3))
        share = dot(grads[3], key, 1, 1) + dot(grads[4], value, 1, 1)
        partial = dot(grads[0], query, 1, 1) + dot(grads[1], key, 1, 1) + dot(grads[2], value, 1, 1)
        give_ref[:, pl.ds(pl.multiple_of(column * 256, 256), 256)] = low(share)
        partial_out[...] = partial
        scale = jnp.sum(partial * normed[...] + share * normed_rest[...], 0, keepdims=True)
        shift = jnp.sum(partial + share, 0, keepdims=True)
        for part in range(2):
            lanes = slice(part * 128, (part + 1) * 128)
            own_vector[pl.ds(column * 2 + part, 1)] = scale[:, lanes]
            own_vector[pl.ds(8 + column * 2 + part, 1)] = shift[:, lanes]

    weight_down, mid = parts["dense"]

    @pl.when((tick >= DENSE) & (tick < DENSE + 16) & (lax.rem(tick, 4) == DENSE % 4))
    def _():
        half = mid.shape[0] // 2

        @pl.loop(0, 2)
        def _(i):
            run = pl.ds(pl.multiple_of(i * half, half), half)
            frames_out[run] = low(mid[run] + dot(lefts[0][run], weight_down[...], 1, 0))

    def other_copy(source, target, out, into, to):
        return pltpu.make_async_remote_copy(
            src_ref=source,
            dst_ref=target,
            send_sem=out,
            recv_sem=into,
            device_id=partners[to],
            device_id_type=MESH,
        )

    give_copy = lambda source, target: other_copy(
        source, target, give_out.at[0], give_in.at[0], "x"
    )
    chunk = give_ref.shape[0] // GIVES
    begin = SHARE + 8

    @pl.when((tick >= begin) & (tick < begin + GIVES))
    def _():
        run = pl.ds(pl.multiple_of((tick - begin) * chunk, chunk), chunk)
        give_copy(give_ref.at[run], got_ref.at[run]).start()

    @pl.when(tick == pl.num_programs(0) - 1)
    def _():
        give_copy(give_ref, got_ref).wait()

    first = other_copy(own_vector, got_vector, vec_out.at[0], vec_in.at[0], "x")
    hops = []
    for number, to in enumerate(("core", "y", "z0", "z1")):
        count = 1 << number
        run = gathered.at[pl.ds((item // count) * count, count)]
        hops.append(other_copy(run, run, vec_out.at[number + 1], vec_in.at[number + 1], to))

    @pl.when(tick == begin)
    def _():
        first.start()

    @pl.when(tick == begin + 2)
    def _():
        first.wait()
        heights = lax.broadcasted_iota(jnp.int32, vector.shape, 0)
        gathered[item] = own_vector[...] + jnp.where(
            heights < vector.shape[0] - 8, got_vector[...], 0.0
        )
        hops[0].start()

    for number in range(4):

        @pl.when(tick == begin + 2 * (number + 2))
        def _(number=number):
            hops[number].wait()
            if number < 3:
                hops[number + 1].start()
            else:
                gathered_out[...] = gathered[...]


ATTENTION_STEPS = 16
SHARE = 32
HELD = 100


def slot_of(which):
    return (which + 1) % 2


DENSE = 41
GIVES = 20
HOPS = {
    1: [
        ("d", "core", (8, 64, 256)),
        ("ay", "y", (4, 64, 256)),
        ("az", "z0", (2, 64, 256)),
        ("aw", "z1", (64, 256)),
        ("ax", "x", (64, 256)),
    ],
    2: [
        ("d", "core", (8, 64, 256)),
        ("ay", "y", (4, 64, 128)),
        ("az", "z0", (2, 64, 128)),
        ("aw", "z1", (64, 128)),
        ("ax", "x", (64, 128)),
        ("bx", "x", (8, 32, 128)),
        ("by", "y", (4, 32, 128)),
        ("bz", "z0", (2, 32, 128)),
        ("bw", "z1", (32, 128)),
        ("bg", "x", (32, 128)),
    ],
}


def sum_weights(weights, lefts, sides, attention, project, dense):
    tile = 256
    stages = 4 + sides
    low = lambda *shape: pltpu.VMEM(shape, jnp.bfloat16)
    full = lambda *shape: pltpu.VMEM(shape, jnp.float32)
    deep = [lefts[weight[0][0][0]].shape[1] // 1024 for weight in weights]
    wide_of = lambda right: 1024 * len(right) if isinstance(right, range) else right.shape[1]
    units = sum(
        wide_of(segment[0][1]) * depth // tile
        for weight, depth in zip(weights, deep)
        for segment in weight
    )
    inputs, outputs, scratch = [], [], []
    for left in lefts:
        spec = pl.BlockSpec(left.shape, lambda i: (0, 0), pipeline_mode=pl.Buffered(1))
        inputs.append(("lefts", left, spec))
    seen, plan = set(), []
    at = flops = rights = 0
    for weight, depth in zip(weights, deep):
        terms, turns = [], []
        place = 0
        for segment in weight:
            across = wide_of(segment[0][1]) // tile
            count = across * depth
            pairs = []
            for which, right in segment:
                if which not in seen:
                    seen.add(which)
                    turns += [(which, place + more) for more in range(0, count if depth > 1 else 1, 8)]
                flops += 2 * 1024 * depth * lefts[0].shape[0] * wide_of(right)
                if isinstance(right, range):
                    pairs.append((which, HELD + right.start))
                    continue
                pairs.append((which, rights))
                rights += 1
                spec = pl.BlockSpec(
                    (right.shape[0], tile),
                    lambda i, start=at + place, count=count, across=across: (
                        0,
                        lax.rem(jnp.clip(i - start, 0, count - 1), across),
                    ),
                )
                inputs.append(("rights", right, spec))
            terms.append((count, tuple(pairs)))
            place += count
        plan.append((place, tuple(terms), tuple(turns)))
        spec = pl.BlockSpec(
            (64, tile),
            lambda i, start=at, count=place, across=place // depth: (
                jnp.clip(i - LAG * stages - start, 0, count - 1) // across,
                lax.rem(jnp.clip(i - LAG * stages - start, 0, count - 1), across),
            ),
        )
        shape = (64 * depth, place // depth * tile)
        outputs.append(("outs", jax.ShapeDtypeStruct(shape, jnp.float32), spec))
        at += place
    hops = HOPS[sides]
    for _, _, shape in hops:
        scratch.append(("send", low(LAG, *shape)))
        scratch.append(("recv", low(2 * LAG, *shape)))
        scratch.append(("keep", full(LAG, *shape)))
    scratch.append(("last", full(LAG, 64, 128)))
    scratch.append(("sems", pltpu.SemaphoreType.DMA((len(hops), LAG))))
    scratch.append(("sems", pltpu.SemaphoreType.DMA((len(hops), 2 * LAG))))
    lim, qkv, kv_rest, do, o, lse = attention
    count, width = do.shape
    blocks = width // 128
    place = lambda skip: pl.BlockSpec(
        (count, 128), lambda i: (0, jnp.minimum(i // 4, blocks - 1) + skip)
    )
    inputs.append(("attention", lim, pl.BlockSpec(memory_space=pltpu.SMEM)))
    skips = (0, blocks, 2 * blocks, 0, blocks, 0, 0, 0)
    for operand, skip in zip((qkv, qkv, qkv, kv_rest, kv_rest, do, o, lse), skips):
        inputs.append(("attention", operand, place(skip)))
    scratch += [("turned", low(2, 1024, count)), ("held", low(5, count, width))]
    scratch += [("held", low(2, count, 128)), ("held", low(2, count, 128)), ("held", full(count, 128))]
    vector, w_qkv, normed, normed_rest = project
    share_of = lambda i: jnp.clip((i - SHARE) // 2, 0, 3)
    dense_of = lambda i: (0, jnp.clip((i - DENSE) // 4, 0, 3))
    column = pl.BlockSpec((count, tile), lambda i: (0, share_of(i)))
    inputs.append(("project", vector, pl.BlockSpec(vector.shape, lambda i: (0, 0))))
    inputs.append(("project", w_qkv, pl.BlockSpec((tile, w_qkv.shape[1]), lambda i: (share_of(i), 0))))
    inputs += [("project", normed, column), ("project", normed_rest, column)]
    for operand in dense:
        inputs.append(("dense", operand, pl.BlockSpec((operand.shape[0], tile), dense_of)))
    shape = (16,) + vector.shape
    result = lambda shape, dtype, spec: ("results", jax.ShapeDtypeStruct(shape, dtype), spec)
    outputs += [
        result(do.shape, jnp.float32, column),
        result(do.shape, jnp.bfloat16, pl.BlockSpec(memory_space=pl.ANY)),
        result(shape, jnp.float32, pl.BlockSpec(shape, lambda i: (0, 0, 0))),
        result(do.shape, jnp.bfloat16, pl.BlockSpec((count, tile), dense_of)),
    ]
    scratch += [("gather", full(*shape)), ("gather", full(*vector.shape)), ("gather", full(*vector.shape))]
    scratch.append(("gather", low(*do.shape)))
    scratch += [("gather_sems", pltpu.SemaphoreType.DMA((5,)))] * 2
    scratch += [("gather_sems", pltpu.SemaphoreType.DMA((1,)))] * 2
    flops += (80 * count + 14 * width) * count * width
    transcendentals = 2 * count * count * width // 64
    groups = (
        ("lefts", "rights", "attention", "project", "dense"),
        ("outs", "results"),
        ("turned", "held", "send", "recv", "keep", "last", "sems", "gather", "gather_sems"),
    )
    layout, ordered = [], []
    for names, entries in zip(groups, (inputs, outputs, scratch)):
        found = [[entry[1:] for entry in entries if entry[0] == name] for name in names]
        layout += [(name, len(run)) for name, run in zip(names, found)]
        ordered.append([entry for run in found for entry in run])
    operands = [operand for operand, _ in ordered[0]]
    results = pl.pallas_call(
        functools.partial(sum_kernel, units, tuple(plan), tuple(layout), sides),
        grid=(units + LAG * stages,),
        in_specs=[spec for _, spec in ordered[0]],
        out_specs=[spec for _, spec in ordered[1]],
        out_shape=[shape for shape, _ in ordered[1]],
        scratch_shapes=[shape for shape, in ordered[2]],
        compiler_params=pltpu.CompilerParams(
            vmem_limit_bytes=63 << 20, collective_id=sides - 1, has_side_effects=True
        ),
        cost_estimate=pl.CostEstimate(
            flops=flops,
            transcendentals=transcendentals,
            bytes_accessed=sum(2 * operand.size for operand in operands),
        ),
    )(*operands)
    return results


def per_device(
    frames,
    cotangent,
    section,
    prompt_len,
    section_embed,
    ada_proj,
    ada_bias,
    w_qkv,
    w_out,
    w_up,
    w_down,
):
    _, row_count, width = frames.shape
    frames, cotangent = frames[0], cotangent[0]
    seq_size = lax.axis_size("seq")
    item_size = lax.axis_size("items")
    seq_me, item_me = lax.axis_index("seq"), lax.axis_index("items")
    side = jnp.bitwise_and(item_me, 1).astype(jnp.int32).reshape(1)
    turns = list(range(1, seq_size))
    fetch = lambda values, turn: lax.ppermute(
        values, "seq", [((i + turn) % seq_size, i) for i in range(seq_size)]
    )
    give = lambda values, turn: lax.ppermute(
        values, "seq", [(i, (i + turn) % seq_size) for i in range(seq_size)]
    )
    others = [fetch(frames, turn) for turn in turns]
    sources = jnp.stack([(seq_me + turn) % seq_size for turn in [0] + turns])
    limits = jnp.where(sources == 0, prompt_len[0], row_count).astype(jnp.int32)

    section_count = section_embed.shape[0]
    onehot = (section[:, None] == jnp.arange(section_count, dtype=jnp.int32)[None, :]).astype(
        jnp.float32
    )
    cond = jnp.dot(onehot, section_embed, precision=HIGHEST)
    modul = jnp.dot(cond, ada_proj.astype(jnp.float32), precision=HIGHEST) + ada_bias[None, :]
    scale_one, shift_one, scale_two, shift_two = jnp.split(modul, 4, axis=-1)
    inputs = frames.astype(jnp.float32)
    normed_one, inv_one = normalize(inputs)
    modulate = lambda normed: (normed * (1.0 + scale_one) + shift_one).astype(jnp.bfloat16)
    attn_in = modulate(normed_one)
    qkv = project(attn_in, w_qkv).astype(jnp.bfloat16)
    grad_act = back_project(cotangent, w_down).astype(jnp.bfloat16)
    others, qkv, grad_act = lax.optimization_barrier((others, qkv, grad_act))
    rest = jnp.concatenate(others) if len(others) > 1 else others[0]
    normed_rest, _ = normalize(rest.astype(jnp.float32))
    attn_rest = modulate(normed_rest)
    kv_rest = project(attn_rest, w_qkv[:, width:]).astype(jnp.bfloat16)
    att, lse = attend(limits, qkv, kv_rest, width)
    mid = inputs + project(att, w_out)
    normed_two, inv_two = normalize(mid)
    ffn_in = (normed_two * (1.0 + scale_two) + shift_two).astype(jnp.bfloat16)
    upper = project(ffn_in, w_up)
    act = gelu_exact(upper).astype(jnp.bfloat16)
    grad_upper = (grad_act.astype(jnp.float32) * gelu_slope(upper)).astype(jnp.bfloat16)

    grad_out = cotangent.astype(jnp.float32)
    fused = seq_size == 2 and item_size == 16 and width == 1024
    grad_ffn_in = lax.optimization_barrier(back_project(grad_upper, w_up))
    grad_scale_two = jnp.sum(grad_ffn_in * normed_two, 0)
    grad_shift_two = jnp.sum(grad_ffn_in, 0)
    grad_mid = grad_out + norm_back(grad_ffn_in * (1.0 + scale_two), normed_two, inv_two)
    grad_mid_low = grad_mid.astype(jnp.bfloat16)
    grad_att = back_project(grad_mid_low, w_out).astype(jnp.bfloat16)
    if fused:
        vector = jnp.concatenate(
            [
                jnp.zeros((2 * width // 128, 128), jnp.float32),
                jnp.concatenate([grad_scale_two, grad_shift_two]).reshape(2 * width // 128, 128),
                jnp.pad(onehot, ((0, 7), (0, 128 - section_count))),
            ]
        )
        sum_down, sum_up, sum_out, sum_qkv, partial, got_share, tagged, out_frames = sum_weights(
            [
                [[(0, cotangent)]],
                [[(1, grad_upper)]],
                [[(2, grad_mid_low)]],
                [[(3, range(0, 1))], [(3, range(1, 3)), (4, range(3, 5))]],
            ],
            [act, ffn_in, att, attn_in, attn_rest],
            2,
            (limits, qkv, kv_rest, grad_att, att, lse),
            (vector, w_qkv, normed_one, normed_rest),
            (w_down, mid),
        )
        grad_rest = [got_share]
        tagged = tagged[:, : 4 * width // 128 + 1].reshape(item_size, 4 * width + 128)
    else:
        out_frames = (mid + project(act, w_down)).astype(jnp.bfloat16)
        grad_query, grad_key, grad_value, key_rest, value_rest = attend_back(
            limits, qkv, kv_rest, grad_att, att, lse
        )
        w_key, w_value = w_qkv[:, width : 2 * width], w_qkv[:, 2 * width :]
        share = back_project(key_rest, w_key) + back_project(value_rest, w_value)
        partial = (
            back_project(grad_query, w_qkv[:, :width])
            + back_project(grad_key, w_key)
            + back_project(grad_value, w_value)
        )
        share_low = share.astype(jnp.bfloat16)
        grad_rest = [
            give(share_low[i * row_count : (i + 1) * row_count], turn)
            for i, turn in enumerate(turns)
        ]
        grad_scale_one = jnp.sum(partial * normed_one, 0) + jnp.sum(share * normed_rest, 0)
        grad_shift_one = jnp.sum(partial, 0) + jnp.sum(share, 0)
        grad_modul = jnp.concatenate(
            [grad_scale_one, grad_shift_one, grad_scale_two, grad_shift_two]
        )[None, :]
        qkv_terms = [
            [(0, grad_query)],
            [(0, grad_key), (1, key_rest)],
            [(0, grad_value), (1, value_rest)],
        ]
        sums = lambda lefts, terms, tile: finish(
            outer(side, lefts, terms, item_size, tile), "items", "seq"
        )
        sum_down = sums([act], [[(0, cotangent)]], 256)
        sum_up = sums([ffn_in], [[(0, grad_upper)]], 512)
        sum_out = sums([att], [[(0, grad_mid_low)]], 512)
        sum_qkv = sums([attn_in, attn_rest], qkv_terms, 512)
        for bit in bits_of("seq"):
            grad_modul = grad_modul + swap(grad_modul, "seq", bit)
        tagged = jnp.concatenate(
            [grad_modul, jnp.pad(onehot, ((0, 0), (0, 128 - section_count)))], -1
        )
        tagged = gather_items(tagged, "items")
    grad_attn_in = partial
    for got in grad_rest:
        grad_attn_in = grad_attn_in + got.astype(jnp.float32)
    frames_grad = (
        grad_mid + norm_back(grad_attn_in * (1.0 + scale_one), normed_one, inv_one)
    ).astype(jnp.bfloat16)

    modul_all, onehot_all = tagged[:, : 4 * width], tagged[:, 4 * width :][:, :section_count]
    block = width // item_size
    own_embed = lax.dynamic_slice_in_dim(section_embed, item_me * block, block, 1)
    own_cond = jnp.dot(onehot_all, own_embed, precision=HIGHEST)
    sum_ada = lax.dot_general(own_cond, modul_all, (((0,), (0,)), ((), ())), precision=HIGHEST)
    sum_bias = jnp.sum(
        lax.dynamic_slice_in_dim(modul_all, item_me * 4 * block, 4 * block, 1), 0
    )
    own_ada = lax.dynamic_slice_in_dim(ada_proj, item_me * block, block, 0).astype(jnp.float32)
    grad_cond = lax.dot_general(modul_all, own_ada, (((1,), (1,)), ((), ())), precision=HIGHEST)
    sum_embed = lax.dot_general(
        onehot_all, grad_cond, (((0,), (0,)), ((), ())), precision=HIGHEST
    )
    return (
        out_frames[None],
        frames_grad[None],
        sum_embed,
        sum_ada,
        sum_bias,
        sum_qkv,
        sum_out,
        sum_up,
        sum_down,
    )


def solution(mesh):
    in_specs = (
        P("items", "seq", None),
        P("items", "seq", None),
        P("items"),
        P("items"),
        P(),
        P(),
        P(),
        P(),
        P(),
        P(),
        P(),
    )
    out_specs = (
        P("items", "seq", None),
        P("items", "seq", None),
        P(None, "items"),
        P("items", None),
        P("items"),
        P("items", None),
        P("items", None),
        P("items", None),
        P("items", None),
    )
    return jax.shard_map(
        per_device, mesh=mesh, in_specs=in_specs, out_specs=out_specs, check_vma=False
    )
```

```python
import functools

import jax
import jax.numpy as jnp
from jax import lax
from jax.experimental import pallas as pl
from jax.experimental.pallas import tpu as pltpu
from jax.sharding import PartitionSpec as P

HEADS = 16


EPS = 1e-05
NEGATIVE = -1e30
SQRT_HALF = 0.7071067811865476
INV_SQRT_TAU = 0.3989422804014327
HIGHEST = lax.Precision.HIGHEST


def normalize(values):
    mean = jnp.mean(values, -1, keepdims=True)
    centered = values - mean
    inverse = lax.rsqrt(jnp.mean(centered * centered, -1, keepdims=True) + EPS)
    return (centered * inverse, inverse)


def norm_back(grad, normed, inverse):
    first = jnp.mean(grad, -1, keepdims=True)
    second = jnp.mean(grad * normed, -1, keepdims=True)
    return (grad - first - normed * second) * inverse


def gelu_exact(values):
    return 0.5 * values * (1.0 + lax.erf(values * SQRT_HALF))


def gelu_slope(values):
    return (
        0.5 * (1.0 + lax.erf(values * SQRT_HALF))
        + values * jnp.exp(-0.5 * values * values) * INV_SQRT_TAU
    )


def project(left, weight):
    flat = left.reshape(-1, left.shape[-1])
    result = jnp.dot(flat, weight, preferred_element_type=jnp.float32)
    return result.reshape(left.shape[:-1] + (weight.shape[1],))


def back_project(grad, weight):
    flat = grad.reshape(-1, grad.shape[-1])
    result = lax.dot_general(
        flat, weight, (((1,), (1,)), ((), ())), preferred_element_type=jnp.float32
    )
    return result.reshape(grad.shape[:-1] + (weight.shape[0],))


BIG = 1e30

def split3(x):
    hi = x.astype(jnp.bfloat16).astype(jnp.float32)
    rest = x - hi
    mid = rest.astype(jnp.bfloat16).astype(jnp.float32)
    return hi, mid, rest - mid

def dot(a, b, ca, cb):
    return lax.dot_general(a, b, (((ca,), (cb,)), ((), ())), preferred_element_type=jnp.float32)


def fwd_kernel(rows, blocks, lim_ref, q_ref, ko_ref, vo_ref, kt_ref, vt_ref, o_ref, lse_ref):
    lane = lax.broadcasted_iota(jnp.int32, (1, 128), 1)
    low = lane < 64
    row = lax.broadcasted_iota(jnp.int32, (rows, 1), 0)
    q = q_ref[...].astype(jnp.float32) * 0.125
    outs, lses = [], []
    for h in range(2):
        own = low if h == 0 else jnp.logical_not(low)
        first = 64 * (1 - h)
        qa = jnp.where(own, q, jnp.where(lane == first, 1.0, 0.0)).astype(jnp.bfloat16)
        scores, values = [], []
        for j in range(blocks):
            k = ko_ref[...] if j == 0 else kt_ref[pl.ds((j - 1) * rows, rows), :]
            v = vo_ref[...] if j == 0 else vt_ref[pl.ds((j - 1) * rows, rows), :]
            bias = jnp.where(row < lim_ref[j], 0.0, -BIG)
            ka = jnp.where(own, k.astype(jnp.float32), jnp.where(lane == first, bias, 0.0)).astype(jnp.bfloat16)
            va = jnp.where(own, v.astype(jnp.float32), 1.0).astype(jnp.bfloat16)
            scores.append(dot(qa, ka, 1, 1))
            values.append(va)
        top = functools.reduce(jnp.maximum, [jnp.max(s, -1, keepdims=True) for s in scores])
        total = None
        for s, va in zip(scores, values):
            p = jnp.exp(s - top).astype(jnp.bfloat16)
            part = dot(p, va, 1, 0)
            total = part if total is None else total + part
        outs.append(total / pltpu.roll(total, 64, 1))
        lses.append(top + jnp.log(total))
    o_ref[...] = jnp.where(low, outs[0], outs[1]).astype(o_ref.dtype)
    lse_ref[...] = jnp.where(low, lses[1], lses[0])


def bwd_kernel(rows, blocks, lim_ref, q_ref, ko_ref, vo_ref, kt_ref, vt_ref, do_ref, o_ref, lse_ref,
               dq_ref, dko_ref, dvo_ref, dkt_ref, dvt_ref):
    lane = lax.broadcasted_iota(jnp.int32, (1, 128), 1)
    low = lane < 64
    row = lax.broadcasted_iota(jnp.int32, (rows, 1), 0)
    q = q_ref[...].astype(jnp.float32) * 0.125
    qs = q.astype(jnp.bfloat16)
    do_low = do_ref[...]
    do = do_low.astype(jnp.float32)
    prod = do * o_ref[...].astype(jnp.float32)
    lh, lm, ll = split3(lse_ref[...])
    heads = []
    for h in range(2):
        own = low if h == 0 else jnp.logical_not(low)
        f = 64 * (1 - h)
        delta = jnp.sum(jnp.where(own, prod, 0.0), -1, keepdims=True)
        dh, dm, dl = split3(delta)
        qa = jnp.where(own, q, jnp.where(lane == f, 1.0, jnp.where(lane == f + 1, -lh, jnp.where(lane == f + 2, -lm, jnp.where(lane == f + 3, -ll, 0.0))))).astype(jnp.bfloat16)
        doa = jnp.where(own, do, jnp.where(lane == f, -dh, jnp.where(lane == f + 1, -dm, jnp.where(lane == f + 2, -dl, 0.0)))).astype(jnp.bfloat16)
        kone = jnp.where((lane > f) & (lane <= f + 3), 1.0, 0.0)
        vone = jnp.where((lane >= f) & (lane < f + 3), 1.0, 0.0)
        dq = None
        res = []
        for j in range(blocks):
            k = ko_ref[...] if j == 0 else kt_ref[pl.ds((j - 1) * rows, rows), :]
            v = vo_ref[...] if j == 0 else vt_ref[pl.ds((j - 1) * rows, rows), :]
            bias = jnp.where(row < lim_ref[j], 0.0, -BIG)
            ka = jnp.where(own, k.astype(jnp.float32), jnp.where(lane == f, bias, kone)).astype(jnp.bfloat16)
            va = jnp.where(own, v.astype(jnp.float32), vone).astype(jnp.bfloat16)
            pt = jnp.exp(dot(ka, qa, 1, 1))
            dpt = dot(va, doa, 1, 1)
            dst = (pt * dpt).astype(jnp.bfloat16)
            dv = dot(pt.astype(jnp.bfloat16), do_low, 1, 0)
            dk = dot(dst, qs, 1, 0)
            part = dot(dst, k, 0, 0)
            dq = part if dq is None else dq + part
            res.append((dk, dv))
        heads.append((dq, res))
    dq_ref[...] = (jnp.where(low, heads[0][0], heads[1][0]) * 0.125).astype(dq_ref.dtype)
    for j in range(blocks):
        dk = jnp.where(low, heads[0][1][j][0], heads[1][1][j][0]).astype(dko_ref.dtype)
        dv = jnp.where(low, heads[0][1][j][1], heads[1][1][j][1]).astype(dko_ref.dtype)
        if j == 0:
            dko_ref[...] = dk
            dvo_ref[...] = dv
        else:
            dkt_ref[pl.ds((j - 1) * rows, rows), :] = dk
            dvt_ref[pl.ds((j - 1) * rows, rows), :] = dv


def specs_of(rows, others, width):
    pairs = width // 128
    place = lambda count, skip: pl.BlockSpec((count, 128), lambda i, lim: (0, i + skip))
    inputs = [place(rows, 0), place(rows, pairs), place(rows, 2 * pairs), place(others, 0), place(others, pairs)]
    return inputs, place(rows, 0), place(others, 0)


def attend(lim, qkv, kv_rest, width):
    rows, others = qkv.shape[0], kv_rest.shape[0]
    blocks = 1 + others // rows
    inputs, own, oth = specs_of(rows, others, width)
    keys = rows + others
    return pl.pallas_call(
        functools.partial(fwd_kernel, rows, blocks),
        grid_spec=pltpu.PrefetchScalarGridSpec(num_scalar_prefetch=1, grid=(width // 128,),
            in_specs=inputs, out_specs=[own, own]),
        out_shape=[jax.ShapeDtypeStruct((rows, width), jnp.bfloat16), jax.ShapeDtypeStruct((rows, width), jnp.float32)],
        compiler_params=pltpu.CompilerParams(vmem_limit_bytes=56 << 20),
        cost_estimate=pl.CostEstimate(flops=16 * rows * keys * width, transcendentals=rows * keys * width // 64,
            bytes_accessed=2 * width * (2 * rows + 2 * keys) + 4 * rows * width),
    )(lim, qkv, qkv, qkv, kv_rest, kv_rest)


def attend_back(lim, qkv, kv_rest, do, o, lse):
    (rows, width), others = do.shape, kv_rest.shape[0]
    blocks = 1 + others // rows
    inputs, own, oth = specs_of(rows, others, width)
    keys = rows + others
    s = lambda n: jax.ShapeDtypeStruct((n, width), jnp.bfloat16)
    return pl.pallas_call(
        functools.partial(bwd_kernel, rows, blocks),
        grid_spec=pltpu.PrefetchScalarGridSpec(num_scalar_prefetch=1, grid=(width // 128,),
            in_specs=inputs + [own, own, own], out_specs=[own, own, own, oth, oth]),
        out_shape=[s(rows), s(rows), s(rows), s(others), s(others)],
        compiler_params=pltpu.CompilerParams(vmem_limit_bytes=56 << 20),
        cost_estimate=pl.CostEstimate(flops=40 * rows * keys * width, transcendentals=rows * keys * width // 64,
            bytes_accessed=2 * width * (4 * rows + 4 * keys) + 4 * rows * width),
    )(lim, qkv, qkv, qkv, kv_rest, kv_rest, do, o, lse)


def outer_kernel(plan, halves, first_tiles, side_ref, *refs):
    lefts, plan_rights, outs, turned = refs[: plan[0]], refs[plan[0] : plan[1]], refs[plan[1] : plan[1] + 4], refs[plan[1] + 4 :]
    step = pl.program_id(0)

    @pl.when(step == 0)
    def _():
        for left, flip in zip(lefts, turned):
            flip[...] = left[...].T

    at = 0
    place = 0
    for tiles, terms in plan[2]:
        rights = plan_rights[place : place + len(terms)]
        place += len(terms)

        @pl.when((step >= at) & (step < at + tiles))
        def _(rights=rights, terms=terms):
            total = None
            for which, right in zip(terms, rights):
                part = dot(turned[which][...], right[...], 1, 0)
                total = part if total is None else total + part
            rows, columns = total.shape
            split = total.astype(jnp.bfloat16).reshape(halves, 2, rows // (2 * halves), columns)
            even = side_ref[0] == 0
            keep = jnp.where(even, split[:, 0], split[:, 1])
            send = jnp.where(even, split[:, 1], split[:, 0])

            @pl.when(step < first_tiles)
            def _():
                outs[0][...] = send
                outs[1][...] = keep

            @pl.when(step >= first_tiles)
            def _():
                outs[2][...] = send
                outs[3][...] = keep

        at += tiles


def outer(side, lefts, segments, parts, tile):
    rows = lefts[0].shape[1]
    halves = parts // 2
    block = rows // parts
    width = sum(segment[0][1].shape[1] for segment in segments)
    steps = width // tile
    first_tiles = steps // 2
    in_specs = [pl.BlockSpec(left.shape, lambda i, s: (0, 0)) for left in lefts]
    operands = list(lefts)
    plan = []
    at = 0
    flops = 0
    for segment in segments:
        tiles = segment[0][1].shape[1] // tile
        for which, right in segment:
            in_specs.append(
                pl.BlockSpec(
                    (right.shape[0], tile),
                    lambda i, s, at=at, tiles=tiles: (0, jnp.clip(i - at, 0, tiles - 1)),
                )
            )
            operands.append(right)
            flops += 2 * rows * right.shape[0] * right.shape[1]
        plan.append((tiles, tuple(which for which, _ in segment)))
        at += tiles
    first = pl.BlockSpec((halves, block, tile), lambda i, s: (0, 0, jnp.minimum(i, first_tiles - 1)))
    second = pl.BlockSpec((halves, block, tile), lambda i, s: (0, 0, jnp.maximum(i - first_tiles, 0)))
    shape = lambda count: jax.ShapeDtypeStruct((halves, block, count * tile), jnp.bfloat16)
    moved = sum(2 * operand.size for operand in operands) + 2 * rows * width
    return pl.pallas_call(
        functools.partial(
            outer_kernel, (len(lefts), len(operands), tuple(plan)), halves, first_tiles
        ),
        grid_spec=pltpu.PrefetchScalarGridSpec(
            num_scalar_prefetch=1,
            grid=(steps,),
            in_specs=in_specs,
            out_specs=[first, first, second, second],
            scratch_shapes=[pltpu.VMEM(left.shape[::-1], jnp.bfloat16) for left in lefts],
        ),
        out_shape=[shape(first_tiles)] * 2 + [shape(steps - first_tiles)] * 2,
        compiler_params=pltpu.CompilerParams(vmem_limit_bytes=58 << 20),
        cost_estimate=pl.CostEstimate(flops=flops, transcendentals=0, bytes_accessed=moved),
    )(side, *operands)


def swap(values, axis, bit):
    size = lax.axis_size(axis)
    return lax.ppermute(values, axis, [(i, i ^ bit) for i in range(size)])


def bits_of(axis):
    size = lax.axis_size(axis)
    return [1 << place for place in range(size.bit_length() - 1)]


def add_low(left, right):
    return (left.astype(jnp.float32) + right.astype(jnp.float32)).astype(jnp.bfloat16)


def half_of(values, dim, which):
    return lax.dynamic_index_in_dim(values, which, dim, keepdims=False)


def reduce_rows(keep, got, axis):
    me = lax.axis_index(axis)
    for bit in bits_of(axis)[1:]:
        mine = jnp.bitwise_and(me // bit, 1)
        shape = keep.shape
        view = (shape[0] // 2, 2) + shape[1:]
        keep, got = keep.reshape(view), got.reshape(view)
        send = add_low(half_of(keep, 1, 1 - mine), half_of(got, 1, 1 - mine))
        keep = add_low(half_of(keep, 1, mine), half_of(got, 1, mine))
        got = swap(send, axis, bit)
    return keep, got


def finish(pieces, rows_axis, seq_axis):
    send_a, keep_a, send_b, keep_b = pieces
    got_a = swap(send_a, rows_axis, 1)
    got_b = swap(send_b, rows_axis, 1)
    keep_a, got_a = reduce_rows(keep_a, got_a, rows_axis)
    total_a = (keep_a.astype(jnp.float32) + got_a.astype(jnp.float32))[0]
    for bit in bits_of(seq_axis):
        low = total_a.astype(jnp.bfloat16)
        total_a = low.astype(jnp.float32) + swap(low, seq_axis, bit).astype(jnp.float32)
    me = lax.axis_index(seq_axis)
    for bit in bits_of(seq_axis):
        mine = jnp.bitwise_and(me // bit, 1)
        width = keep_b.shape[-1] // 2
        cut = lambda values, which: lax.dynamic_slice_in_dim(values, which * width, width, 2)
        send = add_low(cut(keep_b, 1 - mine), cut(got_b, 1 - mine))
        keep_b = add_low(cut(keep_b, mine), cut(got_b, mine))
        got_b = swap(send, seq_axis, bit)
    keep_b, got_b = reduce_rows(keep_b, got_b, rows_axis)
    total_b = add_low(keep_b, got_b)[0]
    for bit in reversed(bits_of(seq_axis)):
        mine = jnp.bitwise_and(me // bit, 1)
        other = swap(total_b, seq_axis, bit)
        total_b = jnp.where(
            mine == 0,
            jnp.concatenate([total_b, other], -1),
            jnp.concatenate([other, total_b], -1),
        )
    return jnp.concatenate([total_a, total_b.astype(jnp.float32)], -1)


def gather_items(values, axis):
    me = lax.axis_index(axis)
    for bit in bits_of(axis):
        other = swap(values, axis, bit)
        mine = jnp.bitwise_and(me // bit, 1)
        values = jnp.where(
            mine == 0, jnp.concatenate([values, other]), jnp.concatenate([other, values])
        )
    return values


LAG = 2
MESH = pl.DeviceIdType.MESH


def attention_step(step, lim_ref, q_ref, ko_ref, vo_ref, kt_ref, vt_ref, do_ref, o_ref, lse_ref,
                   grads, qa_ref, doa_ref, dq_sum):
    rows = q_ref.shape[0]
    j = step % 2
    lanes = pl.ds(pl.multiple_of((step // 2) * 128, 128), 128)
    lane = lax.broadcasted_iota(jnp.int32, (1, 128), 1)
    low = lane < 64
    wide = lambda ref: ref[...].astype(jnp.float32)

    @pl.when(j == 0)
    def _():
        q = wide(q_ref) * 0.125
        do = wide(do_ref)
        prod = do * wide(o_ref)
        lh, lm, ll = split3(lse_ref[...])
        for h in range(2):
            own = low if h == 0 else jnp.logical_not(low)
            f = 64 * (1 - h)
            delta = jnp.sum(jnp.where(own, prod, 0.0), -1, keepdims=True)
            dh, dm, dl = split3(delta)
            qa_ref[h] = jnp.where(own, q, jnp.where(lane == f, 1.0, jnp.where(lane == f + 1, -lh, jnp.where(lane == f + 2, -lm, jnp.where(lane == f + 3, -ll, 0.0))))).astype(jnp.bfloat16)
            doa_ref[h] = jnp.where(own, do, jnp.where(lane == f, -dh, jnp.where(lane == f + 1, -dm, jnp.where(lane == f + 2, -dl, 0.0)))).astype(jnp.bfloat16)

    row = lax.broadcasted_iota(jnp.int32, (rows, 1), 0)
    k = jnp.where(j == 0, wide(ko_ref), wide(kt_ref))
    v = jnp.where(j == 0, wide(vo_ref), wide(vt_ref))
    bias = jnp.where(row < lim_ref[j], 0.0, -BIG)
    heads = []
    for h in range(2):
        own = low if h == 0 else jnp.logical_not(low)
        f = 64 * (1 - h)
        kone = jnp.where((lane > f) & (lane <= f + 3), 1.0, 0.0)
        vone = jnp.where((lane >= f) & (lane < f + 3), 1.0, 0.0)
        ka = jnp.where(own, k, jnp.where(lane == f, bias, kone)).astype(jnp.bfloat16)
        va = jnp.where(own, v, vone).astype(jnp.bfloat16)
        qa, doa = qa_ref[h], doa_ref[h]
        pt = jnp.exp(dot(ka, qa, 1, 1))
        dpt = dot(va, doa, 1, 1)
        dst = (pt * dpt).astype(jnp.bfloat16)
        dv = dot(pt.astype(jnp.bfloat16), doa, 1, 0)
        dk = dot(dst, qa, 1, 0)
        heads.append((dot(dst, ka, 0, 0), dk, dv))
    part, dk, dv = (jnp.where(low, first, second) for first, second in zip(*heads))

    @pl.when(j == 0)
    def _():
        dq_sum[...] = part
        grads[1, :, lanes] = dk.astype(jnp.bfloat16)
        grads[2, :, lanes] = dv.astype(jnp.bfloat16)

    @pl.when(j == 1)
    def _():
        grads[0, :, lanes] = ((dq_sum[...] + part) * 0.125).astype(jnp.bfloat16)
        grads[3, :, lanes] = dk.astype(jnp.bfloat16)
        grads[4, :, lanes] = dv.astype(jnp.bfloat16)


def sum_kernel(units, plan, layout, sides, *refs):
    at = 0
    parts = {}
    for name, count in layout:
        parts[name] = refs[at : at + count]
        at += count
    lefts, rights, outs = (parts[name] for name in ("lefts", "rights", "outs"))
    turned, grads = parts["turned"][0], parts["held"][0]
    send, recv, keep = parts["send"], parts["recv"], parts["keep"]
    out_sem, in_sem = parts["sems"]
    stages = 4 + sides
    cut = 256 // sides
    tick = pl.program_id(0)
    item, seq = lax.axis_index("items"), lax.axis_index("seq")
    bit = lambda value, place: jnp.bitwise_and(value // (1 << place), 1)
    x = seq
    flip = lambda place: item + (1 - 2 * bit(item, place)) * (1 << place)
    partners = {
        "core": (flip(0), seq),
        "y": (flip(1), seq),
        "z0": (flip(2), seq),
        "z1": (flip(3), seq),
        "x": (item, 1 - seq),
    }

    @pl.when(tick == 0)
    def _():
        barrier = pltpu.get_barrier_semaphore()
        for partner in partners.values():
            pl.semaphore_signal(barrier, inc=1, device_id=partner, device_id_type=MESH)
        pl.semaphore_wait(barrier, len(partners))

    wide = lambda values: values.astype(jnp.float32)
    low = lambda values: values.astype(jnp.bfloat16)

    def choose(values, axis, which):
        first = lax.index_in_dim(values, 0, axis, keepdims=False)
        second = lax.index_in_dim(values, 1, axis, keepdims=False)
        mine = jnp.where(which == 0, first, second)
        other = jnp.where(which == 0, second, first)
        return mine, other

    table = {name: (i, to) for i, (name, to, _) in enumerate(HOPS[sides])}

    def copy(name, unit):
        number, to = table[name]
        slot, landing = unit % LAG, unit % (2 * LAG)
        return pltpu.make_async_remote_copy(
            src_ref=send[number].at[slot],
            dst_ref=recv[number].at[landing],
            send_sem=out_sem.at[number, slot],
            recv_sem=in_sem.at[number, landing],
            device_id=partners[to],
            device_id_type=MESH,
        )

    def post(name, unit, mine, other):
        number, _ = table[name]
        keep[number][unit % LAG] = mine
        send[number][unit % LAG] = low(other)
        copy(name, unit).start()

    def take(name, unit):
        number, _ = table[name]
        copy(name, unit).wait()
        return keep[number][unit % LAG] + wide(recv[number][unit % (2 * LAG)])

    def place_of(block):
        differs = [lax.rem(bit(block, place) + bit(item, place), 2) for place in range(4)]
        place = differs[0] * 8 + differs[1] * 4 + differs[2] * 2 + differs[3]
        return pl.ds(pl.multiple_of(place * 64, 64), 64)

    def turn(which, start):
        left = lefts[which]

        @pl.loop(0, 16 if left.shape[1] > 1024 else 8)
        def _(i):
            if left.shape[1] > 1024:
                block = left[:, pl.ds(pl.multiple_of(i * 256 + start * 128, 128), 128)].T
                turned[0, place_of(i)] = block[:64]
                turned[1, place_of(i)] = block[64:]
            else:
                block = left[:, pl.ds(pl.multiple_of(i * 128, 128), 128)].T
                turned[slot_of(which), place_of(2 * i)] = block[:64]
                turned[slot_of(which), place_of(2 * i + 1)] = block[64:]

    def stage_zero(unit):
        at = 0
        for count, terms, turns in plan:

            @pl.when((unit >= at) & (unit < at + count))
            def _(at=at, terms=terms, turns=turns):
                for which, start in turns:

                    @pl.when(unit == at + start)
                    def _(which=which, start=start):
                        turn(which, start // 8)

                place = 0
                for segment, pairs in terms:

                    @pl.when((unit >= at + place) & (unit < at + place + segment))
                    def _(pairs=pairs, place=place):
                        def product(run):
                            total = None
                            for which, right in pairs:
                                deep = lefts[which].shape[1] > 1024
                                half = ((unit - at) // 4) % 2 if deep else slot_of(which)
                                if right < HELD:
                                    values = rights[right][...]
                                else:
                                    local = unit - at - place
                                    column = pl.multiple_of((local % 4) * 256, 256)
                                    values = grads[right - HELD + local // 4, :, pl.ds(column, 256)]
                                part = dot(turned[half, run], values, 1, 0)
                                total = part if total is None else total + part
                            return total.reshape(8, 64, 256)

                        send[0][unit % LAG] = low(product(slice(512, 1024)))
                        copy("d", unit).start()
                        keep[0][unit % LAG] = product(slice(0, 512))

                    place += segment

            at += count

    def halves(values):
        count = values.shape[0] // 2
        return values[:count], values[count:]

    def stage_one(unit):
        total = take("d", unit)
        post("ay", unit, *halves(total[:, :, :cut]))
        if sides == 2:
            post("bx", unit, *choose(total[:, :, cut:].reshape(8, 2, 32, cut), 1, x))

    def stage_two(unit):
        post("az", unit, *halves(take("ay", unit)))
        if sides == 2:
            post("by", unit, *halves(take("bx", unit)))

    def stage_three(unit):
        total = take("az", unit)
        post("aw", unit, total[0], total[1])
        if sides == 2:
            post("bz", unit, *halves(take("by", unit)))

    def stage_four(unit):
        total = low(take("aw", unit))
        post("ax", unit, wide(total), total)
        if sides == 2:
            rest = take("bz", unit)
            post("bw", unit, rest[0], rest[1])

    def stage_five(unit):
        parts["last"][0][unit % LAG] = take("ax", unit)
        total = low(take("bw", unit))
        post("bg", unit, wide(total), total)

    def stage_final(unit):
        if sides == 1:
            block = take("ax", unit)
        else:
            number, _ = table["bg"]
            copy("bg", unit).wait()
            other = wide(recv[number][unit % (2 * LAG)])
            mine = keep[number][unit % LAG]
            top = jnp.where(x == 0, mine, other)
            bottom = jnp.where(x == 0, other, mine)
            block = jnp.concatenate(
                [parts["last"][0][unit % LAG], jnp.concatenate([top, bottom], 0)], 1
            )
        at = 0
        for (count, _, _), out in zip(plan, outs):

            @pl.when((unit >= at) & (unit < at + count))
            def _(out=out):
                out[...] = block

            at += count

    steps = [stage_zero, stage_one, stage_two, stage_three, stage_four, stage_five][:stages]
    steps.append(stage_final)
    for number in range(stages, -1, -1):
        unit = tick - LAG * number

        @pl.when((unit >= 0) & (unit < units))
        def _(number=number, unit=unit):
            steps[number](unit)

    @pl.when((tick < 2 * ATTENTION_STEPS) & (lax.rem(tick, 2) == 0))
    def _():
        attention_step(tick // 2, *parts["attention"], *parts["held"])

    vector, weight, normed, normed_rest = parts["project"]
    partial_out, got_ref, gathered_out, frames_out = parts["results"]
    gathered, got_vector, own_vector, give_ref = parts["gather"]
    vec_out, vec_in, give_out, give_in = parts["gather_sems"]

    @pl.when(tick == 0)
    def _():
        own_vector[...] = vector[...]

    @pl.when((tick >= SHARE) & (tick < SHARE + 4))
    def _():
        column = tick - SHARE
        query, key, value = (weight[:, which * 1024 : (which + 1) * 1024] for which in range(3))
        share = dot(grads[3], key, 1, 1) + dot(grads[4], value, 1, 1)
        partial = dot(grads[0], query, 1, 1) + dot(grads[1], key, 1, 1) + dot(grads[2], value, 1, 1)
        give_ref[:, pl.ds(pl.multiple_of(column * 256, 256), 256)] = low(share)
        partial_out[...] = partial
        scale = jnp.sum(partial * normed[...] + share * normed_rest[...], 0, keepdims=True)
        shift = jnp.sum(partial + share, 0, keepdims=True)
        for part in range(2):
            lanes = slice(part * 128, (part + 1) * 128)
            own_vector[pl.ds(column * 2 + part, 1)] = scale[:, lanes]
            own_vector[pl.ds(8 + column * 2 + part, 1)] = shift[:, lanes]

    weight_down, mid = parts["dense"]

    @pl.when((tick >= DENSE) & (tick < DENSE + 16) & (lax.rem(tick, 4) == DENSE % 4))
    def _():
        half = mid.shape[0] // 2

        @pl.loop(0, 2)
        def _(i):
            run = pl.ds(pl.multiple_of(i * half, half), half)
            frames_out[run] = low(mid[run] + dot(lefts[0][run], weight_down[...], 1, 0))

    def other_copy(source, target, out, into, to):
        return pltpu.make_async_remote_copy(
            src_ref=source,
            dst_ref=target,
            send_sem=out,
            recv_sem=into,
            device_id=partners[to],
            device_id_type=MESH,
        )

    give_copy = lambda source, target: other_copy(
        source, target, give_out.at[0], give_in.at[0], "x"
    )
    chunk = give_ref.shape[0] // GIVES
    begin = SHARE + 4

    @pl.when((tick >= begin) & (tick < begin + GIVES))
    def _():
        run = pl.ds(pl.multiple_of((tick - begin) * chunk, chunk), chunk)
        give_copy(give_ref.at[run], got_ref.at[run]).start()

    @pl.when(tick == pl.num_programs(0) - 1)
    def _():
        give_copy(give_ref, got_ref).wait()

    first = other_copy(own_vector, got_vector, vec_out.at[0], vec_in.at[0], "x")
    hops = []
    for number, to in enumerate(("core", "y", "z0", "z1")):
        count = 1 << number
        run = gathered.at[pl.ds((item // count) * count, count)]
        hops.append(other_copy(run, run, vec_out.at[number + 1], vec_in.at[number + 1], to))

    @pl.when(tick == begin)
    def _():
        first.start()

    @pl.when(tick == begin + 2)
    def _():
        first.wait()
        heights = lax.broadcasted_iota(jnp.int32, vector.shape, 0)
        gathered[item] = own_vector[...] + jnp.where(
            heights < vector.shape[0] - 8, got_vector[...], 0.0
        )
        hops[0].start()

    for number in range(4):

        @pl.when(tick == begin + 2 * (number + 2))
        def _(number=number):
            hops[number].wait()
            if number < 3:
                hops[number + 1].start()
            else:
                gathered_out[...] = gathered[...]


ATTENTION_STEPS = 16
SHARE = 32
HELD = 100


def slot_of(which):
    return (which + 1) % 2


DENSE = 41
GIVES = 20
HOPS = {
    1: [
        ("d", "core", (8, 64, 256)),
        ("ay", "y", (4, 64, 256)),
        ("az", "z0", (2, 64, 256)),
        ("aw", "z1", (64, 256)),
        ("ax", "x", (64, 256)),
    ],
    2: [
        ("d", "core", (8, 64, 256)),
        ("ay", "y", (4, 64, 128)),
        ("az", "z0", (2, 64, 128)),
        ("aw", "z1", (64, 128)),
        ("ax", "x", (64, 128)),
        ("bx", "x", (8, 32, 128)),
        ("by", "y", (4, 32, 128)),
        ("bz", "z0", (2, 32, 128)),
        ("bw", "z1", (32, 128)),
        ("bg", "x", (32, 128)),
    ],
}


def sum_weights(weights, lefts, sides, attention, project, dense):
    tile = 256
    stages = 4 + sides
    low = lambda *shape: pltpu.VMEM(shape, jnp.bfloat16)
    full = lambda *shape: pltpu.VMEM(shape, jnp.float32)
    deep = [lefts[weight[0][0][0]].shape[1] // 1024 for weight in weights]
    wide_of = lambda right: 1024 * len(right) if isinstance(right, range) else right.shape[1]
    units = sum(
        wide_of(segment[0][1]) * depth // tile
        for weight, depth in zip(weights, deep)
        for segment in weight
    )
    inputs, outputs, scratch = [], [], []
    for left in lefts:
        spec = pl.BlockSpec(left.shape, lambda i: (0, 0), pipeline_mode=pl.Buffered(1))
        inputs.append(("lefts", left, spec))
    seen, plan = set(), []
    at = flops = rights = 0
    for weight, depth in zip(weights, deep):
        terms, turns = [], []
        place = 0
        for segment in weight:
            across = wide_of(segment[0][1]) // tile
            count = across * depth
            pairs = []
            for which, right in segment:
                if which not in seen:
                    seen.add(which)
                    turns += [(which, place + more) for more in range(0, count if depth > 1 else 1, 8)]
                flops += 2 * 1024 * depth * lefts[0].shape[0] * wide_of(right)
                if isinstance(right, range):
                    pairs.append((which, HELD + right.start))
                    continue
                pairs.append((which, rights))
                rights += 1
                spec = pl.BlockSpec(
                    (right.shape[0], tile),
                    lambda i, start=at + place, count=count, across=across: (
                        0,
                        lax.rem(jnp.clip(i - start, 0, count - 1), across),
                    ),
                )
                inputs.append(("rights", right, spec))
            terms.append((count, tuple(pairs)))
            place += count
        plan.append((place, tuple(terms), tuple(turns)))
        spec = pl.BlockSpec(
            (64, tile),
            lambda i, start=at, count=place, across=place // depth: (
                jnp.clip(i - LAG * stages - start, 0, count - 1) // across,
                lax.rem(jnp.clip(i - LAG * stages - start, 0, count - 1), across),
            ),
        )
        shape = (64 * depth, place // depth * tile)
        outputs.append(("outs", jax.ShapeDtypeStruct(shape, jnp.float32), spec))
        at += place
    hops = HOPS[sides]
    for _, _, shape in hops:
        scratch.append(("send", low(LAG, *shape)))
        scratch.append(("recv", low(2 * LAG, *shape)))
        scratch.append(("keep", full(LAG, *shape)))
    scratch.append(("last", full(LAG, 64, 128)))
    scratch.append(("sems", pltpu.SemaphoreType.DMA((len(hops), LAG))))
    scratch.append(("sems", pltpu.SemaphoreType.DMA((len(hops), 2 * LAG))))
    lim, qkv, kv_rest, do, o, lse = attention
    count, width = do.shape
    blocks = width // 128
    place = lambda skip: pl.BlockSpec(
        (count, 128), lambda i: (0, jnp.minimum(i // 4, blocks - 1) + skip)
    )
    inputs.append(("attention", lim, pl.BlockSpec(memory_space=pltpu.SMEM)))
    skips = (0, blocks, 2 * blocks, 0, blocks, 0, 0, 0)
    for operand, skip in zip((qkv, qkv, qkv, kv_rest, kv_rest, do, o, lse), skips):
        inputs.append(("attention", operand, place(skip)))
    scratch += [("turned", low(2, 1024, count)), ("held", low(5, count, width))]
    scratch += [("held", low(2, count, 128)), ("held", low(2, count, 128)), ("held", full(count, 128))]
    vector, w_qkv, normed, normed_rest = project
    share_of = lambda i: jnp.clip(i - SHARE, 0, 3)
    dense_of = lambda i: (0, jnp.clip((i - DENSE) // 4, 0, 3))
    column = pl.BlockSpec((count, tile), lambda i: (0, share_of(i)))
    inputs.append(("project", vector, pl.BlockSpec(vector.shape, lambda i: (0, 0))))
    inputs.append(("project", w_qkv, pl.BlockSpec((tile, w_qkv.shape[1]), lambda i: (share_of(i), 0))))
    inputs += [("project", normed, column), ("project", normed_rest, column)]
    for operand in dense:
        inputs.append(("dense", operand, pl.BlockSpec((operand.shape[0], tile), dense_of)))
    shape = (16,) + vector.shape
    result = lambda shape, dtype, spec: ("results", jax.ShapeDtypeStruct(shape, dtype), spec)
    outputs += [
        result(do.shape, jnp.float32, column),
        result(do.shape, jnp.bfloat16, pl.BlockSpec(memory_space=pl.ANY)),
        result(shape, jnp.float32, pl.BlockSpec(shape, lambda i: (0, 0, 0))),
        result(do.shape, jnp.bfloat16, pl.BlockSpec((count, tile), dense_of)),
    ]
    scratch += [("gather", full(*shape)), ("gather", full(*vector.shape)), ("gather", full(*vector.shape))]
    scratch.append(("gather", low(*do.shape)))
    scratch += [("gather_sems", pltpu.SemaphoreType.DMA((5,)))] * 2
    scratch += [("gather_sems", pltpu.SemaphoreType.DMA((1,)))] * 2
    flops += (80 * count + 14 * width) * count * width
    transcendentals = 2 * count * count * width // 64
    groups = (
        ("lefts", "rights", "attention", "project", "dense"),
        ("outs", "results"),
        ("turned", "held", "send", "recv", "keep", "last", "sems", "gather", "gather_sems"),
    )
    layout, ordered = [], []
    for names, entries in zip(groups, (inputs, outputs, scratch)):
        found = [[entry[1:] for entry in entries if entry[0] == name] for name in names]
        layout += [(name, len(run)) for name, run in zip(names, found)]
        ordered.append([entry for run in found for entry in run])
    operands = [operand for operand, _ in ordered[0]]
    results = pl.pallas_call(
        functools.partial(sum_kernel, units, tuple(plan), tuple(layout), sides),
        grid=(units + LAG * stages,),
        in_specs=[spec for _, spec in ordered[0]],
        out_specs=[spec for _, spec in ordered[1]],
        out_shape=[shape for shape, _ in ordered[1]],
        scratch_shapes=[shape for shape, in ordered[2]],
        compiler_params=pltpu.CompilerParams(
            vmem_limit_bytes=63 << 20, collective_id=sides - 1, has_side_effects=True
        ),
        cost_estimate=pl.CostEstimate(
            flops=flops,
            transcendentals=transcendentals,
            bytes_accessed=sum(2 * operand.size for operand in operands),
        ),
    )(*operands)
    return results


def per_device(
    frames,
    cotangent,
    section,
    prompt_len,
    section_embed,
    ada_proj,
    ada_bias,
    w_qkv,
    w_out,
    w_up,
    w_down,
):
    _, row_count, width = frames.shape
    frames, cotangent = frames[0], cotangent[0]
    seq_size = lax.axis_size("seq")
    item_size = lax.axis_size("items")
    seq_me, item_me = lax.axis_index("seq"), lax.axis_index("items")
    side = jnp.bitwise_and(item_me, 1).astype(jnp.int32).reshape(1)
    turns = list(range(1, seq_size))
    fetch = lambda values, turn: lax.ppermute(
        values, "seq", [((i + turn) % seq_size, i) for i in range(seq_size)]
    )
    give = lambda values, turn: lax.ppermute(
        values, "seq", [(i, (i + turn) % seq_size) for i in range(seq_size)]
    )
    others = [fetch(frames, turn) for turn in turns]
    sources = jnp.stack([(seq_me + turn) % seq_size for turn in [0] + turns])
    limits = jnp.where(sources == 0, prompt_len[0], row_count).astype(jnp.int32)

    section_count = section_embed.shape[0]
    onehot = (section[:, None] == jnp.arange(section_count, dtype=jnp.int32)[None, :]).astype(
        jnp.float32
    )
    cond = jnp.dot(onehot, section_embed, precision=HIGHEST)
    modul = jnp.dot(cond, ada_proj.astype(jnp.float32), precision=HIGHEST) + ada_bias[None, :]
    scale_one, shift_one, scale_two, shift_two = jnp.split(modul, 4, axis=-1)
    inputs = frames.astype(jnp.float32)
    normed_one, inv_one = normalize(inputs)
    modulate = lambda normed: (normed * (1.0 + scale_one) + shift_one).astype(jnp.bfloat16)
    attn_in = modulate(normed_one)
    qkv = project(attn_in, w_qkv).astype(jnp.bfloat16)
    grad_act = back_project(cotangent, w_down).astype(jnp.bfloat16)
    others, qkv, grad_act = lax.optimization_barrier((others, qkv, grad_act))
    rest = jnp.concatenate(others) if len(others) > 1 else others[0]
    normed_rest, _ = normalize(rest.astype(jnp.float32))
    attn_rest = modulate(normed_rest)
    kv_rest = project(attn_rest, w_qkv[:, width:]).astype(jnp.bfloat16)
    att, lse = attend(limits, qkv, kv_rest, width)
    mid = inputs + project(att, w_out)
    normed_two, inv_two = normalize(mid)
    ffn_in = (normed_two * (1.0 + scale_two) + shift_two).astype(jnp.bfloat16)
    upper = project(ffn_in, w_up)
    act = gelu_exact(upper).astype(jnp.bfloat16)
    grad_upper = (grad_act.astype(jnp.float32) * gelu_slope(upper)).astype(jnp.bfloat16)

    grad_out = cotangent.astype(jnp.float32)
    fused = seq_size == 2 and item_size == 16 and width == 1024
    grad_ffn_in = lax.optimization_barrier(back_project(grad_upper, w_up))
    grad_scale_two = jnp.sum(grad_ffn_in * normed_two, 0)
    grad_shift_two = jnp.sum(grad_ffn_in, 0)
    grad_mid = grad_out + norm_back(grad_ffn_in * (1.0 + scale_two), normed_two, inv_two)
    grad_mid_low = grad_mid.astype(jnp.bfloat16)
    grad_att = back_project(grad_mid_low, w_out).astype(jnp.bfloat16)
    if fused:
        vector = jnp.concatenate(
            [
                jnp.zeros((2 * width // 128, 128), jnp.float32),
                jnp.concatenate([grad_scale_two, grad_shift_two]).reshape(2 * width // 128, 128),
                jnp.pad(onehot, ((0, 7), (0, 128 - section_count))),
            ]
        )
        sum_down, sum_up, sum_out, sum_qkv, partial, got_share, tagged, out_frames = sum_weights(
            [
                [[(0, cotangent)]],
                [[(1, grad_upper)]],
                [[(2, grad_mid_low)]],
                [[(3, range(0, 1))], [(3, range(1, 3)), (4, range(3, 5))]],
            ],
            [act, ffn_in, att, attn_in, attn_rest],
            2,
            (limits, qkv, kv_rest, grad_att, att, lse),
            (vector, w_qkv, normed_one, normed_rest),
            (w_down, mid),
        )
        grad_rest = [got_share]
        tagged = tagged[:, : 4 * width // 128 + 1].reshape(item_size, 4 * width + 128)
    else:
        out_frames = (mid + project(act, w_down)).astype(jnp.bfloat16)
        grad_query, grad_key, grad_value, key_rest, value_rest = attend_back(
            limits, qkv, kv_rest, grad_att, att, lse
        )
        w_key, w_value = w_qkv[:, width : 2 * width], w_qkv[:, 2 * width :]
        share = back_project(key_rest, w_key) + back_project(value_rest, w_value)
        partial = (
            back_project(grad_query, w_qkv[:, :width])
            + back_project(grad_key, w_key)
            + back_project(grad_value, w_value)
        )
        share_low = share.astype(jnp.bfloat16)
        grad_rest = [
            give(share_low[i * row_count : (i + 1) * row_count], turn)
            for i, turn in enumerate(turns)
        ]
        grad_scale_one = jnp.sum(partial * normed_one, 0) + jnp.sum(share * normed_rest, 0)
        grad_shift_one = jnp.sum(partial, 0) + jnp.sum(share, 0)
        grad_modul = jnp.concatenate(
            [grad_scale_one, grad_shift_one, grad_scale_two, grad_shift_two]
        )[None, :]
        qkv_terms = [
            [(0, grad_query)],
            [(0, grad_key), (1, key_rest)],
            [(0, grad_value), (1, value_rest)],
        ]
        sums = lambda lefts, terms, tile: finish(
            outer(side, lefts, terms, item_size, tile), "items", "seq"
        )
        sum_down = sums([act], [[(0, cotangent)]], 256)
        sum_up = sums([ffn_in], [[(0, grad_upper)]], 512)
        sum_out = sums([att], [[(0, grad_mid_low)]], 512)
        sum_qkv = sums([attn_in, attn_rest], qkv_terms, 512)
        for bit in bits_of("seq"):
            grad_modul = grad_modul + swap(grad_modul, "seq", bit)
        tagged = jnp.concatenate(
            [grad_modul, jnp.pad(onehot, ((0, 0), (0, 128 - section_count)))], -1
        )
        tagged = gather_items(tagged, "items")
    grad_attn_in = partial
    for got in grad_rest:
        grad_attn_in = grad_attn_in + got.astype(jnp.float32)
    frames_grad = (
        grad_mid + norm_back(grad_attn_in * (1.0 + scale_one), normed_one, inv_one)
    ).astype(jnp.bfloat16)

    modul_all, onehot_all = tagged[:, : 4 * width], tagged[:, 4 * width :][:, :section_count]
    block = width // item_size
    own_embed = lax.dynamic_slice_in_dim(section_embed, item_me * block, block, 1)
    own_cond = jnp.dot(onehot_all, own_embed, precision=HIGHEST)
    sum_ada = lax.dot_general(own_cond, modul_all, (((0,), (0,)), ((), ())), precision=HIGHEST)
    sum_bias = jnp.sum(
        lax.dynamic_slice_in_dim(modul_all, item_me * 4 * block, 4 * block, 1), 0
    )
    own_ada = lax.dynamic_slice_in_dim(ada_proj, item_me * block, block, 0).astype(jnp.float32)
    grad_cond = lax.dot_general(modul_all, own_ada, (((1,), (1,)), ((), ())), precision=HIGHEST)
    sum_embed = lax.dot_general(
        onehot_all, grad_cond, (((0,), (0,)), ((), ())), precision=HIGHEST
    )
    return (
        out_frames[None],
        frames_grad[None],
        sum_embed,
        sum_ada,
        sum_bias,
        sum_qkv,
        sum_out,
        sum_up,
        sum_down,
    )


def solution(mesh):
    in_specs = (
        P("items", "seq", None),
        P("items", "seq", None),
        P("items"),
        P("items"),
        P(),
        P(),
        P(),
        P(),
        P(),
        P(),
        P(),
    )
    out_specs = (
        P("items", "seq", None),
        P("items", "seq", None),
        P(None, "items"),
        P("items", None),
        P("items"),
        P("items", None),
        P("items", None),
        P("items", None),
        P("items", None),
    )
    return jax.shard_map(
        per_device, mesh=mesh, in_specs=in_specs, out_specs=out_specs, check_vma=False
    )
```
